256 devices in a mesh: gx: 16 (over z, x_lo), gy: 16 (over x_hi, y, core).
Axes of the slice: x: 4 (x_hi: 2, x_lo: 2; x = x_hi * 2 + x_lo), y: 4, z: 8, core: 2. Of those that a mesh axis runs over, the one named last changes fastest.
Arguments:
- object_field: float32 [2, 4096, 4096], P(None, 'gx', 'gy'), may hold values from -4.5 to 4.5
- probe_field: float32 [2, 2, 256, 256], replicated, may hold values from -4.2 to 4.2
- amplitude: float32 [64, 16, 256, 256], P('gx', 'gy'), may hold values from 0.2 to 3
- offsets: int32 [64, 16, 2], P('gx', 'gy'), may hold values from -128 to 128
Outputs:
- updated_object: float32 [2, 4096, 4096], P(None, 'gx', 'gy')
- updated_probe: float32 [2, 2, 256, 256], replicated
The draws below stay inside these ranges and needn't reach their ends.
All inputs are finite; a program needn't handle non-finite values.
Results may differ from the reference program's by a relative error of at most 0.0006.
The reference program's roundings to bfloat16 on the way count: a program that leaves them out, or rounds other values in their place, can miss the bound.
Values sent between devices are 32-bit elements; how exact they have to be, the bound alone decides.
No kernel may reach another device: no remote copies, remote signals or barrier semaphores. Data moves between devices by JAX's collectives and lax.ppermute only.
A program may use at most 64 MiB of HBM per device.

```python
import math
import jax
import jax.numpy as jnp
from jax import lax

W = 256
MODES = 2
TILE = 256
POS = 4
NR = 4096
NC = 4096
N_GX = 16
N_GY = 16


def draw_object_field(key, part):
    key_mag = jax.random.fold_in(key, 11)
    key_phase = jax.random.fold_in(key, 12)
    rows = jnp.arange(NR, dtype=jnp.float32)[:, None] / NR
    cols = jnp.arange(NC, dtype=jnp.float32)[None, :] / NC
    ramp = jnp.sqrt((1.0 + 2.0 * rows) * (1.0 + 2.0 * cols)) / 1.7
    rough = jax.random.uniform(key_mag, (NR, NC), jnp.float32, 0.5, 1.2)
    angles = jax.random.uniform(key_phase, (NR, NC), jnp.float32, -math.pi, math.pi)
    magnitude = rough * ramp
    return jnp.stack([magnitude * jnp.cos(angles), magnitude * jnp.sin(angles)], 0)


def touch_ends(entries, key, smallest, high):
    longest = entries.shape.index(max(entries.shape))
    spots = []
    for shift in (0, 1):
        where = [jax.random.randint(jax.random.fold_in(key, axis), (), 0, length) for axis, length in enumerate(entries.shape)]
        where[longest] = (where[longest] + shift) % entries.shape[longest]
        spots.append(tuple(where))
    return entries.at[spots[0]].set(smallest).at[spots[1]].set(high)


def levels(rng, dims, split, smallest, largest):
    level = 1.0
    for axis_at, shards_of in split:
        draws = jax.random.uniform(jax.random.fold_in(jax.random.fold_in(rng, 6), axis_at), (shards_of,), jnp.float32, smallest / len(split), largest / len(split))
        level = level * jnp.repeat(jnp.exp(draws), dims[axis_at] // shards_of).reshape((-1,) + (1,) * (len(dims) - 1 - axis_at))
    return level


def scatter_about(key, dims, scale, most, kind=jnp.bfloat16):
    entries = scale * jax.random.normal(key, dims, jnp.float32)
    return jnp.clip(entries, min=-most, max=most).astype(kind)


def setup_inputs(seed: int = 0) -> dict:
    keys = jax.random.split(jax.random.key(seed), 5)
    object_field = draw_object_field(jax.random.fold_in(keys[4], 71), 0)
    probe_field = scatter_about(keys[1], (MODES, 2, W, W), 0.7, 4.2, jnp.float32)
    amplitude = jnp.clip(jnp.exp(math.log(3.0) - 2.7080502 * jax.random.uniform(keys[2], (POS * N_GX, N_GY, W, W), jnp.float32) ** levels(keys[2], (POS * N_GX, N_GY, W, W), ((0, 16), (1, 16)), -0.2, 0.2)), 0.2, 3.0)
    offsets = touch_ends(jax.random.randint(keys[3], (POS * N_GX, N_GY, 2), 0 - W // 2, TILE - W // 2 + 1), jax.random.fold_in(keys[3], 1), 0 - W // 2, (TILE - W // 2 + 1) - 1).astype(jnp.int32)
    return {"object_field": object_field, "probe_field": probe_field, "amplitude": amplitude, "offsets": offsets}


def dft_tables(extent):
    indices = jnp.arange(extent, dtype=jnp.int32)
    phases = indices[:, None] * indices[None, :] % extent
    angles = phases.astype(jnp.float32) * (2.0 * math.pi / extent)
    norm_factor = 1.0 / math.sqrt(extent)
    return ((jnp.cos(angles) * norm_factor).astype(jnp.bfloat16), (jnp.sin(angles) * norm_factor).astype(jnp.bfloat16))

def to_half(values):
    return lax.optimization_barrier(values.astype(jnp.bfloat16)).astype(jnp.float32)

def row_pass(cosine, sine, real_part, imag_part, orient):
    amount = real_part.shape[0]
    stacked = jnp.concatenate([real_part, imag_part], 0).astype(jnp.float32)
    with_cos = jnp.einsum('jk,bkl->bjl', cosine.astype(jnp.float32), stacked)
    with_sin = jnp.einsum('jk,bkl->bjl', sine.astype(jnp.float32), stacked)
    return (with_cos[:amount] + orient * with_sin[amount:], with_cos[amount:] - orient * with_sin[:amount])

def col_pass(cosine, sine, real_part, imag_part, orient):
    amount = real_part.shape[0]
    stacked = jnp.concatenate([real_part, imag_part], 0).astype(jnp.float32)
    with_cos = jnp.einsum('bjk,kl->bjl', stacked, cosine.astype(jnp.float32))
    with_sin = jnp.einsum('bjk,kl->bjl', stacked, sine.astype(jnp.float32))
    return (with_cos[:amount] + orient * with_sin[amount:], with_cos[amount:] - orient * with_sin[:amount])

def corrections(windows, probe_field, amplitude, cosine, sine):
    extent = probe_field.shape[-1]
    obj_real = windows[:, None, 0]
    obj_imag = windows[:, None, 1]
    probe_real = probe_field[None, :, 0]
    probe_imag = probe_field[None, :, 1]
    psi_real = probe_real * obj_real - probe_imag * obj_imag
    psi_imag = probe_real * obj_imag + probe_imag * obj_real
    amount = psi_real.shape[0]
    mode_count = psi_real.shape[1]
    shape_flat = (amount * mode_count, extent, extent)
    shape_full = (amount, mode_count, extent, extent)
    rows_real, rows_imag = row_pass(cosine, sine, to_half(psi_real.reshape(shape_flat)), to_half(psi_imag.reshape(shape_flat)), 1.0)
    far_real, far_imag = col_pass(cosine, sine, to_half(rows_real), to_half(rows_imag), 1.0)
    far_real = far_real.reshape(shape_full)
    far_imag = far_imag.reshape(shape_full)
    intensity = lax.optimization_barrier(jnp.sum(far_real * far_real + far_imag * far_imag, axis=1))
    factor = (amplitude / jnp.maximum(jnp.sqrt(intensity), 0.25))[:, None]
    proj_real = to_half((far_real * factor).reshape(shape_flat))
    proj_imag = to_half((far_imag * factor).reshape(shape_flat))
    back_rows_real, back_rows_imag = row_pass(cosine, sine, proj_real, proj_imag, -1.0)
    back_real, back_imag = col_pass(cosine, sine, to_half(back_rows_real), to_half(back_rows_imag), -1.0)
    diff_real = back_real.reshape(shape_full) - psi_real
    diff_imag = back_imag.reshape(shape_full) - psi_imag
    object_real = lax.optimization_barrier(jnp.sum(probe_real * diff_real + probe_imag * diff_imag, axis=1))
    object_imag = lax.optimization_barrier(jnp.sum(probe_real * diff_imag - probe_imag * diff_real, axis=1))
    grad_real = lax.optimization_barrier(jnp.sum(obj_real * diff_real + obj_imag * diff_imag, axis=0))
    grad_imag = lax.optimization_barrier(jnp.sum(obj_real * diff_imag - obj_imag * diff_real, axis=0))
    weight = lax.optimization_barrier(jnp.sum(windows[:, 0] * windows[:, 0] + windows[:, 1] * windows[:, 1], axis=0))
    return (jnp.stack([object_real, object_imag], 1), grad_real, grad_imag, weight)

def reference(object_field, probe_field, amplitude, offsets):
    extent = probe_field.shape[-1]
    margin = extent // 2
    mode_count = probe_field.shape[0]
    cosine, sine = dft_tables(extent)
    padded = jnp.pad(object_field, ((0, 0), (margin, margin), (margin, margin)), mode='wrap')
    zero_index = jnp.zeros((), jnp.int32)

    def tile_step(running, tile_number):
        accum, grad_real, grad_imag, weight = running
        tile_row = tile_number // N_GY
        tile_col = tile_number % N_GY
        tile_offsets = lax.dynamic_slice(offsets, (tile_row * POS, tile_col, zero_index), (POS, 1, 2))[:, 0]
        tile_amp = lax.dynamic_slice(amplitude, (tile_row * POS, tile_col, zero_index, zero_index), (POS, 1, extent, extent))[:, 0]
        row_starts = (tile_row * TILE + tile_offsets[:, 0] + margin).astype(jnp.int32)
        col_starts = (tile_col * TILE + tile_offsets[:, 1] + margin).astype(jnp.int32)
        windows = jnp.stack([lax.dynamic_slice(padded, (zero_index, row_starts[position], col_starts[position]), (2, extent, extent)) for position in range(POS)], 0)
        terms, step_real, step_imag, step_weight = corrections(windows, probe_field, tile_amp, cosine, sine)
        for position in range(POS):
            where = (zero_index, row_starts[position], col_starts[position])
            current = lax.dynamic_slice(accum, where, (2, extent, extent))
            accum = lax.dynamic_update_slice(accum, current + terms[position], where)
        return ((accum, grad_real + step_real, grad_imag + step_imag, weight + step_weight), None)
    start_state = (jnp.zeros((2, NR + 2 * margin, NC + 2 * margin), jnp.float32), jnp.zeros((mode_count, extent, extent), jnp.float32), jnp.zeros((mode_count, extent, extent), jnp.float32), jnp.zeros((extent, extent), jnp.float32))
    final_state, _ = lax.scan(tile_step, start_state, jnp.arange(N_GX * N_GY, dtype=jnp.int32))
    accum, grad_real, grad_imag, weight = final_state
    cols_core = accum[:, :, margin:margin + NC]
    cols_core = cols_core.at[:, :, NC - margin:].add(accum[:, :, :margin])
    cols_core = cols_core.at[:, :, :margin].add(accum[:, :, NC + margin:])
    object_step = cols_core[:, margin:margin + NR]
    object_step = object_step.at[:, NR - margin:].add(cols_core[:, :margin])
    object_step = object_step.at[:, :margin].add(cols_core[:, NR + margin:])
    updated_probe = probe_field + jnp.stack([grad_real, grad_imag], 1) / (weight + 1e-05)
    power = lax.optimization_barrier(jnp.sum(probe_field * probe_field, axis=(0, 1)))
    scale_max = jnp.max(power) + 1e-06
    updated_object = object_field + object_step / scale_max
    return (updated_object, updated_probe)
```

```python
import functools
import math

import jax
import jax.numpy as jnp
import ml_dtypes
import numpy as np
from jax import lax
from jax.experimental import pallas as pl
from jax.experimental.pallas import tpu as pltpu
from jax.sharding import Mesh
from jax.sharding import PartitionSpec as P

W = 256
HALF = 128
POS = 4
MODES = 2
CH = 32
BF = jnp.bfloat16
F32 = jnp.float32


def dft_matrices():
    k = np.arange(W)
    phase = (k[:, None] * k[None, :]) % W
    angle = phase.astype(np.float32) * np.float32(2.0 * math.pi / W)
    norm = np.float32(1.0 / math.sqrt(W))
    c = (np.cos(angle) * norm).astype(ml_dtypes.bfloat16)
    s = (np.sin(angle) * norm).astype(ml_dtypes.bfloat16)
    fwd = np.block([[c, s], [-s, c]])
    bwd = np.block([[c, -s], [s, c]])
    return fwd, bwd


def kernel(
    offs, half, tile, top, bot, left, right, probe, amp, fwd, bwd,
    mine, other, acc,
    ext, win, stack, side, far, weight, grads,
):
    lanes = lax.broadcasted_iota(jnp.int32, (CH, HALF), 1)
    for q in range(2):
        cols = pl.ds(q * HALF, HALF)
        ext[:, q + 1, 0:HALF, :] = top[:, :, cols]
        ext[:, q + 1, HALF : HALF + W, :] = tile[:, :, cols]
        ext[:, q + 1, HALF + W :, :] = bot[:, :, cols]
    ext[:, 0] = left[...]
    ext[:, 3] = right[...]
    acc[...] = jnp.zeros_like(acc)
    weight[...] = jnp.zeros_like(weight)
    grads[...] = jnp.zeros_like(grads)

    def position(p, carry):
        r = offs[p, 0, 0] + HALF
        c = offs[p, 0, 1] + HALF
        q = c // HALF
        s = c - q * HALF
        back_shift = lax.rem(HALF - s, HALF)
        keep = lanes < HALF - s
        q2 = jnp.minimum(q + 2, 3)

        def cut(i, carry):
            rows = pl.ds(pl.multiple_of(i * CH, CH), CH)
            w = []
            for d in range(2):
                src = pl.ds(r + i * CH, CH)
                a = pltpu.roll(ext[d, q, src, :], back_shift, 1)
                b = pltpu.roll(ext[d, q + 1, src, :], back_shift, 1)
                e = pltpu.roll(ext[d, q2, src, :], back_shift, 1)
                w.append(jnp.concatenate([jnp.where(keep, a, b), jnp.where(keep, b, e)], 1))
                win[d, rows, :] = w[d]
            weight[rows, :] += w[0] * w[0] + w[1] * w[1]
            for k in range(MODES):
                pr = probe[k, 0, rows, :]
                pi = probe[k, 1, rows, :]
                stack[k, rows, :] = (pr * w[0] - pi * w[1]).astype(BF)
                stack[k, pl.ds(pl.multiple_of(W + i * CH, CH), CH), :] = (pr * w[1] + pi * w[0]).astype(BF)
            return carry

        lax.fori_loop(0, W // CH, cut, 0)
        for k in range(MODES):
            rows_f = jnp.dot(fwd[...], stack[k], preferred_element_type=F32)
            side[k, :, 0:W] = rows_f[0:W].astype(BF)
            side[k, :, W:] = rows_f[W:].astype(BF)
        for k in range(MODES):
            far[k] = jnp.dot(side[k], bwd[...], preferred_element_type=F32)

        def project(i, carry):
            rows = pl.ds(pl.multiple_of(i * CH, CH), CH)
            rows_im = pl.ds(pl.multiple_of(W + i * CH, CH), CH)
            f = [far[k, rows, :] for k in range(MODES)]
            total = f[0] * f[0] + f[1] * f[1]
            intensity = total[:, 0:W] + total[:, W:]
            factor = amp[p, 0, rows, :] * lax.rsqrt(jnp.maximum(intensity, 0.0625))
            for k in range(MODES):
                stack[k, rows, :] = (f[k][:, 0:W] * factor).astype(BF)
                stack[k, rows_im, :] = (f[k][:, W:] * factor).astype(BF)
            return carry

        lax.fori_loop(0, W // CH, project, 0)
        for k in range(MODES):
            rows_b = jnp.dot(bwd[...], stack[k], preferred_element_type=F32)
            side[k, :, 0:W] = rows_b[0:W].astype(BF)
            side[k, :, W:] = rows_b[W:].astype(BF)
        for k in range(MODES):
            far[k] = jnp.dot(side[k], fwd[...], preferred_element_type=F32)

        def spread(i, carry):
            rows = pl.ds(pl.multiple_of(i * CH, CH), CH)
            wr = win[0, rows, :]
            wi = win[1, rows, :]
            power = jnp.zeros((CH, W), F32)
            tr = jnp.zeros((CH, W), F32)
            ti = jnp.zeros((CH, W), F32)
            for k in range(MODES):
                pr = probe[k, 0, rows, :]
                pi = probe[k, 1, rows, :]
                br = far[k, rows, 0:W]
                bi = far[k, rows, W:]
                power += pr * pr + pi * pi
                tr += pr * br + pi * bi
                ti += pr * bi - pi * br
                grads[2 * k, rows, :] += wr * br + wi * bi
                grads[2 * k + 1, rows, :] += wr * bi - wi * br
            dst = pl.ds(r + i * CH, CH)
            for d, t in ((0, tr - power * wr), (1, ti - power * wi)):
                a = pltpu.roll(t[:, 0:HALF], s, 1)
                b = pltpu.roll(t[:, HALF:], s, 1)
                low = lanes < s
                acc[d, q, dst, :] += jnp.where(low, 0.0, a)
                acc[d, q + 1, dst, :] += jnp.where(low, a, b)
                acc[d, q2, dst, :] += jnp.where(low, b, 0.0)
            return carry

        lax.fori_loop(0, W // CH, spread, 0)
        return carry

    lax.fori_loop(0, POS, position, 0)
    h = half[0]
    for out, side_of in ((mine, h), (other, 1 - h)):

        def flush(i, carry):
            rows = pl.ds(pl.multiple_of(side_of * HALF + i * 8, 8), 8)
            for n in range(2 * MODES):
                out[i, n] = grads[n, rows, :]
            out[i, 2 * MODES] = weight[rows, :]
            return carry

        lax.fori_loop(0, 16, flush, 0)


def correct(offsets, half, tile, top, bot, left, right, probe, amplitude):
    fwd, bwd = dft_matrices()
    vmem = pl.BlockSpec(memory_space=pltpu.VMEM)
    smem = pl.BlockSpec(memory_space=pltpu.SMEM)
    part = jax.ShapeDtypeStruct((16, 2 * MODES + 1, 8, W), F32)
    return pl.pallas_call(
        kernel,
        out_shape=(part, part, jax.ShapeDtypeStruct((2, 4, 2 * W, HALF), F32)),
        in_specs=[smem, smem] + [vmem] * 9,
        out_specs=(vmem, vmem, vmem),
        scratch_shapes=[
            pltpu.VMEM((2, 4, 2 * W, HALF), F32),
            pltpu.VMEM((2, W, W), F32),
            pltpu.VMEM((MODES, 2 * W, W), BF),
            pltpu.VMEM((MODES, W, 2 * W), BF),
            pltpu.VMEM((MODES, W, 2 * W), F32),
            pltpu.VMEM((W, W), F32),
            pltpu.VMEM((2 * MODES, W, W), F32),
        ],
        compiler_params=pltpu.CompilerParams(vmem_limit_bytes=48 << 20),
    )(offsets, half, tile, top, bot, left, right, probe, amplitude, jnp.asarray(fwd), jnp.asarray(bwd))


GX = ("z", "xl")
GY = ("xh", "y", "co")
UP = [(i, (i + 1) % 16) for i in range(16)]
DOWN = [(j, i) for i, j in UP]
SWAP = [(0, 1), (1, 0)]


def body(object_field, probe_field, amplitude, offsets):
    top = lax.ppermute(object_field[:, HALF:], GX, UP)
    bot = lax.ppermute(object_field[:, :HALF], GX, DOWN)
    cols = lambda sl: jnp.concatenate([top[:, :, sl], object_field[:, :, sl], bot[:, :, sl]], 1)
    left = lax.ppermute(cols(slice(HALF, W)), GY, UP)
    right = lax.ppermute(cols(slice(0, HALF)), GY, DOWN)
    co = lax.axis_index("co")
    mine, other, acc = correct(
        offsets, co.reshape(1), object_field, top, bot, left, right, probe_field, amplitude
    )
    group = ("xh", "xl", "y")
    part = mine + lax.ppermute(other, "co", SWAP)
    from_right = lax.ppermute(acc[:, 0], GY, DOWN)
    from_left = lax.ppermute(acc[:, 3], GY, UP)
    part = jnp.sum(lax.all_to_all(part, group, 0, 0, tiled=True), 0)
    for step in (1, 2, 4):
        part = part + lax.ppermute(part, "z", [(i, i ^ step) for i in range(8)])
    block = co * 16 + lax.axis_index(group)
    planes = probe_field.reshape(2 * MODES, W, W)
    local = lax.dynamic_slice_in_dim(planes, block * 8, 8, 1)
    weight = part[2 * MODES]
    local = local + (part[: 2 * MODES] - local * weight) / (weight + 1e-05)
    gathered = lax.all_to_all(jnp.broadcast_to(local[None], (16,) + local.shape), group, 0, 0, tiled=True)
    opposite = lax.ppermute(gathered, "co", SWAP)
    halves = jnp.where(co == 0, jnp.stack([gathered, opposite]), jnp.stack([opposite, gathered]))
    updated_probe = halves.transpose(2, 0, 1, 3, 4).reshape(MODES, 2, W, W)

    folded = jnp.concatenate([acc[:, 1] + from_left, acc[:, 2] + from_right], 2)
    from_below = lax.ppermute(folded[:, :HALF], GX, DOWN)
    from_above = lax.ppermute(folded[:, HALF + W :], GX, UP)
    object_step = folded[:, HALF : HALF + W] + jnp.concatenate([from_above, from_below], 1)
    scale_max = jnp.max(jnp.sum(probe_field * probe_field, axis=(0, 1))) + 1e-06
    return (object_field + object_step / scale_max, updated_probe)


def solution(mesh):
    fine = Mesh(mesh.devices.reshape(8, 2, 2, 4, 2), ("z", "xl", "xh", "y", "co"))
    in_specs = (P(None, GX, GY), P(), P(GX, GY, None, None), P(GX, GY, None))
    out_specs = (P(None, GX, GY), P())
    return jax.shard_map(body, mesh=fine, in_specs=in_specs, out_specs=out_specs, check_vma=False)
```

```python
import functools
import math

import jax
import jax.numpy as jnp
import ml_dtypes
import numpy as np
from jax import lax
from jax.experimental import pallas as pl
from jax.experimental.pallas import tpu as pltpu
from jax.sharding import Mesh
from jax.sharding import PartitionSpec as P

W = 256
HALF = 128
POS = 4
MODES = 2
CH = 32
BF = jnp.bfloat16
F32 = jnp.float32


def dft_matrices():
    k = np.arange(W)
    phase = (k[:, None] * k[None, :]) % W
    angle = phase.astype(np.float32) * np.float32(2.0 * math.pi / W)
    norm = np.float32(1.0 / math.sqrt(W))
    c = (np.cos(angle) * norm).astype(ml_dtypes.bfloat16)
    s = (np.sin(angle) * norm).astype(ml_dtypes.bfloat16)
    fwd = np.block([[c, s], [-s, c]])
    bwd = np.block([[c, -s], [s, c]])
    return fwd, bwd


def kernel(
    offs, half, tile, top, bot, left, right, left_ends, right_ends, probe, amp, fwd, bwd,
    mine, other, acc,
    ext, win, stack, side, far, weight, grads,
):
    lanes = lax.broadcasted_iota(jnp.int32, (CH, HALF), 1)
    for q in range(2):
        cols = pl.ds(q * HALF, HALF)
        ext[:, q + 1, 0:HALF, :] = top[:, :, cols]
        ext[:, q + 1, HALF : HALF + W, :] = tile[:, :, cols]
        ext[:, q + 1, HALF + W :, :] = bot[:, :, cols]
    for q, middle, ends in ((0, left, left_ends), (3, right, right_ends)):
        ext[:, q, 0:HALF, :] = ends[0]
        ext[:, q, HALF : HALF + W, :] = middle[...]
        ext[:, q, HALF + W :, :] = ends[1]
    acc[...] = jnp.zeros_like(acc)
    weight[...] = jnp.zeros_like(weight)
    grads[...] = jnp.zeros_like(grads)

    def position(p, carry):
        r = offs[p, 0, 0] + HALF
        c = offs[p, 0, 1] + HALF
        q = c // HALF
        s = c - q * HALF
        back_shift = lax.rem(HALF - s, HALF)
        keep = lanes < HALF - s
        q2 = jnp.minimum(q + 2, 3)

        def cut(i, carry):
            rows = pl.ds(pl.multiple_of(i * CH, CH), CH)
            w = []
            for d in range(2):
                src = pl.ds(r + i * CH, CH)
                a = pltpu.roll(ext[d, q, src, :], back_shift, 1)
                b = pltpu.roll(ext[d, q + 1, src, :], back_shift, 1)
                e = pltpu.roll(ext[d, q2, src, :], back_shift, 1)
                w.append(jnp.concatenate([jnp.where(keep, a, b), jnp.where(keep, b, e)], 1))
                win[d, rows, :] = w[d]
            weight[rows, :] += w[0] * w[0] + w[1] * w[1]
            for k in range(MODES):
                pr = probe[k, 0, rows, :]
                pi = probe[k, 1, rows, :]
                stack[k, rows, :] = (pr * w[0] - pi * w[1]).astype(BF)
                stack[k, pl.ds(pl.multiple_of(W + i * CH, CH), CH), :] = (pr * w[1] + pi * w[0]).astype(BF)
            return carry

        lax.fori_loop(0, W // CH, cut, 0, unroll=True)
        for k in range(MODES):
            rows_f = jnp.dot(fwd[...], stack[k], preferred_element_type=F32)
            side[k, :, 0:W] = rows_f[0:W].astype(BF)
            side[k, :, W:] = rows_f[W:].astype(BF)
        for k in range(MODES):
            far[k] = jnp.dot(side[k], bwd[...], preferred_element_type=F32)

        def project(i, carry):
            rows = pl.ds(pl.multiple_of(i * CH, CH), CH)
            rows_im = pl.ds(pl.multiple_of(W + i * CH, CH), CH)
            f = [far[k, rows, :] for k in range(MODES)]
            total = f[0] * f[0] + f[1] * f[1]
            intensity = total[:, 0:W] + total[:, W:]
            factor = amp[p, 0, rows, :] * lax.rsqrt(jnp.maximum(intensity, 0.0625))
            for k in range(MODES):
                stack[k, rows, :] = (f[k][:, 0:W] * factor).astype(BF)
                stack[k, rows_im, :] = (f[k][:, W:] * factor).astype(BF)
            return carry

        lax.fori_loop(0, W // CH, project, 0, unroll=True)
        for k in range(MODES):
            rows_b = jnp.dot(bwd[...], stack[k], preferred_element_type=F32)
            side[k, :, 0:W] = rows_b[0:W].astype(BF)
            side[k, :, W:] = rows_b[W:].astype(BF)
        for k in range(MODES):
            far[k] = jnp.dot(side[k], fwd[...], preferred_element_type=F32)

        def spread(i, carry):
            rows = pl.ds(pl.multiple_of(i * CH, CH), CH)
            wr = win[0, rows, :]
            wi = win[1, rows, :]
            power = jnp.zeros((CH, W), F32)
            tr = jnp.zeros((CH, W), F32)
            ti = jnp.zeros((CH, W), F32)
            for k in range(MODES):
                pr = probe[k, 0, rows, :]
                pi = probe[k, 1, rows, :]
                br = far[k, rows, 0:W]
                bi = far[k, rows, W:]
                power += pr * pr + pi * pi
                tr += pr * br + pi * bi
                ti += pr * bi - pi * br
                grads[2 * k, rows, :] += wr * br + wi * bi
                grads[2 * k + 1, rows, :] += wr * bi - wi * br
            dst = pl.ds(r + i * CH, CH)
            for d, t in ((0, tr - power * wr), (1, ti - power * wi)):
                a = pltpu.roll(t[:, 0:HALF], s, 1)
                b = pltpu.roll(t[:, HALF:], s, 1)
                low = lanes < s
                acc[d, q, dst, :] += jnp.where(low, 0.0, a)
                acc[d, q + 1, dst, :] += jnp.where(low, a, b)
                acc[d, q2, dst, :] += jnp.where(low, b, 0.0)
            return carry

        lax.fori_loop(0, W // CH, spread, 0, unroll=True)
        return carry

    lax.fori_loop(0, POS, position, 0)
    h = half[0]
    for out, side_of in ((mine, h), (other, 1 - h)):

        def flush(i, carry):
            rows = pl.ds(pl.multiple_of(side_of * HALF + i * 8, 8), 8)
            for n in range(2 * MODES):
                out[i, n] = grads[n, rows, :]
            out[i, 2 * MODES] = weight[rows, :]
            return carry

        lax.fori_loop(0, 16, flush, 0)


def correct(offsets, half, border, probe, amplitude):
    fwd, bwd = dft_matrices()
    vmem = pl.BlockSpec(memory_space=pltpu.VMEM)
    smem = pl.BlockSpec(memory_space=pltpu.SMEM)
    part = jax.ShapeDtypeStruct((16, 2 * MODES + 1, 8, W), F32)
    return pl.pallas_call(
        kernel,
        out_shape=(part, part, jax.ShapeDtypeStruct((2, 4, 2 * W, HALF), F32)),
        in_specs=[smem, smem] + [vmem] * 11,
        out_specs=(vmem, vmem, vmem),
        scratch_shapes=[
            pltpu.VMEM((2, 4, 2 * W, HALF), F32),
            pltpu.VMEM((2, W, W), F32),
            pltpu.VMEM((MODES, 2 * W, W), BF),
            pltpu.VMEM((MODES, W, 2 * W), BF),
            pltpu.VMEM((MODES, W, 2 * W), F32),
            pltpu.VMEM((W, W), F32),
            pltpu.VMEM((2 * MODES, W, W), F32),
        ],
        compiler_params=pltpu.CompilerParams(vmem_limit_bytes=48 << 20),
    )(offsets, half, *border, probe, amplitude, jnp.asarray(fwd), jnp.asarray(bwd))


GX = ("z", "xl")
GY = ("xh", "y", "co")
UP = [(i, (i + 1) % 16) for i in range(16)]
DOWN = [(j, i) for i, j in UP]
SWAP = [(0, 1), (1, 0)]


def arrange_kernel(half, own, swapped, out):
    h = half[0]
    for source, side_of in ((own, h), (swapped, 1 - h)):
        for i in range(16):
            rows = pl.ds(pl.multiple_of(side_of * HALF + i * 8, 8), 8)
            for n in range(2 * MODES):
                out[n // 2, n % 2, rows, :] = source[i, n]


def arrange(half, own, swapped):
    vmem = pl.BlockSpec(memory_space=pltpu.VMEM)
    return pl.pallas_call(
        arrange_kernel,
        out_shape=jax.ShapeDtypeStruct((MODES, 2, W, W), F32),
        in_specs=[pl.BlockSpec(memory_space=pltpu.SMEM), vmem, vmem],
        out_specs=vmem,
    )(half, own, swapped)


def body(object_field, probe_field, amplitude, offsets):
    first, last = slice(0, HALF), slice(HALF, W)
    top = lax.ppermute(object_field[:, last], GX, UP)
    bot = lax.ppermute(object_field[:, first], GX, DOWN)
    left = lax.ppermute(object_field[:, :, last], GY, UP)
    right = lax.ppermute(object_field[:, :, first], GY, DOWN)
    left_ends = lax.ppermute(jnp.stack([top[:, :, last], bot[:, :, last]]), GY, UP)
    right_ends = lax.ppermute(jnp.stack([top[:, :, first], bot[:, :, first]]), GY, DOWN)
    co = lax.axis_index("co")
    half = co.reshape(1)
    border = (object_field, top, bot, left, right, left_ends, right_ends)
    mine, other, acc = correct(offsets, half, border, probe_field, amplitude)
    from_right = lax.ppermute(acc[:, 0], GY, DOWN)
    from_left = lax.ppermute(acc[:, 3], GY, UP)
    group = ("xh", "xl", "y")
    part = mine + lax.ppermute(other, "co", SWAP)
    part = jnp.sum(lax.all_to_all(part, group, 0, 0, tiled=True), 0)
    folded = jnp.concatenate([acc[:, 1] + from_left, acc[:, 2] + from_right], 2)
    part, folded = lax.optimization_barrier((part, folded))
    from_below = lax.ppermute(folded[:, :HALF], GX, DOWN)
    from_above = lax.ppermute(folded[:, HALF + W :], GX, UP)
    for step in (1, 2, 4):
        part = part + lax.ppermute(part, "z", [(i, i ^ step) for i in range(8)])
    block = co * 16 + lax.axis_index(group)
    planes = probe_field.reshape(2 * MODES, W, W)
    local = lax.dynamic_slice_in_dim(planes, block * 8, 8, 1)
    weight = part[2 * MODES]
    local = local + (part[: 2 * MODES] - local * weight) / (weight + 1e-05)
    local, from_below, from_above = lax.optimization_barrier((local, from_below, from_above))
    gathered = lax.all_to_all(jnp.broadcast_to(local[None], (16,) + local.shape), group, 0, 0, tiled=True)
    updated_probe = arrange(half, gathered, lax.ppermute(gathered, "co", SWAP))

    object_step = folded[:, HALF : HALF + W] + jnp.concatenate([from_above, from_below], 1)
    scale_max = jnp.max(jnp.sum(probe_field * probe_field, axis=(0, 1))) + 1e-06
    return (object_field + object_step / scale_max, updated_probe)


def solution(mesh):
    fine = Mesh(mesh.devices.reshape(8, 2, 2, 4, 2), ("z", "xl", "xh", "y", "co"))
    in_specs = (P(None, GX, GY), P(), P(GX, GY, None, None), P(GX, GY, None))
    out_specs = (P(None, GX, GY), P())
    return jax.shard_map(body, mesh=fine, in_specs=in_specs, out_specs=out_specs, check_vma=False)
```

```python
import functools
import math

import jax
import jax.numpy as jnp
import ml_dtypes
import numpy as np
from jax import lax
from jax.experimental import pallas as pl
from jax.experimental.pallas import tpu as pltpu
from jax.sharding import Mesh
from jax.sharding import PartitionSpec as P

W = 256
HALF = 128
POS = 4
MODES = 2
CH = 32
BF = jnp.bfloat16
F32 = jnp.float32


def dft_matrices():
    k = np.arange(W)
    phase = (k[:, None] * k[None, :]) % W
    angle = phase.astype(np.float32) * np.float32(2.0 * math.pi / W)
    norm = np.float32(1.0 / math.sqrt(W))
    c = (np.cos(angle) * norm).astype(ml_dtypes.bfloat16)
    s = (np.sin(angle) * norm).astype(ml_dtypes.bfloat16)
    fwd = np.block([[c, s], [-s, c]])
    bwd = np.block([[c, -s], [s, c]])
    return fwd, bwd


def kernel(
    offs, half, tile, top, bot, left, right, left_ends, right_ends, probe, amp, fwd, bwd,
    mine, other, out_left, out_mid, out_right,
    ext, acc, win, stack, side, far, weight, grads,
):
    lanes = lax.broadcasted_iota(jnp.int32, (CH, HALF), 1)
    for q in range(2):
        cols = pl.ds(q * HALF, HALF)
        ext[:, q + 1, 0:HALF, :] = top[:, :, cols]
        ext[:, q + 1, HALF : HALF + W, :] = tile[:, :, cols]
        ext[:, q + 1, HALF + W :, :] = bot[:, :, cols]
    for q, middle, ends in ((0, left, left_ends), (3, right, right_ends)):
        ext[:, q, 0:HALF, :] = ends[0]
        ext[:, q, HALF : HALF + W, :] = middle[...]
        ext[:, q, HALF + W :, :] = ends[1]
    acc[...] = jnp.zeros_like(acc)
    weight[...] = jnp.zeros_like(weight)
    grads[...] = jnp.zeros_like(grads)

    def position(p, carry):
        r = offs[p, 0, 0] + HALF
        c = offs[p, 0, 1] + HALF
        q = c // HALF
        s = c - q * HALF
        back_shift = lax.rem(HALF - s, HALF)
        keep = lanes < HALF - s
        q2 = jnp.minimum(q + 2, 3)

        def cut(i, carry):
            rows = pl.ds(pl.multiple_of(i * CH, CH), CH)
            w = []
            for d in range(2):
                src = pl.ds(r + i * CH, CH)
                a = pltpu.roll(ext[d, q, src, :], back_shift, 1)
                b = pltpu.roll(ext[d, q + 1, src, :], back_shift, 1)
                e = pltpu.roll(ext[d, q2, src, :], back_shift, 1)
                w.append(jnp.concatenate([jnp.where(keep, a, b), jnp.where(keep, b, e)], 1))
                win[d, rows, :] = w[d]
            weight[rows, :] += w[0] * w[0] + w[1] * w[1]
            for k in range(MODES):
                pr = probe[k, 0, rows, :]
                pi = probe[k, 1, rows, :]
                stack[k, rows, :] = (pr * w[0] - pi * w[1]).astype(BF)
                stack[k, pl.ds(pl.multiple_of(W + i * CH, CH), CH), :] = (pr * w[1] + pi * w[0]).astype(BF)
            return carry

        lax.fori_loop(0, W // CH, cut, 0, unroll=True)
        for k in range(MODES):
            rows_f = jnp.dot(fwd[...], stack[k], preferred_element_type=F32)
            side[k, :, 0:W] = rows_f[0:W].astype(BF)
            side[k, :, W:] = rows_f[W:].astype(BF)
        for k in range(MODES):
            far[k] = jnp.dot(side[k], bwd[...], preferred_element_type=F32)

        def project(i, carry):
            rows = pl.ds(pl.multiple_of(i * CH, CH), CH)
            rows_im = pl.ds(pl.multiple_of(W + i * CH, CH), CH)
            f = [far[k, rows, :] for k in range(MODES)]
            total = f[0] * f[0] + f[1] * f[1]
            intensity = total[:, 0:W] + total[:, W:]
            factor = amp[p, 0, rows, :] * lax.rsqrt(jnp.maximum(intensity, 0.0625))
            for k in range(MODES):
                stack[k, rows, :] = (f[k][:, 0:W] * factor).astype(BF)
                stack[k, rows_im, :] = (f[k][:, W:] * factor).astype(BF)
            return carry

        lax.fori_loop(0, W // CH, project, 0, unroll=True)
        for k in range(MODES):
            rows_b = jnp.dot(bwd[...], stack[k], preferred_element_type=F32)
            side[k, :, 0:W] = rows_b[0:W].astype(BF)
            side[k, :, W:] = rows_b[W:].astype(BF)
        for k in range(MODES):
            far[k] = jnp.dot(side[k], fwd[...], preferred_element_type=F32)

        def spread(i, carry):
            rows = pl.ds(pl.multiple_of(i * CH, CH), CH)
            wr = win[0, rows, :]
            wi = win[1, rows, :]
            power = jnp.zeros((CH, W), F32)
            tr = jnp.zeros((CH, W), F32)
            ti = jnp.zeros((CH, W), F32)
            for k in range(MODES):
                pr = probe[k, 0, rows, :]
                pi = probe[k, 1, rows, :]
                br = far[k, rows, 0:W]
                bi = far[k, rows, W:]
                power += pr * pr + pi * pi
                tr += pr * br + pi * bi
                ti += pr * bi - pi * br
                grads[2 * k, rows, :] += wr * br + wi * bi
                grads[2 * k + 1, rows, :] += wr * bi - wi * br
            dst = pl.ds(r + i * CH, CH)
            for d, t in ((0, tr - power * wr), (1, ti - power * wi)):
                a = pltpu.roll(t[:, 0:HALF], s, 1)
                b = pltpu.roll(t[:, HALF:], s, 1)
                low = lanes < s
                acc[d, q, dst, :] += jnp.where(low, 0.0, a)
                acc[d, q + 1, dst, :] += jnp.where(low, a, b)
                acc[d, q2, dst, :] += jnp.where(low, b, 0.0)
            return carry

        lax.fori_loop(0, W // CH, spread, 0, unroll=True)
        return carry

    lax.fori_loop(0, POS, position, 0)
    out_left[...] = acc[:, 0]
    out_mid[:, :, 0:HALF] = acc[:, 1]
    out_mid[:, :, HALF:] = acc[:, 2]
    out_right[...] = acc[:, 3]
    h = half[0]
    for out, side_of in ((mine, h), (other, 1 - h)):

        def flush(i, carry):
            rows = pl.ds(pl.multiple_of(side_of * HALF + i * 8, 8), 8)
            for n in range(2 * MODES):
                out[i, n] = grads[n, rows, :]
            out[i, 2 * MODES] = weight[rows, :]
            return carry

        lax.fori_loop(0, 16, flush, 0)


def correct(offsets, half, border, probe, amplitude):
    fwd, bwd = dft_matrices()
    vmem = pl.BlockSpec(memory_space=pltpu.VMEM)
    smem = pl.BlockSpec(memory_space=pltpu.SMEM)
    part = jax.ShapeDtypeStruct((16, 2 * MODES + 1, 8, W), F32)
    strip = jax.ShapeDtypeStruct((2, 2 * W, HALF), F32)
    return pl.pallas_call(
        kernel,
        out_shape=(part, part, strip, jax.ShapeDtypeStruct((2, 2 * W, W), F32), strip),
        in_specs=[smem, smem] + [vmem] * 11,
        out_specs=(vmem,) * 5,
        scratch_shapes=[
            pltpu.VMEM((2, 4, 2 * W, HALF), F32),
            pltpu.VMEM((2, 4, 2 * W, HALF), F32),
            pltpu.VMEM((2, W, W), F32),
            pltpu.VMEM((MODES, 2 * W, W), BF),
            pltpu.VMEM((MODES, W, 2 * W), BF),
            pltpu.VMEM((MODES, W, 2 * W), F32),
            pltpu.VMEM((W, W), F32),
            pltpu.VMEM((2 * MODES, W, W), F32),
        ],
        compiler_params=pltpu.CompilerParams(vmem_limit_bytes=20 << 20),
    )(offsets, half, *border, probe, amplitude, jnp.asarray(fwd), jnp.asarray(bwd))


GX = ("z", "xl")
GY = ("xh", "y", "co")
UP = [(i, (i + 1) % 16) for i in range(16)]
DOWN = [(j, i) for i, j in UP]
SWAP = [(0, 1), (1, 0)]


def arrange_kernel(half, own, swapped, out):
    h = half[0]
    for source, side_of in ((own, h), (swapped, 1 - h)):
        for i in range(16):
            rows = pl.ds(pl.multiple_of(side_of * HALF + i * 8, 8), 8)
            for n in range(2 * MODES):
                out[n // 2, n % 2, rows, :] = source[i, n]


def arrange(half, own, swapped):
    vmem = pl.BlockSpec(memory_space=pltpu.VMEM)
    return pl.pallas_call(
        arrange_kernel,
        out_shape=jax.ShapeDtypeStruct((MODES, 2, W, W), F32),
        in_specs=[pl.BlockSpec(memory_space=pltpu.SMEM), vmem, vmem],
        out_specs=vmem,
        compiler_params=pltpu.CompilerParams(vmem_limit_bytes=4 << 20),
    )(half, own, swapped)


def body(object_field, probe_field, amplitude, offsets):
    first, last = slice(0, HALF), slice(HALF, W)
    top = lax.ppermute(object_field[:, last], GX, UP)
    bot = lax.ppermute(object_field[:, first], GX, DOWN)
    left = lax.ppermute(object_field[:, :, last], GY, UP)
    right = lax.ppermute(object_field[:, :, first], GY, DOWN)
    left_ends = lax.ppermute(jnp.stack([top[:, :, last], bot[:, :, last]]), GY, UP)
    right_ends = lax.ppermute(jnp.stack([top[:, :, first], bot[:, :, first]]), GY, DOWN)
    co = lax.axis_index("co")
    half = co.reshape(1)
    scale_max = jnp.max(jnp.sum(probe_field * probe_field, axis=(0, 1))) + 1e-06
    half, scale_max = lax.optimization_barrier((half, scale_max))
    border = (object_field, top, bot, left, right, left_ends, right_ends)
    mine, other, out_left, out_mid, out_right = correct(offsets, half, border, probe_field, amplitude)
    group = ("xh", "xl", "y")
    part = mine + lax.ppermute(other, "co", SWAP)
    part = jnp.sum(lax.all_to_all(part, group, 0, 0, tiled=True), 0)
    part, out_left, out_right = lax.optimization_barrier((part, out_left, out_right))
    from_right = lax.ppermute(out_left, GY, DOWN)
    from_left = lax.ppermute(out_right, GY, UP)
    peers = [lax.ppermute(part, "z", [(i, i ^ step) for i in range(8)]) for step in (1, 2, 3)]
    part = (part + peers[0]) + (peers[1] + peers[2])
    part = part + lax.ppermute(part, "z", [(i, i ^ 4) for i in range(8)])
    block = co * 16 + lax.axis_index(group)
    planes = probe_field.reshape(2 * MODES, W, W)
    local = lax.dynamic_slice_in_dim(planes, block * 8, 8, 1)
    weight = part[2 * MODES]
    local = local + (part[: 2 * MODES] - local * weight) / (weight + 1e-05)
    folded = out_mid + jnp.concatenate([from_left, from_right], 2)
    local, folded = lax.optimization_barrier((local, folded))
    from_below = lax.ppermute(folded[:, :HALF], GX, DOWN)
    from_above = lax.ppermute(folded[:, HALF + W :], GX, UP)
    gathered = lax.all_to_all(jnp.broadcast_to(local[None], (16,) + local.shape), group, 0, 0, tiled=True)
    gathered, from_below, from_above = lax.optimization_barrier((gathered, from_below, from_above))
    updated_probe = arrange(half, gathered, lax.ppermute(gathered, "co", SWAP))
    object_step = folded[:, HALF : HALF + W] + jnp.concatenate([from_above, from_below], 1)
    return (object_field + object_step / scale_max, updated_probe)


def solution(mesh):
    fine = Mesh(mesh.devices.reshape(8, 2, 2, 4, 2), ("z", "xl", "xh", "y", "co"))
    in_specs = (P(None, GX, GY), P(), P(GX, GY, None, None), P(GX, GY, None))
    out_specs = (P(None, GX, GY), P())
    return jax.shard_map(body, mesh=fine, in_specs=in_specs, out_specs=out_specs, check_vma=False)
```

```python
import functools
import math

import jax
import jax.numpy as jnp
import ml_dtypes
import numpy as np
from jax import lax
from jax.experimental import pallas as pl
from jax.experimental.pallas import tpu as pltpu
from jax.sharding import Mesh
from jax.sharding import PartitionSpec as P

W = 256
HALF = 128
POS = 4
MODES = 2
CH = 32
BF = jnp.bfloat16
F32 = jnp.float32


def dft_matrices():
    k = np.arange(W)
    phase = (k[:, None] * k[None, :]) % W
    angle = phase.astype(np.float32) * np.float32(2.0 * math.pi / W)
    norm = np.float32(1.0 / math.sqrt(W))
    c = (np.cos(angle) * norm).astype(ml_dtypes.bfloat16)
    s = (np.sin(angle) * norm).astype(ml_dtypes.bfloat16)
    fwd = np.block([[c, s], [-s, c]])
    bwd = np.block([[c, -s], [s, c]])
    return fwd, bwd


def kernel(
    offs, half, tile, top, bot, left, right, left_ends, right_ends, probe, amp, fwd_hbm, bwd_hbm,
    mine, other, out_left, out_mid, out_right,
    ext, acc, win, stack, side, far, weight, grads, power, fwd, bwd, sems,
):
    copies = [
        pltpu.make_async_copy(fwd_hbm, fwd, sems.at[0]),
        pltpu.make_async_copy(bwd_hbm, bwd, sems.at[1]),
    ]
    for copy in copies:
        copy.start()
    lanes = lax.broadcasted_iota(jnp.int32, (CH, HALF), 1)
    for q in range(2):
        cols = pl.ds(q * HALF, HALF)
        ext[:, q + 1, 0:HALF, :] = top[:, :, cols]
        ext[:, q + 1, HALF : HALF + W, :] = tile[:, :, cols]
        ext[:, q + 1, HALF + W :, :] = bot[:, :, cols]
    for q, middle, ends in ((0, left, left_ends), (3, right, right_ends)):
        ext[:, q, 0:HALF, :] = ends[0]
        ext[:, q, HALF : HALF + W, :] = middle[...]
        ext[:, q, HALF + W :, :] = ends[1]
    acc[...] = jnp.zeros_like(acc)
    weight[...] = jnp.zeros_like(weight)
    grads[...] = jnp.zeros_like(grads)
    top_power = jnp.zeros((CH, W), F32)
    for i in range(W // CH):
        rows = pl.ds(i * CH, CH)
        total = jnp.zeros((CH, W), F32)
        for k in range(MODES):
            total += probe[k, 0, rows, :] * probe[k, 0, rows, :] + probe[k, 1, rows, :] * probe[k, 1, rows, :]
        power[rows, :] = total
        top_power = jnp.maximum(top_power, total)
    scale = 1.0 / (jnp.max(top_power, axis=(0, 1), keepdims=True) + 1e-06)
    for copy in copies:
        copy.wait()

    def position(p, carry):
        r = offs[2 * p] + HALF
        c = offs[2 * p + 1] + HALF
        q = c // HALF
        s = c - q * HALF
        back_shift = lax.rem(HALF - s, HALF)
        keep = lanes < HALF - s
        q2 = jnp.minimum(q + 2, 3)

        def cut(i, carry):
            rows = pl.ds(pl.multiple_of(i * CH, CH), CH)
            w = []
            for d in range(2):
                src = pl.ds(r + i * CH, CH)
                a = pltpu.roll(ext[d, q, src, :], back_shift, 1)
                b = pltpu.roll(ext[d, q + 1, src, :], back_shift, 1)
                e = pltpu.roll(ext[d, q2, src, :], back_shift, 1)
                w.append(jnp.concatenate([jnp.where(keep, a, b), jnp.where(keep, b, e)], 1))
                win[d, rows, :] = w[d]
            weight[rows, :] += w[0] * w[0] + w[1] * w[1]
            for k in range(MODES):
                pr = probe[k, 0, rows, :]
                pi = probe[k, 1, rows, :]
                stack[k, rows, :] = (pr * w[0] - pi * w[1]).astype(BF)
                stack[k, pl.ds(pl.multiple_of(W + i * CH, CH), CH), :] = (pr * w[1] + pi * w[0]).astype(BF)
            return carry

        lax.fori_loop(0, W // CH, cut, 0, unroll=True)
        for k in range(MODES):
            rows_f = jnp.dot(fwd[...], stack[k], preferred_element_type=F32)
            side[k, :, 0:W] = rows_f[0:W].astype(BF)
            side[k, :, W:] = rows_f[W:].astype(BF)
        for k in range(MODES):
            far[k] = jnp.dot(side[k], bwd[...], preferred_element_type=F32)

        def project(i, carry):
            rows = pl.ds(pl.multiple_of(i * CH, CH), CH)
            rows_im = pl.ds(pl.multiple_of(W + i * CH, CH), CH)
            f = [far[k, rows, :] for k in range(MODES)]
            total = f[0] * f[0] + f[1] * f[1]
            intensity = total[:, 0:W] + total[:, W:]
            factor = amp[p, 0, rows, :] * lax.rsqrt(jnp.maximum(intensity, 0.0625))
            for k in range(MODES):
                stack[k, rows, :] = (f[k][:, 0:W] * factor).astype(BF)
                stack[k, rows_im, :] = (f[k][:, W:] * factor).astype(BF)
            return carry

        lax.fori_loop(0, W // CH, project, 0, unroll=True)
        for k in range(MODES):
            rows_b = jnp.dot(bwd[...], stack[k], preferred_element_type=F32)
            side[k, :, 0:W] = rows_b[0:W].astype(BF)
            side[k, :, W:] = rows_b[W:].astype(BF)
        for k in range(MODES):
            far[k] = jnp.dot(side[k], fwd[...], preferred_element_type=F32)

        def spread(i, carry):
            rows = pl.ds(pl.multiple_of(i * CH, CH), CH)
            wr = win[0, rows, :]
            wi = win[1, rows, :]
            both = power[rows, :]
            tr = jnp.zeros((CH, W), F32)
            ti = jnp.zeros((CH, W), F32)
            for k in range(MODES):
                pr = probe[k, 0, rows, :]
                pi = probe[k, 1, rows, :]
                br = far[k, rows, 0:W]
                bi = far[k, rows, W:]
                tr += pr * br + pi * bi
                ti += pr * bi - pi * br
                grads[2 * k, rows, :] += wr * br + wi * bi
                grads[2 * k + 1, rows, :] += wr * bi - wi * br
            dst = pl.ds(r + i * CH, CH)
            for d, t in ((0, tr - both * wr), (1, ti - both * wi)):
                a = pltpu.roll(t[:, 0:HALF], s, 1)
                b = pltpu.roll(t[:, HALF:], s, 1)
                low = lanes < s
                acc[d, q, dst, :] += jnp.where(low, 0.0, a)
                acc[d, q + 1, dst, :] += jnp.where(low, a, b)
                acc[d, q2, dst, :] += jnp.where(low, b, 0.0)
            return carry

        lax.fori_loop(0, W // CH, spread, 0, unroll=True)
        return carry

    lax.fori_loop(0, POS, position, 0)
    for d in range(2):
        for i in range(2 * W // HALF):
            rows = pl.ds(i * HALF, HALF)
            out_left[d, rows, :] = acc[d, 0, rows, :] * scale
            out_right[d, rows, :] = acc[d, 3, rows, :] * scale
            for q in range(2):
                cols = pl.ds(q * HALF, HALF)
                step = acc[d, q + 1, rows, :] * scale
                if 1 <= i <= 2:
                    step += tile[d, pl.ds((i - 1) * HALF, HALF), cols]
                out_mid[d, rows, cols] = step
    h = half[0]
    for out, side_of in ((mine, h), (other, 1 - h)):

        def flush(i, carry):
            rows = pl.ds(pl.multiple_of(side_of * HALF + i * 8, 8), 8)
            for n in range(2 * MODES):
                out[i, n] = grads[n, rows, :]
            out[i, 2 * MODES] = weight[rows, :]
            return carry

        lax.fori_loop(0, 16, flush, 0)


def correct(offsets, half, border, probe, amplitude):
    fwd, bwd = dft_matrices()
    vmem = pl.BlockSpec(memory_space=pltpu.VMEM)
    smem = pl.BlockSpec(memory_space=pltpu.SMEM)
    part = jax.ShapeDtypeStruct((16, 2 * MODES + 1, 8, W), F32)
    strip = jax.ShapeDtypeStruct((2, 2 * W, HALF), F32)
    return pl.pallas_call(
        kernel,
        out_shape=(part, part, strip, jax.ShapeDtypeStruct((2, 2 * W, W), F32), strip),
        in_specs=[smem, smem] + [vmem] * 9 + [pl.BlockSpec(memory_space=pl.ANY)] * 2,
        out_specs=(vmem,) * 5,
        scratch_shapes=[
            pltpu.VMEM((2, 4, 2 * W, HALF), F32),
            pltpu.VMEM((2, 4, 2 * W, HALF), F32),
            pltpu.VMEM((2, W, W), F32),
            pltpu.VMEM((MODES, 2 * W, W), BF),
            pltpu.VMEM((MODES, W, 2 * W), BF),
            pltpu.VMEM((MODES, W, 2 * W), F32),
            pltpu.VMEM((W, W), F32),
            pltpu.VMEM((2 * MODES, W, W), F32),
            pltpu.VMEM((W, W), F32),
            pltpu.VMEM((2 * W, 2 * W), BF),
            pltpu.VMEM((2 * W, 2 * W), BF),
            pltpu.SemaphoreType.DMA((2,)),
        ],
        compiler_params=pltpu.CompilerParams(vmem_limit_bytes=20 << 20),
    )(offsets, half, *border, probe, amplitude, jnp.asarray(fwd), jnp.asarray(bwd))


GX = ("z", "xl")
GY = ("xh", "y", "co")
UP = [(i, (i + 1) % 16) for i in range(16)]
DOWN = [(j, i) for i, j in UP]
SWAP = [(0, 1), (1, 0)]


def arrange_kernel(half, own, swapped, out):
    h = half[0]
    for source, side_of in ((own, h), (swapped, 1 - h)):
        for i in range(16):
            rows = pl.ds(pl.multiple_of(side_of * HALF + i * 8, 8), 8)
            for n in range(2 * MODES):
                out[n // 2, n % 2, rows, :] = source[i, n]


def arrange(half, own, swapped):
    vmem = pl.BlockSpec(memory_space=pltpu.VMEM)
    return pl.pallas_call(
        arrange_kernel,
        out_shape=jax.ShapeDtypeStruct((MODES, 2, W, W), F32),
        in_specs=[pl.BlockSpec(memory_space=pltpu.SMEM), vmem, vmem],
        out_specs=vmem,
        compiler_params=pltpu.CompilerParams(vmem_limit_bytes=4 << 20),
    )(half, own, swapped)


def body(object_field, probe_field, amplitude, offsets):
    group = ("xh", "xl", "y")
    co = lax.axis_index("co")
    half = co.reshape(1)
    block = (co * 16 + lax.axis_index(group)) * 8
    offs = offsets.reshape(2 * POS)
    object_field, half, block, offs = lax.optimization_barrier((object_field, half, block, offs))
    first, last = slice(0, HALF), slice(HALF, W)
    top = lax.ppermute(object_field[:, last], GX, UP)
    bot = lax.ppermute(object_field[:, first], GX, DOWN)
    left = lax.ppermute(object_field[:, :, last], GY, UP)
    right = lax.ppermute(object_field[:, :, first], GY, DOWN)
    left_ends = lax.ppermute(jnp.stack([top[:, :, last], bot[:, :, last]]), GY, UP)
    right_ends = lax.ppermute(jnp.stack([top[:, :, first], bot[:, :, first]]), GY, DOWN)
    border = (object_field, top, bot, left, right, left_ends, right_ends)
    mine, other, out_left, out_mid, out_right = correct(offs, half, border, probe_field, amplitude)
    from_right = lax.ppermute(out_left, GY, DOWN)
    from_left = lax.ppermute(out_right, GY, UP)
    part = mine + lax.ppermute(other, "co", SWAP)
    pieces = lax.all_to_all(part, group, 0, 0, tiled=True)
    part = sum(pieces[i] for i in range(16))
    part, from_left, from_right = lax.optimization_barrier((part, from_left, from_right))
    folded = out_mid + jnp.concatenate([from_left, from_right], 2)
    from_below = lax.ppermute(folded[:, :HALF], GX, DOWN)
    from_above = lax.ppermute(folded[:, HALF + W :], GX, UP)
    peers = [lax.ppermute(part, "z", [(i, i ^ step) for i in range(8)]) for step in (1, 2, 3)]
    part = (part + peers[0]) + (peers[1] + peers[2])
    part, from_below, from_above = lax.optimization_barrier((part, from_below, from_above))
    part = part + lax.ppermute(part, "z", [(i, i ^ 4) for i in range(8)])
    planes = probe_field.reshape(2 * MODES, W, W)
    local = lax.dynamic_slice_in_dim(planes, block, 8, 1)
    weight = part[2 * MODES]
    local = local + (part[: 2 * MODES] - local * weight) / (weight + 1e-05)
    gathered = lax.all_to_all(jnp.broadcast_to(local[None], (16,) + local.shape), group, 0, 0, tiled=True)
    updated_object = folded[:, HALF : HALF + W] + jnp.concatenate([from_above, from_below], 1)
    updated_probe = arrange(half, gathered, lax.ppermute(gathered, "co", SWAP))
    return (updated_object, updated_probe)


def solution(mesh):
    fine = Mesh(mesh.devices.reshape(8, 2, 2, 4, 2), ("z", "xl", "xh", "y", "co"))
    in_specs = (P(None, GX, GY), P(), P(GX, GY, None, None), P(GX, GY, None))
    out_specs = (P(None, GX, GY), P())
    return jax.shard_map(body, mesh=fine, in_specs=in_specs, out_specs=out_specs, check_vma=False)
```

```python
import functools
import math

import jax
import jax.numpy as jnp
import ml_dtypes
import numpy as np
from jax import lax
from jax.experimental import pallas as pl
from jax.experimental.pallas import tpu as pltpu
from jax.sharding import Mesh
from jax.sharding import PartitionSpec as P

W = 256
HALF = 128
POS = 4
MODES = 2
CH = 32
BF = jnp.bfloat16
F32 = jnp.float32


def dft_matrices():
    k = np.arange(W)
    phase = (k[:, None] * k[None, :]) % W
    angle = phase.astype(np.float32) * np.float32(2.0 * math.pi / W)
    norm = np.float32(1.0 / math.sqrt(W))
    c = (np.cos(angle) * norm).astype(ml_dtypes.bfloat16)
    s = (np.sin(angle) * norm).astype(ml_dtypes.bfloat16)
    fwd = np.block([[c, s], [-s, c]])
    bwd = np.block([[c, -s], [s, c]])
    return fwd, bwd


def kernel(
    offs, half, tile, top, bot, left, right, left_ends, right_ends, probe, amp, fwd_hbm, bwd_hbm,
    mine, other, out_left, out_mid, out_right,
    ext, acc, win, stack, side, far, weight, grads, power, fwd, bwd, sems,
):
    copies = [
        pltpu.make_async_copy(fwd_hbm, fwd, sems.at[0]),
        pltpu.make_async_copy(bwd_hbm, bwd, sems.at[1]),
    ]
    for copy in copies:
        copy.start()
    lanes = lax.broadcasted_iota(jnp.int32, (CH, HALF), 1)
    for q in range(2):
        cols = pl.ds(q * HALF, HALF)
        ext[:, q + 1, 0:HALF, :] = top[:, :, cols]
        ext[:, q + 1, HALF : HALF + W, :] = tile[:, :, cols]
        ext[:, q + 1, HALF + W :, :] = bot[:, :, cols]
    for q, middle, ends in ((0, left, left_ends), (3, right, right_ends)):
        ext[:, q, 0:HALF, :] = ends[0]
        ext[:, q, HALF : HALF + W, :] = middle[...]
        ext[:, q, HALF + W :, :] = ends[1]
    acc[...] = jnp.zeros_like(acc)
    weight[...] = jnp.zeros_like(weight)
    grads[...] = jnp.zeros_like(grads)
    top_power = jnp.zeros((CH, W), F32)
    for i in range(W // CH):
        rows = pl.ds(i * CH, CH)
        total = jnp.zeros((CH, W), F32)
        for k in range(MODES):
            total += probe[k, 0, rows, :] * probe[k, 0, rows, :] + probe[k, 1, rows, :] * probe[k, 1, rows, :]
        power[rows, :] = total
        top_power = jnp.maximum(top_power, total)
    scale = 1.0 / (jnp.max(top_power, axis=(0, 1), keepdims=True) + 1e-06)
    for copy in copies:
        copy.wait()

    def position(p, carry):
        r = offs[0, p] + HALF
        c = offs[1, p] + HALF
        q = c // HALF
        s = c - q * HALF
        back_shift = lax.rem(HALF - s, HALF)
        keep = lanes < HALF - s
        q2 = jnp.minimum(q + 2, 3)

        def cut(i, carry):
            rows = pl.ds(pl.multiple_of(i * CH, CH), CH)
            w = []
            for d in range(2):
                src = pl.ds(r + i * CH, CH)
                a = pltpu.roll(ext[d, q, src, :], back_shift, 1)
                b = pltpu.roll(ext[d, q + 1, src, :], back_shift, 1)
                e = pltpu.roll(ext[d, q2, src, :], back_shift, 1)
                w.append(jnp.concatenate([jnp.where(keep, a, b), jnp.where(keep, b, e)], 1))
                win[d, rows, :] = w[d]
            weight[rows, :] += w[0] * w[0] + w[1] * w[1]
            for k in range(MODES):
                pr = probe[k, 0, rows, :]
                pi = probe[k, 1, rows, :]
                stack[k, rows, :] = (pr * w[0] - pi * w[1]).astype(BF)
                stack[k, pl.ds(pl.multiple_of(W + i * CH, CH), CH), :] = (pr * w[1] + pi * w[0]).astype(BF)
            return carry

        lax.fori_loop(0, W // CH, cut, 0, unroll=True)
        for k in range(MODES):
            rows_f = jnp.dot(fwd[...], stack[k], preferred_element_type=F32)
            side[k, :, 0:W] = rows_f[0:W].astype(BF)
            side[k, :, W:] = rows_f[W:].astype(BF)
        for k in range(MODES):
            far[k] = jnp.dot(side[k], bwd[...], preferred_element_type=F32)

        def project(i, carry):
            rows = pl.ds(pl.multiple_of(i * CH, CH), CH)
            rows_im = pl.ds(pl.multiple_of(W + i * CH, CH), CH)
            f = [far[k, rows, :] for k in range(MODES)]
            total = f[0] * f[0] + f[1] * f[1]
            intensity = total[:, 0:W] + total[:, W:]
            factor = amp[p, 0, rows, :] * lax.rsqrt(jnp.maximum(intensity, 0.0625))
            for k in range(MODES):
                stack[k, rows, :] = (f[k][:, 0:W] * factor).astype(BF)
                stack[k, rows_im, :] = (f[k][:, W:] * factor).astype(BF)
            return carry

        lax.fori_loop(0, W // CH, project, 0, unroll=True)
        for k in range(MODES):
            rows_b = jnp.dot(bwd[...], stack[k], preferred_element_type=F32)
            side[k, :, 0:W] = rows_b[0:W].astype(BF)
            side[k, :, W:] = rows_b[W:].astype(BF)
        for k in range(MODES):
            far[k] = jnp.dot(side[k], fwd[...], preferred_element_type=F32)

        def spread(i, carry):
            rows = pl.ds(pl.multiple_of(i * CH, CH), CH)
            wr = win[0, rows, :]
            wi = win[1, rows, :]
            both = power[rows, :]
            tr = jnp.zeros((CH, W), F32)
            ti = jnp.zeros((CH, W), F32)
            for k in range(MODES):
                pr = probe[k, 0, rows, :]
                pi = probe[k, 1, rows, :]
                br = far[k, rows, 0:W]
                bi = far[k, rows, W:]
                tr += pr * br + pi * bi
                ti += pr * bi - pi * br
                grads[2 * k, rows, :] += wr * br + wi * bi
                grads[2 * k + 1, rows, :] += wr * bi - wi * br
            dst = pl.ds(r + i * CH, CH)
            for d, t in ((0, tr - both * wr), (1, ti - both * wi)):
                a = pltpu.roll(t[:, 0:HALF], s, 1)
                b = pltpu.roll(t[:, HALF:], s, 1)
                low = lanes < s
                acc[d, q, dst, :] += jnp.where(low, 0.0, a)
                acc[d, q + 1, dst, :] += jnp.where(low, a, b)
                acc[d, q2, dst, :] += jnp.where(low, b, 0.0)
            return carry

        lax.fori_loop(0, W // CH, spread, 0, unroll=True)
        return carry

    lax.fori_loop(0, POS, position, 0)
    for d in range(2):
        for i in range(2 * W // HALF):
            rows = pl.ds(i * HALF, HALF)
            out_left[d, rows, :] = acc[d, 0, rows, :] * scale
            out_right[d, rows, :] = acc[d, 3, rows, :] * scale
            for q in range(2):
                cols = pl.ds(q * HALF, HALF)
                step = acc[d, q + 1, rows, :] * scale
                if 1 <= i <= 2:
                    step += tile[d, pl.ds((i - 1) * HALF, HALF), cols]
                out_mid[d, rows, cols] = step
    h = half[0]
    for out, side_of in ((mine, h), (other, 1 - h)):

        def flush(i, carry):
            rows = pl.ds(pl.multiple_of(side_of * HALF + i * 8, 8), 8)
            for n in range(2 * MODES):
                out[i, n] = grads[n, rows, :]
            out[i, 2 * MODES] = weight[rows, :]
            return carry

        lax.fori_loop(0, 16, flush, 0)


def correct(offsets, half, border, probe, amplitude):
    fwd, bwd = dft_matrices()
    vmem = pl.BlockSpec(memory_space=pltpu.VMEM)
    smem = pl.BlockSpec(memory_space=pltpu.SMEM)
    part = jax.ShapeDtypeStruct((16, 2 * MODES + 1, 8, W), F32)
    strip = jax.ShapeDtypeStruct((2, 2 * W, HALF), F32)
    return pl.pallas_call(
        kernel,
        out_shape=(part, part, strip, jax.ShapeDtypeStruct((2, 2 * W, W), F32), strip),
        in_specs=[smem, smem] + [vmem] * 9 + [pl.BlockSpec(memory_space=pl.ANY)] * 2,
        out_specs=(vmem,) * 5,
        scratch_shapes=[
            pltpu.VMEM((2, 4, 2 * W, HALF), F32),
            pltpu.VMEM((2, 4, 2 * W, HALF), F32),
            pltpu.VMEM((2, W, W), F32),
            pltpu.VMEM((MODES, 2 * W, W), BF),
            pltpu.VMEM((MODES, W, 2 * W), BF),
            pltpu.VMEM((MODES, W, 2 * W), F32),
            pltpu.VMEM((W, W), F32),
            pltpu.VMEM((2 * MODES, W, W), F32),
            pltpu.VMEM((W, W), F32),
            pltpu.VMEM((2 * W, 2 * W), BF),
            pltpu.VMEM((2 * W, 2 * W), BF),
            pltpu.SemaphoreType.DMA((2,)),
        ],
        compiler_params=pltpu.CompilerParams(vmem_limit_bytes=20 << 20),
    )(offsets, half, *border, probe, amplitude, jnp.asarray(fwd), jnp.asarray(bwd))


GX = ("z", "xl")
GY = ("xh", "y", "co")
UP = [(i, (i + 1) % 16) for i in range(16)]
DOWN = [(j, i) for i, j in UP]
SWAP = [(0, 1), (1, 0)]


def arrange_kernel(half, own, swapped, out):
    h = half[0]
    for source, side_of in ((own, h), (swapped, 1 - h)):
        for i in range(16):
            rows = pl.ds(pl.multiple_of(side_of * HALF + i * 8, 8), 8)
            for n in range(2 * MODES):
                out[n // 2, n % 2, rows, :] = source[i, n]


def arrange(half, own, swapped):
    vmem = pl.BlockSpec(memory_space=pltpu.VMEM)
    return pl.pallas_call(
        arrange_kernel,
        out_shape=jax.ShapeDtypeStruct((MODES, 2, W, W), F32),
        in_specs=[pl.BlockSpec(memory_space=pltpu.SMEM), vmem, vmem],
        out_specs=vmem,
        compiler_params=pltpu.CompilerParams(vmem_limit_bytes=4 << 20),
    )(half, own, swapped)


def body(object_field, probe_field, amplitude, offsets):
    group = ("xh", "xl", "y")
    co = lax.axis_index("co")
    half = co.reshape(1)
    block = (co * 16 + lax.axis_index(group)) * 8
    offs = offsets.transpose(1, 2, 0).reshape(2, POS)
    object_field, half, block = lax.optimization_barrier((object_field, half, block))
    first, last = slice(0, HALF), slice(HALF, W)
    top = lax.ppermute(object_field[:, last], GX, UP)
    bot = lax.ppermute(object_field[:, first], GX, DOWN)
    left = lax.ppermute(object_field[:, :, last], GY, UP)
    right = lax.ppermute(object_field[:, :, first], GY, DOWN)
    left_ends = lax.ppermute(jnp.stack([top[:, :, last], bot[:, :, last]]), GY, UP)
    right_ends = lax.ppermute(jnp.stack([top[:, :, first], bot[:, :, first]]), GY, DOWN)
    border = (object_field, top, bot, left, right, left_ends, right_ends)
    mine, other, out_left, out_mid, out_right = correct(offs, half, border, probe_field, amplitude)
    part = mine + lax.ppermute(other, "co", SWAP)
    from_right = lax.ppermute(out_left, GY, DOWN)
    from_left = lax.ppermute(out_right, GY, UP)
    pieces = lax.all_to_all(part, group, 0, 0, tiled=True)
    part = sum(pieces[i] for i in range(16))
    folded = out_mid + jnp.concatenate([from_left, from_right], 2)
    part, folded = lax.optimization_barrier((part, folded))
    from_below = lax.ppermute(folded[:, :HALF], GX, DOWN)
    from_above = lax.ppermute(folded[:, HALF + W :], GX, UP)
    peers = [lax.ppermute(part, "z", [(i, i ^ step) for i in range(8)]) for step in (2, 4, 6)]
    part = (part + peers[0]) + (peers[1] + peers[2])
    part = part + lax.ppermute(part, "z", [(i, i ^ 1) for i in range(8)])
    part, from_below, from_above = lax.optimization_barrier((part, from_below, from_above))
    planes = probe_field.reshape(2 * MODES, W, W)
    local = lax.dynamic_slice_in_dim(planes, block, 8, 1)
    weight = part[2 * MODES]
    local = local + (part[: 2 * MODES] - local * weight) / (weight + 1e-05)
    gathered = lax.all_to_all(jnp.broadcast_to(local[None], (16,) + local.shape), group, 0, 0, tiled=True)
    updated_object = folded[:, HALF : HALF + W] + jnp.concatenate([from_above, from_below], 1)
    updated_probe = arrange(half, gathered, lax.ppermute(gathered, "co", SWAP))
    return (updated_object, updated_probe)


def solution(mesh):
    fine = Mesh(mesh.devices.reshape(8, 2, 2, 4, 2), ("z", "xl", "xh", "y", "co"))
    in_specs = (P(None, GX, GY), P(), P(GX, GY, None, None), P(GX, GY, None))
    out_specs = (P(None, GX, GY), P())
    return jax.shard_map(body, mesh=fine, in_specs=in_specs, out_specs=out_specs, check_vma=False)
```

```python
import functools
import math

import jax
import jax.numpy as jnp
import ml_dtypes
import numpy as np
from jax import lax
from jax.experimental import pallas as pl
from jax.experimental.pallas import tpu as pltpu
from jax.sharding import Mesh
from jax.sharding import PartitionSpec as P

W = 256
HALF = 128
POS = 4
MODES = 2
CH = 32
BF = jnp.bfloat16
F32 = jnp.float32


def dft_matrices():
    k = np.arange(W)
    phase = (k[:, None] * k[None, :]) % W
    angle = phase.astype(np.float32) * np.float32(2.0 * math.pi / W)
    norm = np.float32(1.0 / math.sqrt(W))
    c = (np.cos(angle) * norm).astype(ml_dtypes.bfloat16)
    s = (np.sin(angle) * norm).astype(ml_dtypes.bfloat16)
    fwd = np.block([[c, s], [-s, c]])
    bwd = np.block([[c, -s], [s, c]])
    return fwd, bwd


def kernel(
    offs, half, tile, top, bot, left, right, left_ends, right_ends, probe, amp, fwd_hbm, bwd_hbm,
    mine, other, out_left, out_mid, out_right,
    ext, acc, win, stack, side, far, weight, grads, power, fwd, bwd, sems,
):
    copies = [
        pltpu.make_async_copy(fwd_hbm, fwd, sems.at[0]),
        pltpu.make_async_copy(bwd_hbm, bwd, sems.at[1]),
    ]
    for copy in copies:
        copy.start()
    lanes = lax.broadcasted_iota(jnp.int32, (CH, HALF), 1)
    for q in range(2):
        cols = pl.ds(q * HALF, HALF)
        ext[:, q + 1, 0:HALF, :] = top[:, :, cols]
        ext[:, q + 1, HALF : HALF + W, :] = tile[:, :, cols]
        ext[:, q + 1, HALF + W :, :] = bot[:, :, cols]
    for q, middle, ends in ((0, left, left_ends), (3, right, right_ends)):
        ext[:, q, 0:HALF, :] = ends[0]
        ext[:, q, HALF : HALF + W, :] = middle[...]
        ext[:, q, HALF + W :, :] = ends[1]
    acc[...] = jnp.zeros_like(acc)
    weight[...] = jnp.zeros_like(weight)
    grads[...] = jnp.zeros_like(grads)
    top_power = jnp.zeros((CH, W), F32)
    for i in range(W // CH):
        rows = pl.ds(i * CH, CH)
        total = jnp.zeros((CH, W), F32)
        for k in range(MODES):
            total += probe[k, 0, rows, :] * probe[k, 0, rows, :] + probe[k, 1, rows, :] * probe[k, 1, rows, :]
        power[rows, :] = total
        top_power = jnp.maximum(top_power, total)
    scale = 1.0 / (jnp.max(top_power, axis=(0, 1), keepdims=True) + 1e-06)
    for copy in copies:
        copy.wait()

    def position(p, carry):
        r = offs[0, p] + HALF
        c = offs[1, p] + HALF
        q = c // HALF
        s = c - q * HALF
        back_shift = lax.rem(HALF - s, HALF)
        keep = lanes < HALF - s
        q2 = jnp.minimum(q + 2, 3)

        def cut(i, carry):
            rows = pl.ds(pl.multiple_of(i * CH, CH), CH)
            w = []
            for d in range(2):
                src = pl.ds(r + i * CH, CH)
                a = pltpu.roll(ext[d, q, src, :], back_shift, 1)
                b = pltpu.roll(ext[d, q + 1, src, :], back_shift, 1)
                e = pltpu.roll(ext[d, q2, src, :], back_shift, 1)
                w.append(jnp.concatenate([jnp.where(keep, a, b), jnp.where(keep, b, e)], 1))
                win[d, rows, :] = w[d]
            weight[rows, :] += w[0] * w[0] + w[1] * w[1]
            for k in range(MODES):
                pr = probe[k, 0, rows, :]
                pi = probe[k, 1, rows, :]
                stack[k, rows, :] = (pr * w[0] - pi * w[1]).astype(BF)
                stack[k, pl.ds(pl.multiple_of(W + i * CH, CH), CH), :] = (pr * w[1] + pi * w[0]).astype(BF)
            return carry

        lax.fori_loop(0, W // CH, cut, 0, unroll=True)
        for k in range(MODES):
            rows_f = jnp.dot(fwd[...], stack[k], preferred_element_type=F32)
            side[k, :, 0:W] = rows_f[0:W].astype(BF)
            side[k, :, W:] = rows_f[W:].astype(BF)
        for k in range(MODES):
            far[k] = jnp.dot(side[k], bwd[...], preferred_element_type=F32)

        def project(i, carry):
            rows = pl.ds(pl.multiple_of(i * CH, CH), CH)
            rows_im = pl.ds(pl.multiple_of(W + i * CH, CH), CH)
            f = [far[k, rows, :] for k in range(MODES)]
            total = f[0] * f[0] + f[1] * f[1]
            intensity = total[:, 0:W] + total[:, W:]
            factor = amp[p, 0, rows, :] * lax.rsqrt(jnp.maximum(intensity, 0.0625))
            for k in range(MODES):
                stack[k, rows, :] = (f[k][:, 0:W] * factor).astype(BF)
                stack[k, rows_im, :] = (f[k][:, W:] * factor).astype(BF)
            return carry

        lax.fori_loop(0, W // CH, project, 0, unroll=True)
        for k in range(MODES):
            rows_b = jnp.dot(bwd[...], stack[k], preferred_element_type=F32)
            side[k, :, 0:W] = rows_b[0:W].astype(BF)
            side[k, :, W:] = rows_b[W:].astype(BF)
        for k in range(MODES):
            far[k] = jnp.dot(side[k], fwd[...], preferred_element_type=F32)

        def spread(i, carry):
            rows = pl.ds(pl.multiple_of(i * CH, CH), CH)
            wr = win[0, rows, :]
            wi = win[1, rows, :]
            both = power[rows, :]
            tr = jnp.zeros((CH, W), F32)
            ti = jnp.zeros((CH, W), F32)
            for k in range(MODES):
                pr = probe[k, 0, rows, :]
                pi = probe[k, 1, rows, :]
                br = far[k, rows, 0:W]
                bi = far[k, rows, W:]
                tr += pr * br + pi * bi
                ti += pr * bi - pi * br
                grads[2 * k, rows, :] += wr * br + wi * bi
                grads[2 * k + 1, rows, :] += wr * bi - wi * br
            dst = pl.ds(r + i * CH, CH)
            for d, t in ((0, tr - both * wr), (1, ti - both * wi)):
                a = pltpu.roll(t[:, 0:HALF], s, 1)
                b = pltpu.roll(t[:, HALF:], s, 1)
                low = lanes < s
                acc[d, q, dst, :] += jnp.where(low, 0.0, a)
                acc[d, q + 1, dst, :] += jnp.where(low, a, b)
                acc[d, q2, dst, :] += jnp.where(low, b, 0.0)
            return carry

        lax.fori_loop(0, W // CH, spread, 0, unroll=True)
        return carry

    lax.fori_loop(0, POS, position, 0)
    for d in range(2):
        for i in range(2 * W // HALF):
            rows = pl.ds(i * HALF, HALF)
            out_left[d, rows, :] = acc[d, 0, rows, :] * scale
            out_right[d, rows, :] = acc[d, 3, rows, :] * scale
            for q in range(2):
                cols = pl.ds(q * HALF, HALF)
                step = acc[d, q + 1, rows, :] * scale
                if 1 <= i <= 2:
                    step += tile[d, pl.ds((i - 1) * HALF, HALF), cols]
                out_mid[d, rows, cols] = step
    h = half[0]
    for out, side_of in ((mine, h), (other, 1 - h)):

        def flush(i, carry):
            rows = pl.ds(pl.multiple_of(side_of * HALF + i * 8, 8), 8)
            for n in range(2 * MODES):
                out[i, n] = grads[n, rows, :]
            out[i, 2 * MODES] = weight[rows, :]
            return carry

        lax.fori_loop(0, 16, flush, 0)


def correct(offsets, half, border, probe, amplitude):
    fwd, bwd = dft_matrices()
    vmem = pl.BlockSpec(memory_space=pltpu.VMEM)
    smem = pl.BlockSpec(memory_space=pltpu.SMEM)
    part = jax.ShapeDtypeStruct((16, 2 * MODES + 1, 8, W), F32)
    strip = jax.ShapeDtypeStruct((2, 2 * W, HALF), F32)
    return pl.pallas_call(
        kernel,
        out_shape=(part, part, strip, jax.ShapeDtypeStruct((2, 2 * W, W), F32), strip),
        in_specs=[smem, smem] + [vmem] * 9 + [pl.BlockSpec(memory_space=pl.ANY)] * 2,
        out_specs=(vmem,) * 5,
        scratch_shapes=[
            pltpu.VMEM((2, 4, 2 * W, HALF), F32),
            pltpu.VMEM((2, 4, 2 * W, HALF), F32),
            pltpu.VMEM((2, W, W), F32),
            pltpu.VMEM((MODES, 2 * W, W), BF),
            pltpu.VMEM((MODES, W, 2 * W), BF),
            pltpu.VMEM((MODES, W, 2 * W), F32),
            pltpu.VMEM((W, W), F32),
            pltpu.VMEM((2 * MODES, W, W), F32),
            pltpu.VMEM((W, W), F32),
            pltpu.VMEM((2 * W, 2 * W), BF),
            pltpu.VMEM((2 * W, 2 * W), BF),
            pltpu.SemaphoreType.DMA((2,)),
        ],
        compiler_params=pltpu.CompilerParams(vmem_limit_bytes=20 << 20),
    )(offsets, half, *border, probe, amplitude, jnp.asarray(fwd), jnp.asarray(bwd))


GX = ("z", "xl")
GY = ("xh", "y", "co")
UP = [(i, (i + 1) % 16) for i in range(16)]
DOWN = [(j, i) for i, j in UP]
SWAP = [(0, 1), (1, 0)]


def arrange_kernel(half, own, swapped, out):
    h = half[0]
    for source, side_of in ((own, h), (swapped, 1 - h)):
        for i in range(16):
            rows = pl.ds(pl.multiple_of(side_of * HALF + i * 8, 8), 8)
            for n in range(2 * MODES):
                out[n // 2, n % 2, rows, :] = source[i, n]


def arrange(half, own, swapped):
    vmem = pl.BlockSpec(memory_space=pltpu.VMEM)
    return pl.pallas_call(
        arrange_kernel,
        out_shape=jax.ShapeDtypeStruct((MODES, 2, W, W), F32),
        in_specs=[pl.BlockSpec(memory_space=pltpu.SMEM), vmem, vmem],
        out_specs=vmem,
        compiler_params=pltpu.CompilerParams(vmem_limit_bytes=4 << 20),
    )(half, own, swapped)


def body(object_field, probe_field, amplitude, offsets):
    group = ("xh", "xl", "y")
    co = lax.axis_index("co")
    half = co.reshape(1)
    block = (co * 16 + lax.axis_index(group)) * 8
    offs = offsets.transpose(1, 2, 0).reshape(2, POS)
    object_field, half, block = lax.optimization_barrier((object_field, half, block))
    first, last = slice(0, HALF), slice(HALF, W)
    top = lax.ppermute(object_field[:, last], GX, UP)
    bot = lax.ppermute(object_field[:, first], GX, DOWN)
    left = lax.ppermute(object_field[:, :, last], GY, UP)
    right = lax.ppermute(object_field[:, :, first], GY, DOWN)
    left_ends = lax.ppermute(jnp.stack([top[:, :, last], bot[:, :, last]]), GY, UP)
    right_ends = lax.ppermute(jnp.stack([top[:, :, first], bot[:, :, first]]), GY, DOWN)
    border = (object_field, top, bot, left, right, left_ends, right_ends)
    mine, other, out_left, out_mid, out_right = correct(offs, half, border, probe_field, amplitude)
    part = mine + lax.ppermute(other, "co", SWAP)
    from_right = lax.ppermute(out_left, GY, DOWN)
    from_left = lax.ppermute(out_right, GY, UP)
    pieces = lax.all_to_all(part, group, 0, 0, tiled=True)
    part = sum(pieces[i] for i in range(16))
    folded = out_mid + jnp.concatenate([from_left, from_right], 2)
    from_below = lax.ppermute(folded[:, :HALF], GX, DOWN)
    part, from_below = lax.optimization_barrier((part, from_below))
    from_above = lax.ppermute(folded[:, HALF + W :], GX, UP)
    peers = [lax.ppermute(part, "z", [(i, i ^ step) for i in range(8)]) for step in (2, 4, 6)]
    part = (part + peers[0]) + (peers[1] + peers[2])
    part = part + lax.ppermute(part, "z", [(i, i ^ 1) for i in range(8)])
    part, from_above = lax.optimization_barrier((part, from_above))
    planes = probe_field.reshape(2 * MODES, W, W)
    local = lax.dynamic_slice_in_dim(planes, block, 8, 1)
    weight = part[2 * MODES]
    local = local + (part[: 2 * MODES] - local * weight) / (weight + 1e-05)
    gathered = lax.all_to_all(jnp.broadcast_to(local[None], (16,) + local.shape), group, 0, 0, tiled=True)
    updated_object = folded[:, HALF : HALF + W] + jnp.concatenate([from_above, from_below], 1)
    updated_probe = arrange(half, gathered, lax.ppermute(gathered, "co", SWAP))
    return (updated_object, updated_probe)


def solution(mesh):
    fine = Mesh(mesh.devices.reshape(8, 2, 2, 4, 2), ("z", "xl", "xh", "y", "co"))
    in_specs = (P(None, GX, GY), P(), P(GX, GY, None, None), P(GX, GY, None))
    out_specs = (P(None, GX, GY), P())
    return jax.shard_map(body, mesh=fine, in_specs=in_specs, out_specs=out_specs, check_vma=False)
```

```python
import functools
import math

import jax
import jax.numpy as jnp
import ml_dtypes
import numpy as np
from jax import lax
from jax.experimental import pallas as pl
from jax.experimental.pallas import tpu as pltpu
from jax.sharding import Mesh
from jax.sharding import PartitionSpec as P

W = 256
HALF = 128
POS = 4
MODES = 2
CH = 32
BF = jnp.bfloat16
F32 = jnp.float32


def dft_matrices():
    k = np.arange(W)
    phase = (k[:, None] * k[None, :]) % W
    angle = phase.astype(np.float32) * np.float32(2.0 * math.pi / W)
    norm = np.float32(1.0 / math.sqrt(W))
    c = (np.cos(angle) * norm).astype(ml_dtypes.bfloat16)
    s = (np.sin(angle) * norm).astype(ml_dtypes.bfloat16)
    fwd = np.block([[c, s], [-s, c]])
    bwd = np.block([[c, -s], [s, c]])
    return fwd, bwd


def kernel(
    offs, half, tile, top, bot, left, right, left_ends, right_ends, probe, amp, fwd_hbm, bwd_hbm,
    mine, other, out_left, out_mid, out_right,
    ext, acc, win, stack, side, far, weight, grads, power, fwd, bwd, sems,
):
    copies = [
        pltpu.make_async_copy(fwd_hbm, fwd, sems.at[0]),
        pltpu.make_async_copy(bwd_hbm, bwd, sems.at[1]),
    ]
    for copy in copies:
        copy.start()
    lanes = lax.broadcasted_iota(jnp.int32, (CH, HALF), 1)
    for q in range(2):
        cols = pl.ds(q * HALF, HALF)
        ext[:, q + 1, 0:HALF, :] = top[:, :, cols]
        ext[:, q + 1, HALF : HALF + W, :] = tile[:, :, cols]
        ext[:, q + 1, HALF + W :, :] = bot[:, :, cols]
    for q, middle, ends in ((0, left, left_ends), (3, right, right_ends)):
        ext[:, q, 0:HALF, :] = ends[0]
        ext[:, q, HALF : HALF + W, :] = middle[...]
        ext[:, q, HALF + W :, :] = ends[1]
    acc[...] = jnp.zeros_like(acc)
    weight[...] = jnp.zeros_like(weight)
    grads[...] = jnp.zeros_like(grads)
    top_power = jnp.zeros((CH, W), F32)
    for i in range(W // CH):
        rows = pl.ds(i * CH, CH)
        total = jnp.zeros((CH, W), F32)
        for k in range(MODES):
            total += probe[k, 0, rows, :] * probe[k, 0, rows, :] + probe[k, 1, rows, :] * probe[k, 1, rows, :]
        power[rows, :] = total
        top_power = jnp.maximum(top_power, total)
    scale = 1.0 / (jnp.max(top_power, axis=(0, 1), keepdims=True) + 1e-06)
    for copy in copies:
        copy.wait()

    def position(p, carry):
        r = offs[0, p] + HALF
        c = offs[1, p] + HALF
        q = c // HALF
        s = c - q * HALF
        back_shift = lax.rem(HALF - s, HALF)
        keep = lanes < HALF - s
        q2 = jnp.minimum(q + 2, 3)

        def cut(i, carry):
            rows = pl.ds(pl.multiple_of(i * CH, CH), CH)
            w = []
            for d in range(2):
                src = pl.ds(r + i * CH, CH)
                a = pltpu.roll(ext[d, q, src, :], back_shift, 1)
                b = pltpu.roll(ext[d, q + 1, src, :], back_shift, 1)
                e = pltpu.roll(ext[d, q2, src, :], back_shift, 1)
                w.append(jnp.concatenate([jnp.where(keep, a, b), jnp.where(keep, b, e)], 1))
                win[d, rows, :] = w[d]
            weight[rows, :] += w[0] * w[0] + w[1] * w[1]
            for k in range(MODES):
                pr = probe[k, 0, rows, :]
                pi = probe[k, 1, rows, :]
                stack[k, rows, :] = (pr * w[0] - pi * w[1]).astype(BF)
                stack[k, pl.ds(pl.multiple_of(W + i * CH, CH), CH), :] = (pr * w[1] + pi * w[0]).astype(BF)
            return carry

        lax.fori_loop(0, W // CH, cut, 0, unroll=True)
        for k in range(MODES):
            rows_f = jnp.dot(fwd[...], stack[k], preferred_element_type=F32)
            side[k, :, 0:W] = rows_f[0:W].astype(BF)
            side[k, :, W:] = rows_f[W:].astype(BF)
        for k in range(MODES):
            far[k] = jnp.dot(side[k], bwd[...], preferred_element_type=F32)

        def project(i, carry):
            rows = pl.ds(pl.multiple_of(i * CH, CH), CH)
            rows_im = pl.ds(pl.multiple_of(W + i * CH, CH), CH)
            f = [far[k, rows, :] for k in range(MODES)]
            total = f[0] * f[0] + f[1] * f[1]
            intensity = total[:, 0:W] + total[:, W:]
            factor = amp[p, 0, rows, :] * lax.rsqrt(jnp.maximum(intensity, 0.0625))
            for k in range(MODES):
                stack[k, rows, :] = (f[k][:, 0:W] * factor).astype(BF)
                stack[k, rows_im, :] = (f[k][:, W:] * factor).astype(BF)
            return carry

        lax.fori_loop(0, W // CH, project, 0, unroll=True)
        for k in range(MODES):
            rows_b = jnp.dot(bwd[...], stack[k], preferred_element_type=F32)
            side[k, :, 0:W] = rows_b[0:W].astype(BF)
            side[k, :, W:] = rows_b[W:].astype(BF)
        for k in range(MODES):
            far[k] = jnp.dot(side[k], fwd[...], preferred_element_type=F32)

        def spread(i, carry):
            rows = pl.ds(pl.multiple_of(i * CH, CH), CH)
            wr = win[0, rows, :]
            wi = win[1, rows, :]
            both = power[rows, :]
            tr = jnp.zeros((CH, W), F32)
            ti = jnp.zeros((CH, W), F32)
            for k in range(MODES):
                pr = probe[k, 0, rows, :]
                pi = probe[k, 1, rows, :]
                br = far[k, rows, 0:W]
                bi = far[k, rows, W:]
                tr += pr * br + pi * bi
                ti += pr * bi - pi * br
                grads[2 * k, rows, :] += wr * br + wi * bi
                grads[2 * k + 1, rows, :] += wr * bi - wi * br
            dst = pl.ds(r + i * CH, CH)
            for d, t in ((0, tr - both * wr), (1, ti - both * wi)):
                a = pltpu.roll(t[:, 0:HALF], s, 1)
                b = pltpu.roll(t[:, HALF:], s, 1)
                low = lanes < s
                acc[d, q, dst, :] += jnp.where(low, 0.0, a)
                acc[d, q + 1, dst, :] += jnp.where(low, a, b)
                acc[d, q2, dst, :] += jnp.where(low, b, 0.0)
            return carry

        lax.fori_loop(0, W // CH, spread, 0, unroll=True)
        return carry

    lax.fori_loop(0, POS, position, 0, unroll=True)
    for d in range(2):
        for i in range(2 * W // HALF):
            rows = pl.ds(i * HALF, HALF)
            out_left[d, rows, :] = acc[d, 0, rows, :] * scale
            out_right[d, rows, :] = acc[d, 3, rows, :] * scale
            for q in range(2):
                cols = pl.ds(q * HALF, HALF)
                step = acc[d, q + 1, rows, :] * scale
                if 1 <= i <= 2:
                    step += tile[d, pl.ds((i - 1) * HALF, HALF), cols]
                out_mid[d, rows, cols] = step
    h = half[0]
    for out, side_of in ((mine, h), (other, 1 - h)):

        def flush(i, carry):
            rows = pl.ds(pl.multiple_of(side_of * HALF + i * 8, 8), 8)
            for n in range(2 * MODES):
                out[i, n] = grads[n, rows, :]
            out[i, 2 * MODES] = weight[rows, :]
            return carry

        lax.fori_loop(0, 16, flush, 0)


def correct(offsets, half, border, probe, amplitude):
    fwd, bwd = dft_matrices()
    vmem = pl.BlockSpec(memory_space=pltpu.VMEM)
    smem = pl.BlockSpec(memory_space=pltpu.SMEM)
    part = jax.ShapeDtypeStruct((16, 2 * MODES + 1, 8, W), F32)
    strip = jax.ShapeDtypeStruct((2, 2 * W, HALF), F32)
    return pl.pallas_call(
        kernel,
        out_shape=(part, part, strip, jax.ShapeDtypeStruct((2, 2 * W, W), F32), strip),
        in_specs=[smem, smem] + [vmem] * 9 + [pl.BlockSpec(memory_space=pl.ANY)] * 2,
        out_specs=(vmem,) * 5,
        scratch_shapes=[
            pltpu.VMEM((2, 4, 2 * W, HALF), F32),
            pltpu.VMEM((2, 4, 2 * W, HALF), F32),
            pltpu.VMEM((2, W, W), F32),
            pltpu.VMEM((MODES, 2 * W, W), BF),
            pltpu.VMEM((MODES, W, 2 * W), BF),
            pltpu.VMEM((MODES, W, 2 * W), F32),
            pltpu.VMEM((W, W), F32),
            pltpu.VMEM((2 * MODES, W, W), F32),
            pltpu.VMEM((W, W), F32),
            pltpu.VMEM((2 * W, 2 * W), BF),
            pltpu.VMEM((2 * W, 2 * W), BF),
            pltpu.SemaphoreType.DMA((2,)),
        ],
        compiler_params=pltpu.CompilerParams(vmem_limit_bytes=20 << 20),
    )(offsets, half, *border, probe, amplitude, jnp.asarray(fwd), jnp.asarray(bwd))


GX = ("z", "xl")
GY = ("xh", "y", "co")
UP = [(i, (i + 1) % 16) for i in range(16)]
DOWN = [(j, i) for i, j in UP]
SWAP = [(0, 1), (1, 0)]


def arrange_kernel(half, own, swapped, out):
    h = half[0]
    for source, side_of in ((own, h), (swapped, 1 - h)):
        for i in range(16):
            rows = pl.ds(pl.multiple_of(side_of * HALF + i * 8, 8), 8)
            for n in range(2 * MODES):
                out[n // 2, n % 2, rows, :] = source[i, n]


def arrange(half, own, swapped):
    vmem = pl.BlockSpec(memory_space=pltpu.VMEM)
    return pl.pallas_call(
        arrange_kernel,
        out_shape=jax.ShapeDtypeStruct((MODES, 2, W, W), F32),
        in_specs=[pl.BlockSpec(memory_space=pltpu.SMEM), vmem, vmem],
        out_specs=vmem,
        compiler_params=pltpu.CompilerParams(vmem_limit_bytes=4 << 20),
    )(half, own, swapped)


def body(object_field, probe_field, amplitude, offsets):
    group = ("xh", "xl", "y")
    co = lax.axis_index("co")
    half = co.reshape(1)
    block = (co * 16 + lax.axis_index(group)) * 8
    offs = offsets.transpose(1, 2, 0).reshape(2, POS)
    object_field, half, block = lax.optimization_barrier((object_field, half, block))
    first, last = slice(0, HALF), slice(HALF, W)
    top = lax.ppermute(object_field[:, last], GX, UP)
    bot = lax.ppermute(object_field[:, first], GX, DOWN)
    left = lax.ppermute(object_field[:, :, last], GY, UP)
    right = lax.ppermute(object_field[:, :, first], GY, DOWN)
    left_ends = lax.ppermute(jnp.stack([top[:, :, last], bot[:, :, last]]), GY, UP)
    right_ends = lax.ppermute(jnp.stack([top[:, :, first], bot[:, :, first]]), GY, DOWN)
    border = (object_field, top, bot, left, right, left_ends, right_ends)
    mine, other, out_left, out_mid, out_right = correct(offs, half, border, probe_field, amplitude)
    part = mine + lax.ppermute(other, "co", SWAP)
    from_right = lax.ppermute(out_left, GY, DOWN)
    from_left = lax.ppermute(out_right, GY, UP)
    pieces = lax.all_to_all(part, group, 0, 0, tiled=True)
    part = sum(pieces[i] for i in range(16))
    folded = out_mid + jnp.concatenate([from_left, from_right], 2)
    part, folded = lax.optimization_barrier((part, folded))
    from_below = lax.ppermute(folded[:, :HALF], GX, DOWN)
    from_above = lax.ppermute(folded[:, HALF + W :], GX, UP)
    peers = [lax.ppermute(part, "z", [(i, i ^ step) for i in range(8)]) for step in (2, 4, 6)]
    part = (part + peers[0]) + (peers[1] + peers[2])
    part = part + lax.ppermute(part, "z", [(i, i ^ 1) for i in range(8)])
    part, from_below, from_above = lax.optimization_barrier((part, from_below, from_above))
    planes = probe_field.reshape(2 * MODES, W, W)
    local = lax.dynamic_slice_in_dim(planes, block, 8, 1)
    weight = part[2 * MODES]
    local = local + (part[: 2 * MODES] - local * weight) / (weight + 1e-05)
    gathered = lax.all_to_all(jnp.broadcast_to(local[None], (16,) + local.shape), group, 0, 0, tiled=True)
    updated_object = folded[:, HALF : HALF + W] + jnp.concatenate([from_above, from_below], 1)
    updated_probe = arrange(half, gathered, lax.ppermute(gathered, "co", SWAP))
    return (updated_object, updated_probe)


def solution(mesh):
    fine = Mesh(mesh.devices.reshape(8, 2, 2, 4, 2), ("z", "xl", "xh", "y", "co"))
    in_specs = (P(None, GX, GY), P(), P(GX, GY, None, None), P(GX, GY, None))
    out_specs = (P(None, GX, GY), P())
    return jax.shard_map(body, mesh=fine, in_specs=in_specs, out_specs=out_specs, check_vma=False)
```

```python
import functools
import math

import jax
import jax.numpy as jnp
import ml_dtypes
import numpy as np
from jax import lax
from jax.experimental import pallas as pl
from jax.experimental.pallas import tpu as pltpu
from jax.sharding import Mesh
from jax.sharding import PartitionSpec as P

W = 256
HALF = 128
POS = 4
MODES = 2
CH = 32
BF = jnp.bfloat16
F32 = jnp.float32


def dft_matrices():
    k = np.arange(W)
    phase = (k[:, None] * k[None, :]) % W
    angle = phase.astype(np.float32) * np.float32(2.0 * math.pi / W)
    norm = np.float32(1.0 / math.sqrt(W))
    c = (np.cos(angle) * norm).astype(ml_dtypes.bfloat16)
    s = (np.sin(angle) * norm).astype(ml_dtypes.bfloat16)
    fwd = np.block([[c, s], [-s, c]])
    bwd = np.block([[c, -s], [s, c]])
    return fwd, bwd


SMEM = pl.BlockSpec(memory_space=pltpu.SMEM)
VMEM = pl.BlockSpec(memory_space=pltpu.VMEM)
HBM = pl.BlockSpec(memory_space=pltpu.HBM)


def spot(number, unit):
    return pl.ds(pl.multiple_of(number * unit, unit), HALF)


def kernel(
    offs, flags, rows_in, rows_out, cols_in, cols_out, ends_in, ends_out, tile, probe, amp, power, inverse, fwd, bwd,
    mine, other, back_in, back_out, out_mid,
    ext, acc, win, stack, side, far, weight, grads,
):
    co, xl = flags[0], flags[1]
    q_in, q_out = 3 * (1 - co), 3 * co
    at_in, at_out = spot(1 - xl, W + HALF), spot(xl, W + HALF)
    middle = pl.ds(HALF, W)
    lanes = lax.broadcasted_iota(jnp.int32, (CH, HALF), 1)
    for q in range(2):
        cols = pl.ds(q * HALF, HALF)
        ext[:, q + 1, middle, :] = tile[:, :, cols]
        ext[:, q + 1, at_in, :] = rows_in[:, :, cols]
        ext[:, q + 1, at_out, :] = rows_out[:, :, cols]
    for q, cols, ends in ((q_in, cols_in, ends_in), (q_out, cols_out, ends_out)):
        ext[:, q, middle, :] = cols[...]
        ext[:, q, at_in, :] = ends[0]
        ext[:, q, at_out, :] = ends[1]
    acc[...] = jnp.zeros_like(acc)
    weight[...] = jnp.zeros_like(weight)
    grads[...] = jnp.zeros_like(grads)
    scale = inverse[0:1, :]

    def position(p, carry):
        r = offs[0, p] + HALF
        c = offs[1, p] + HALF
        q = c // HALF
        s = c - q * HALF
        back_shift = lax.rem(HALF - s, HALF)
        keep = lanes < HALF - s
        q2 = jnp.minimum(q + 2, 3)

        def cut(i, carry):
            rows = pl.ds(pl.multiple_of(i * CH, CH), CH)
            w = []
            for d in range(2):
                src = pl.ds(r + i * CH, CH)
                a = pltpu.roll(ext[d, q, src, :], back_shift, 1)
                b = pltpu.roll(ext[d, q + 1, src, :], back_shift, 1)
                e = pltpu.roll(ext[d, q2, src, :], back_shift, 1)
                w.append(jnp.concatenate([jnp.where(keep, a, b), jnp.where(keep, b, e)], 1))
                win[d, rows, :] = w[d]
            weight[rows, :] += w[0] * w[0] + w[1] * w[1]
            for k in range(MODES):
                pr = probe[k, 0, rows, :]
                pi = probe[k, 1, rows, :]
                stack[k, rows, :] = (pr * w[0] - pi * w[1]).astype(BF)
                stack[k, pl.ds(pl.multiple_of(W + i * CH, CH), CH), :] = (pr * w[1] + pi * w[0]).astype(BF)
            return carry

        lax.fori_loop(0, W // CH, cut, 0, unroll=True)
        for k in range(MODES):
            rows_f = jnp.dot(fwd[...], stack[k], preferred_element_type=F32)
            side[k, :, 0:W] = rows_f[0:W].astype(BF)
            side[k, :, W:] = rows_f[W:].astype(BF)
        for k in range(MODES):
            far[k] = jnp.dot(side[k], bwd[...], preferred_element_type=F32)

        def project(i, carry):
            rows = pl.ds(pl.multiple_of(i * CH, CH), CH)
            rows_im = pl.ds(pl.multiple_of(W + i * CH, CH), CH)
            f = [far[k, rows, :] for k in range(MODES)]
            total = f[0] * f[0] + f[1] * f[1]
            intensity = total[:, 0:W] + total[:, W:]
            factor = amp[p, 0, rows, :] * lax.rsqrt(jnp.maximum(intensity, 0.0625))
            for k in range(MODES):
                stack[k, rows, :] = (f[k][:, 0:W] * factor).astype(BF)
                stack[k, rows_im, :] = (f[k][:, W:] * factor).astype(BF)
            return carry

        lax.fori_loop(0, W // CH, project, 0, unroll=True)
        for k in range(MODES):
            rows_b = jnp.dot(bwd[...], stack[k], preferred_element_type=F32)
            side[k, :, 0:W] = rows_b[0:W].astype(BF)
            side[k, :, W:] = rows_b[W:].astype(BF)
        for k in range(MODES):
            far[k] = jnp.dot(side[k], fwd[...], preferred_element_type=F32)

        def spread(i, carry):
            rows = pl.ds(pl.multiple_of(i * CH, CH), CH)
            wr = win[0, rows, :]
            wi = win[1, rows, :]
            both = power[rows, :]
            tr = jnp.zeros((CH, W), F32)
            ti = jnp.zeros((CH, W), F32)
            for k in range(MODES):
                pr = probe[k, 0, rows, :]
                pi = probe[k, 1, rows, :]
                br = far[k, rows, 0:W]
                bi = far[k, rows, W:]
                tr += pr * br + pi * bi
                ti += pr * bi - pi * br
                grads[2 * k, rows, :] += wr * br + wi * bi
                grads[2 * k + 1, rows, :] += wr * bi - wi * br
            dst = pl.ds(r + i * CH, CH)
            for d, t in ((0, tr - both * wr), (1, ti - both * wi)):
                a = pltpu.roll(t[:, 0:HALF], s, 1)
                b = pltpu.roll(t[:, HALF:], s, 1)
                low = lanes < s
                acc[d, q, dst, :] += jnp.where(low, 0.0, a)
                acc[d, q + 1, dst, :] += jnp.where(low, a, b)
                acc[d, q2, dst, :] += jnp.where(low, b, 0.0)
            return carry

        lax.fori_loop(0, W // CH, spread, 0, unroll=True)
        return carry

    lax.fori_loop(0, POS, position, 0, unroll=True)
    for d in range(2):
        for i in range(2 * W // HALF):
            rows = pl.ds(i * HALF, HALF)
            back_in[d, rows, :] = acc[d, q_in, rows, :] * scale
            back_out[d, rows, :] = acc[d, q_out, rows, :] * scale
            for q in range(2):
                cols = pl.ds(q * HALF, HALF)
                step = acc[d, q + 1, rows, :] * scale
                if 1 <= i <= 2:
                    step += tile[d, pl.ds((i - 1) * HALF, HALF), cols]
                out_mid[d, rows, cols] = step
    for out, side_of in ((mine, co), (other, 1 - co)):

        def flush(i, carry):
            rows = pl.ds(pl.multiple_of(side_of * HALF + i * 8, 8), 8)
            for n in range(2 * MODES):
                out[i, n] = grads[n, rows, :]
            out[i, 2 * MODES] = weight[rows, :]
            return carry

        lax.fori_loop(0, 16, flush, 0)


def correct(offsets, flags, border, staged):
    part = jax.ShapeDtypeStruct((16, 2 * MODES + 1, 8, W), F32)
    strip = jax.ShapeDtypeStruct((2, 2 * W, HALF), F32)
    return pl.pallas_call(
        kernel,
        out_shape=(part, part, strip, strip, jax.ShapeDtypeStruct((2, 2 * W, W), F32)),
        in_specs=[SMEM, SMEM] + [VMEM] * 13,
        out_specs=(VMEM,) * 5,
        scratch_shapes=[
            pltpu.VMEM((2, 4, 2 * W, HALF), F32),
            pltpu.VMEM((2, 4, 2 * W, HALF), F32),
            pltpu.VMEM((2, W, W), F32),
            pltpu.VMEM((MODES, 2 * W, W), BF),
            pltpu.VMEM((MODES, W, 2 * W), BF),
            pltpu.VMEM((MODES, W, 2 * W), F32),
            pltpu.VMEM((W, W), F32),
            pltpu.VMEM((2 * MODES, W, W), F32),
        ],
        compiler_params=pltpu.CompilerParams(vmem_limit_bytes=20 << 20),
    )(offsets, flags, *border, *staged)


GX = ("z", "xl")
GY = ("xh", "y", "co")
NEAR = [(0, 1), (1, 0)]
FAR = [(i, (i + 1) % 16 if i % 2 else (i - 1) % 16) for i in range(16)]


def small_call(body, shapes, in_specs, scratch=()):
    return pl.pallas_call(
        body,
        out_shape=tuple(jax.ShapeDtypeStruct(shape, dtype) for shape, dtype in shapes),
        in_specs=in_specs,
        out_specs=(VMEM,) * len(shapes),
        scratch_shapes=scratch,
        compiler_params=pltpu.CompilerParams(vmem_limit_bytes=6 << 20),
    )


def cut_borders(flags, tile):
    def run(flags, tile, rows_in, rows_out, cols_in, cols_out, sems):
        co, xl = flags[0], flags[1]
        copies = [
            pltpu.make_async_copy(tile.at[:, spot(1 - xl, HALF), :], rows_in, sems.at[0]),
            pltpu.make_async_copy(tile.at[:, spot(xl, HALF), :], rows_out, sems.at[1]),
            pltpu.make_async_copy(tile.at[:, :, spot(1 - co, HALF)], cols_in, sems.at[2]),
            pltpu.make_async_copy(tile.at[:, :, spot(co, HALF)], cols_out, sems.at[3]),
        ]
        for copy in copies:
            copy.start()
        for copy in copies:
            copy.wait()

    return small_call(
        run,
        [((2, HALF, W), F32)] * 2 + [((2, W, HALF), F32)] * 2,
        [SMEM, HBM],
        [pltpu.SemaphoreType.DMA((4,))],
    )(flags, tile)


def stage(offsets, tile, probe, amplitude, after):
    fwd, bwd = (jnp.asarray(matrix) for matrix in dft_matrices())
    arrays = (tile, probe, amplitude, fwd, bwd)

    def run(offs, tile, probe, amp, fwd, bwd, after, offs_s, tile_v, probe_v, amp_v, power, inverse, fwd_v, bwd_v, sems):
        pairs = ((probe, probe_v), (tile, tile_v), (fwd, fwd_v), (bwd, bwd_v), (amp, amp_v))
        copies = [pltpu.make_async_copy(a, b, sems.at[n]) for n, (a, b) in enumerate(pairs)]
        for copy in copies:
            copy.start()
        for i in range(2):
            for p in range(POS):
                offs_s[i, p] = offs[i, p]
        copies[0].wait()
        largest = jnp.zeros((CH, W), F32)
        for i in range(W // CH):
            rows = pl.ds(i * CH, CH)
            total = jnp.zeros((CH, W), F32)
            for k in range(MODES):
                total += probe_v[k, 0, rows, :] * probe_v[k, 0, rows, :] + probe_v[k, 1, rows, :] * probe_v[k, 1, rows, :]
            power[rows, :] = total
            largest = jnp.maximum(largest, total)
        scale = 1.0 / (jnp.max(largest, axis=(0, 1), keepdims=True) + 1e-06)
        inverse[...] = jnp.broadcast_to(scale, inverse.shape)
        for copy in copies[1:]:
            copy.wait()

    shapes = [(a.shape, a.dtype) for a in arrays[:3]] + [((W, W), F32), ((8, HALF), F32)]
    shapes += [(a.shape, a.dtype) for a in arrays[3:]]
    return pl.pallas_call(
        run,
        out_shape=[jax.ShapeDtypeStruct(offsets.shape, jnp.int32)] + [jax.ShapeDtypeStruct(*a) for a in shapes],
        in_specs=[SMEM] + [HBM] * 5 + [pl.BlockSpec(memory_space=pl.ANY)],
        out_specs=[SMEM] + [VMEM] * 7,
        scratch_shapes=[pltpu.SemaphoreType.DMA((5,))],
        compiler_params=pltpu.CompilerParams(vmem_limit_bytes=6 << 20),
    )(offsets, *arrays, after)


def cut_ends(flags, rows_in, rows_out):
    def run(flags, rows_in, rows_out, ends_in, ends_out):
        co = flags[0]
        for n, rows in enumerate((rows_in, rows_out)):
            ends_in[n] = rows[:, :, spot(1 - co, HALF)]
            ends_out[n] = rows[:, :, spot(co, HALF)]

    return small_call(run, [((2, 2, HALF, HALF), F32)] * 2, [SMEM, VMEM, VMEM])(flags, rows_in, rows_out)


def fold(flags, middle, from_in, from_out):
    def run(flags, middle, from_in, from_out, back_in, back_out, center):
        co, xl = flags[0], flags[1]
        for c in range(2):

            @pl.when(co == c)
            def _():
                for q, extra in ((1 - c, from_in), (c, from_out)):
                    cols = pl.ds(q * HALF, HALF)
                    for dst, at in ((back_in, spot(1 - xl, W + HALF)), (back_out, spot(xl, W + HALF)), (center, pl.ds(HALF, W))):
                        dst[:, :, cols] = middle[:, at, cols] + extra[:, at, :]

    return small_call(run, [((2, HALF, W), F32)] * 2 + [((2, W, W), F32)], [SMEM] + [VMEM] * 3)(flags, middle, from_in, from_out)


def finish(flags, center, from_in, from_out):
    def run(flags, center, from_in, from_out, out):
        xl = flags[1]
        for at, extra in ((spot(1 - xl, HALF), from_in), (spot(xl, HALF), from_out)):
            out[:, at, :] = center[:, at, :] + extra[...]

    return small_call(run, [((2, W, W), F32)], [SMEM] + [VMEM] * 3)(flags, center, from_in, from_out)[0]


def arrange(flags, own, swapped):
    def run(flags, own, swapped, out):
        co = flags[0]
        for source, side_of in ((own, co), (swapped, 1 - co)):
            for i in range(16):
                rows = pl.ds(pl.multiple_of(side_of * HALF + i * 8, 8), 8)
                for n in range(2 * MODES):
                    out[n // 2, n % 2, rows, :] = source[i, n]

    return small_call(run, [((MODES, 2, W, W), F32)], [SMEM, VMEM, VMEM])(flags, own, swapped)[0]


def body(object_field, probe_field, amplitude, offsets):
    group = ("xh", "xl", "y")
    co = lax.axis_index("co")
    flags = jnp.stack([co, lax.axis_index("xl")])
    block = (co * 16 + lax.axis_index(group)) * 8
    offs = offsets.transpose(1, 2, 0).reshape(2, POS)
    object_field, flags, block = lax.optimization_barrier((object_field, flags, block))
    rows_in, rows_out, cols_in, cols_out = cut_borders(flags, object_field)
    rows_out = lax.ppermute(rows_out, GX, FAR)
    rows_in = lax.ppermute(rows_in, "xl", NEAR)
    cols_out = lax.ppermute(cols_out, GY, FAR)
    cols_in = lax.ppermute(cols_in, "co", NEAR)
    ends_in, ends_out = cut_ends(flags, rows_in, rows_out)
    ends_out = lax.ppermute(ends_out, GY, FAR)
    ends_in = lax.ppermute(ends_in, "co", NEAR)
    offs, *staged = stage(offs, object_field, probe_field, amplitude, cols_in)
    border = (rows_in, rows_out, cols_in, cols_out, ends_in, ends_out)
    mine, other, back_in, back_out, middle = correct(offs, flags, border, staged)
    from_out = lax.ppermute(back_out, GY, FAR)
    from_in = lax.ppermute(back_in, "co", NEAR)
    part = mine + lax.ppermute(other, "co", NEAR)
    pieces = lax.all_to_all(part, group, 0, 0, tiled=True)
    part = sum(pieces[i] for i in range(16))
    back_in, back_out, center = fold(flags, middle, from_in, from_out)
    part, back_in, back_out = lax.optimization_barrier((part, back_in, back_out))
    from_out = lax.ppermute(back_out, GX, FAR)
    from_in = lax.ppermute(back_in, "xl", NEAR)
    peers = [lax.ppermute(part, "z", [(i, i ^ step) for i in range(8)]) for step in (2, 4, 6)]
    part = (part + peers[0]) + (peers[1] + peers[2])
    part = part + lax.ppermute(part, "z", [(i, i ^ 1) for i in range(8)])
    part, from_in, from_out = lax.optimization_barrier((part, from_in, from_out))
    planes = probe_field.reshape(2 * MODES, W, W)
    local = lax.dynamic_slice_in_dim(planes, block, 8, 1)
    weight = part[2 * MODES]
    local = local + (part[: 2 * MODES] - local * weight) / (weight + 1e-05)
    gathered = lax.all_to_all(jnp.broadcast_to(local[None], (16,) + local.shape), group, 0, 0, tiled=True)
    updated_object = finish(flags, center, from_in, from_out)
    updated_probe = arrange(flags, gathered, lax.ppermute(gathered, "co", NEAR))
    return (updated_object, updated_probe)


def solution(mesh):
    fine = Mesh(mesh.devices.reshape(8, 2, 2, 4, 2), ("z", "xl", "xh", "y", "co"))
    in_specs = (P(None, GX, GY), P(), P(GX, GY, None, None), P(GX, GY, None))
    out_specs = (P(None, GX, GY), P())
    return jax.shard_map(body, mesh=fine, in_specs=in_specs, out_specs=out_specs, check_vma=False)
```

```python
import functools
import math

import jax
import jax.numpy as jnp
import ml_dtypes
import numpy as np
from jax import lax
from jax.experimental import pallas as pl
from jax.experimental.pallas import tpu as pltpu
from jax.sharding import Mesh
from jax.sharding import PartitionSpec as P

W = 256
HALF = 128
POS = 4
MODES = 2
CH = 32
FOLD_FLOPS = 4_000_000_000
BF = jnp.bfloat16
F32 = jnp.float32


def dft_matrices():
    k = np.arange(W)
    phase = (k[:, None] * k[None, :]) % W
    angle = phase.astype(np.float32) * np.float32(2.0 * math.pi / W)
    norm = np.float32(1.0 / math.sqrt(W))
    c = (np.cos(angle) * norm).astype(ml_dtypes.bfloat16)
    s = (np.sin(angle) * norm).astype(ml_dtypes.bfloat16)
    fwd = np.block([[c, s], [-s, c]])
    bwd = np.block([[c, -s], [s, c]])
    return fwd, bwd


SMEM = pl.BlockSpec(memory_space=pltpu.SMEM)
VMEM = pl.BlockSpec(memory_space=pltpu.VMEM)
HBM = pl.BlockSpec(memory_space=pltpu.HBM)


def spot(number, unit):
    return pl.ds(pl.multiple_of(number * unit, unit), HALF)


def kernel(
    offs, flags, rows_in, rows_out, cols_in, cols_out, ends_in, ends_out, tile, probe, amp, power, inverse, fwd, bwd,
    mine, other, back_in, back_out, out_mid,
    ext, acc, win, stack, side, far, weight, grads,
):
    co, xl = flags[0], flags[1]
    q_in, q_out = 3 * (1 - co), 3 * co
    at_in, at_out = spot(1 - xl, W + HALF), spot(xl, W + HALF)
    middle = pl.ds(HALF, W)
    lanes = lax.broadcasted_iota(jnp.int32, (CH, HALF), 1)
    for q in range(2):
        cols = pl.ds(q * HALF, HALF)
        ext[:, q + 1, middle, :] = tile[:, :, cols]
        ext[:, q + 1, at_in, :] = rows_in[:, :, cols]
        ext[:, q + 1, at_out, :] = rows_out[:, :, cols]
    for q, cols, ends in ((q_in, cols_in, ends_in), (q_out, cols_out, ends_out)):
        ext[:, q, middle, :] = cols[...]
        ext[:, q, at_in, :] = ends[0]
        ext[:, q, at_out, :] = ends[1]
    acc[...] = jnp.zeros_like(acc)
    weight[...] = jnp.zeros_like(weight)
    grads[...] = jnp.zeros_like(grads)
    scale = inverse[0:1, :]

    def position(p, carry):
        r = offs[0, p] + HALF
        c = offs[1, p] + HALF
        q = c // HALF
        s = c - q * HALF
        back_shift = lax.rem(HALF - s, HALF)
        keep = lanes < HALF - s
        q2 = jnp.minimum(q + 2, 3)

        def cut(i, carry):
            rows = pl.ds(pl.multiple_of(i * CH, CH), CH)
            w = []
            for d in range(2):
                src = pl.ds(r + i * CH, CH)
                a = pltpu.roll(ext[d, q, src, :], back_shift, 1)
                b = pltpu.roll(ext[d, q + 1, src, :], back_shift, 1)
                e = pltpu.roll(ext[d, q2, src, :], back_shift, 1)
                w.append(jnp.concatenate([jnp.where(keep, a, b), jnp.where(keep, b, e)], 1))
                win[d, rows, :] = w[d]
            weight[rows, :] += w[0] * w[0] + w[1] * w[1]
            for k in range(MODES):
                pr = probe[k, 0, rows, :]
                pi = probe[k, 1, rows, :]
                stack[k, rows, :] = (pr * w[0] - pi * w[1]).astype(BF)
                stack[k, pl.ds(pl.multiple_of(W + i * CH, CH), CH), :] = (pr * w[1] + pi * w[0]).astype(BF)
            return carry

        lax.fori_loop(0, W // CH, cut, 0, unroll=True)
        for k in range(MODES):
            rows_f = jnp.dot(fwd[...], stack[k], preferred_element_type=F32)
            side[k, :, 0:W] = rows_f[0:W].astype(BF)
            side[k, :, W:] = rows_f[W:].astype(BF)
        for k in range(MODES):
            far[k] = jnp.dot(side[k], bwd[...], preferred_element_type=F32)

        def project(i, carry):
            rows = pl.ds(pl.multiple_of(i * CH, CH), CH)
            rows_im = pl.ds(pl.multiple_of(W + i * CH, CH), CH)
            f = [far[k, rows, :] for k in range(MODES)]
            total = f[0] * f[0] + f[1] * f[1]
            intensity = total[:, 0:W] + total[:, W:]
            factor = amp[p, 0, rows, :] * lax.rsqrt(jnp.maximum(intensity, 0.0625))
            for k in range(MODES):
                stack[k, rows, :] = (f[k][:, 0:W] * factor).astype(BF)
                stack[k, rows_im, :] = (f[k][:, W:] * factor).astype(BF)
            return carry

        lax.fori_loop(0, W // CH, project, 0, unroll=True)
        for k in range(MODES):
            rows_b = jnp.dot(bwd[...], stack[k], preferred_element_type=F32)
            side[k, :, 0:W] = rows_b[0:W].astype(BF)
            side[k, :, W:] = rows_b[W:].astype(BF)
        for k in range(MODES):
            far[k] = jnp.dot(side[k], fwd[...], preferred_element_type=F32)

        def spread(i, carry):
            rows = pl.ds(pl.multiple_of(i * CH, CH), CH)
            wr = win[0, rows, :]
            wi = win[1, rows, :]
            both = power[rows, :]
            tr = jnp.zeros((CH, W), F32)
            ti = jnp.zeros((CH, W), F32)
            for k in range(MODES):
                pr = probe[k, 0, rows, :]
                pi = probe[k, 1, rows, :]
                br = far[k, rows, 0:W]
                bi = far[k, rows, W:]
                tr += pr * br + pi * bi
                ti += pr * bi - pi * br
                grads[2 * k, rows, :] += wr * br + wi * bi
                grads[2 * k + 1, rows, :] += wr * bi - wi * br
            dst = pl.ds(r + i * CH, CH)
            for d, t in ((0, tr - both * wr), (1, ti - both * wi)):
                a = pltpu.roll(t[:, 0:HALF], s, 1)
                b = pltpu.roll(t[:, HALF:], s, 1)
                low = lanes < s
                acc[d, q, dst, :] += jnp.where(low, 0.0, a)
                acc[d, q + 1, dst, :] += jnp.where(low, a, b)
                acc[d, q2, dst, :] += jnp.where(low, b, 0.0)
            return carry

        lax.fori_loop(0, W // CH, spread, 0, unroll=True)
        return carry

    lax.fori_loop(0, POS, position, 0, unroll=True)
    for d in range(2):
        for i in range(2 * W // HALF):
            rows = pl.ds(i * HALF, HALF)
            back_in[d, rows, :] = acc[d, q_in, rows, :] * scale
            back_out[d, rows, :] = acc[d, q_out, rows, :] * scale
            for q in range(2):
                cols = pl.ds(q * HALF, HALF)
                step = acc[d, q + 1, rows, :] * scale
                if 1 <= i <= 2:
                    step += tile[d, pl.ds((i - 1) * HALF, HALF), cols]
                out_mid[d, rows, cols] = step
    for out, side_of in ((mine, co), (other, 1 - co)):

        def flush(i, carry):
            rows = pl.ds(pl.multiple_of(side_of * HALF + i * 8, 8), 8)
            for n in range(2 * MODES):
                out[i, n] = grads[n, rows, :]
            out[i, 2 * MODES] = weight[rows, :]
            return carry

        lax.fori_loop(0, 16, flush, 0)


def correct(offsets, flags, border, staged):
    part = jax.ShapeDtypeStruct((16, 2 * MODES + 1, 8, W), F32)
    strip = jax.ShapeDtypeStruct((2, 2 * W, HALF), F32)
    return pl.pallas_call(
        kernel,
        out_shape=(part, part, strip, strip, jax.ShapeDtypeStruct((2, 2 * W, W), F32)),
        in_specs=[SMEM, SMEM] + [VMEM] * 13,
        out_specs=(VMEM,) * 5,
        scratch_shapes=[
            pltpu.VMEM((2, 4, 2 * W, HALF), F32),
            pltpu.VMEM((2, 4, 2 * W, HALF), F32),
            pltpu.VMEM((2, W, W), F32),
            pltpu.VMEM((MODES, 2 * W, W), BF),
            pltpu.VMEM((MODES, W, 2 * W), BF),
            pltpu.VMEM((MODES, W, 2 * W), F32),
            pltpu.VMEM((W, W), F32),
            pltpu.VMEM((2 * MODES, W, W), F32),
        ],
        cost_estimate=cost([((8 << 20,), jnp.int8)], 4 * MODES * POS * 2 * (2 * W) ** 2 * W),
        compiler_params=pltpu.CompilerParams(vmem_limit_bytes=20 << 20),
    )(offsets, flags, *border, *staged)


GX = ("z", "xl")
GY = ("xh", "y", "co")
NEAR = [(0, 1), (1, 0)]
FAR = [(i, (i + 1) % 16 if i % 2 else (i - 1) % 16) for i in range(16)]


def cost(shapes, flops=0):
    size = sum(2 * math.prod(shape) * jnp.dtype(dtype).itemsize for shape, dtype in shapes)
    return pl.CostEstimate(flops=flops, bytes_accessed=size, transcendentals=0)


def small_call(body, shapes, in_specs, scratch=(), limit=6 << 20, flops=0):
    return pl.pallas_call(
        body,
        out_shape=tuple(jax.ShapeDtypeStruct(shape, dtype) for shape, dtype in shapes),
        in_specs=in_specs,
        out_specs=(VMEM,) * len(shapes),
        scratch_shapes=scratch,
        cost_estimate=cost(shapes, flops),
        compiler_params=pltpu.CompilerParams(vmem_limit_bytes=limit),
    )


def cut_borders(flags, tile):
    def run(flags, tile, rows_in, rows_out, cols_in, cols_out, sems):
        co, xl = flags[0], flags[1]
        copies = [
            pltpu.make_async_copy(tile.at[:, spot(1 - xl, HALF), :], rows_in, sems.at[0]),
            pltpu.make_async_copy(tile.at[:, spot(xl, HALF), :], rows_out, sems.at[1]),
            pltpu.make_async_copy(tile.at[:, :, spot(1 - co, HALF)], cols_in, sems.at[2]),
            pltpu.make_async_copy(tile.at[:, :, spot(co, HALF)], cols_out, sems.at[3]),
        ]
        for copy in copies:
            copy.start()
        for copy in copies:
            copy.wait()

    return small_call(
        run,
        [((2, HALF, W), F32)] * 2 + [((2, W, HALF), F32)] * 2,
        [SMEM, HBM],
        [pltpu.SemaphoreType.DMA((4,))],
        125 << 19,
    )(flags, tile)


def stage(offsets, flags, tile, probe, amplitude):
    fwd, bwd = (jnp.asarray(matrix) for matrix in dft_matrices())
    arrays = (tile, probe, amplitude, fwd, bwd)

    def run(offs, flags, tile, probe, amp, fwd, bwd, offs_s, own, tile_v, probe_v, amp_v, power, inverse, fwd_v, bwd_v, sems):
        pairs = ((probe, probe_v), (tile, tile_v), (fwd, fwd_v), (bwd, bwd_v), (amp, amp_v))
        copies = [pltpu.make_async_copy(a, b, sems.at[n]) for n, (a, b) in enumerate(pairs)]
        for copy in copies:
            copy.start()
        for i in range(2):
            for p in range(POS):
                offs_s[i, p] = offs[i, p]
        copies[0].wait()
        largest = jnp.zeros((CH, W), F32)
        for i in range(W // CH):
            rows = pl.ds(i * CH, CH)
            total = jnp.zeros((CH, W), F32)
            for k in range(MODES):
                total += probe_v[k, 0, rows, :] * probe_v[k, 0, rows, :] + probe_v[k, 1, rows, :] * probe_v[k, 1, rows, :]
            power[rows, :] = total
            largest = jnp.maximum(largest, total)
        for n in range(2 * MODES):
            own[n] = probe_v[n // 2, n % 2, pl.ds(pl.multiple_of(flags[2], 8), 8), :]
        scale = 1.0 / (jnp.max(largest, axis=(0, 1), keepdims=True) + 1e-06)
        inverse[...] = jnp.broadcast_to(scale, inverse.shape)
        for copy in copies[1:]:
            copy.wait()

    shapes = [((2 * MODES, 8, W), F32)] + [(a.shape, a.dtype) for a in arrays[:3]] + [((W, W), F32), ((8, HALF), F32)]
    shapes += [(a.shape, a.dtype) for a in arrays[3:]]
    return pl.pallas_call(
        run,
        out_shape=[jax.ShapeDtypeStruct(offsets.shape, jnp.int32)] + [jax.ShapeDtypeStruct(*a) for a in shapes],
        in_specs=[SMEM, SMEM] + [HBM] * 5,
        out_specs=[SMEM] + [VMEM] * 8,
        scratch_shapes=[pltpu.SemaphoreType.DMA((5,))],
        cost_estimate=cost(shapes),
        compiler_params=pltpu.CompilerParams(vmem_limit_bytes=6 << 20),
    )(offsets, flags, *arrays)


def cut_ends(flags, rows_in, rows_out):
    def run(flags, rows_in, rows_out, ends_in, ends_out):
        co = flags[0]
        for n, rows in enumerate((rows_in, rows_out)):
            ends_in[n] = rows[:, :, spot(1 - co, HALF)]
            ends_out[n] = rows[:, :, spot(co, HALF)]

    return small_call(run, [((2, 2, HALF, HALF), F32)] * 2, [SMEM, VMEM, VMEM])(flags, rows_in, rows_out)


def fold(flags, middle, from_in, from_out):
    def run(flags, middle, from_in, from_out, back_in, back_out, center):
        co, xl = flags[0], flags[1]
        for c in range(2):

            @pl.when(co == c)
            def _():
                for q, extra in ((1 - c, from_in), (c, from_out)):
                    cols = pl.ds(q * HALF, HALF)
                    for dst, at in ((back_in, spot(1 - xl, W + HALF)), (back_out, spot(xl, W + HALF)), (center, pl.ds(HALF, W))):
                        dst[:, :, cols] = middle[:, at, cols] + extra[:, at, :]

    shapes = [((2, HALF, W), F32)] * 2 + [((2, W, W), F32)]
    return small_call(run, shapes, [SMEM] + [VMEM] * 3, flops=FOLD_FLOPS)(flags, middle, from_in, from_out)


def finish(flags, center, from_in, from_out):
    def run(flags, center, from_in, from_out, out):
        xl = flags[1]
        for at, extra in ((spot(1 - xl, HALF), from_in), (spot(xl, HALF), from_out)):
            out[:, at, :] = center[:, at, :] + extra[...]

    return small_call(run, [((2, W, W), F32)], [SMEM] + [VMEM] * 3)(flags, center, from_in, from_out)[0]


def arrange(flags, own, swapped):
    def run(flags, own, swapped, out):
        co = flags[0]
        for source, side_of in ((own, co), (swapped, 1 - co)):
            for i in range(16):
                rows = pl.ds(pl.multiple_of(side_of * HALF + i * 8, 8), 8)
                for n in range(2 * MODES):
                    out[n // 2, n % 2, rows, :] = source[i, n]

    return small_call(run, [((MODES, 2, W, W), F32)], [SMEM, VMEM, VMEM])(flags, own, swapped)[0]


def body(object_field, probe_field, amplitude, offsets):
    group = ("xh", "xl", "y")
    co = lax.axis_index("co")
    flags = jnp.stack([co, lax.axis_index("xl"), (co * 16 + lax.axis_index(group)) * 8])
    offs = offsets.transpose(1, 2, 0).reshape(2, POS)
    object_field, flags = lax.optimization_barrier((object_field, flags))
    rows_in, rows_out, cols_in, cols_out = cut_borders(flags, object_field)
    rows_out = lax.ppermute(rows_out, GX, FAR)
    rows_in = lax.ppermute(rows_in, "xl", NEAR)
    cols_out = lax.ppermute(cols_out, GY, FAR)
    cols_in = lax.ppermute(cols_in, "co", NEAR)
    staged = stage(offs, flags, object_field, probe_field, amplitude)
    rows_in, rows_out, staged = lax.optimization_barrier((rows_in, rows_out, staged))
    offs, local, *staged = staged
    ends_in, ends_out = cut_ends(flags, rows_in, rows_out)
    ends_out = lax.ppermute(ends_out, GY, FAR)
    ends_in = lax.ppermute(ends_in, "co", NEAR)
    border = (rows_in, rows_out, cols_in, cols_out, ends_in, ends_out)
    mine, other, back_in, back_out, middle = correct(offs, flags, border, staged)
    from_out = lax.ppermute(back_out, GY, FAR)
    from_in = lax.ppermute(back_in, "co", NEAR)
    part = mine + lax.ppermute(other, "co", NEAR)
    pieces = lax.all_to_all(part, group, 0, 0, tiled=True)
    part = sum(pieces[i] for i in range(16))
    back_in, back_out, center = fold(flags, middle, from_in, from_out)
    part, back_in, back_out = lax.optimization_barrier((part, back_in, back_out))
    from_out = lax.ppermute(back_out, GX, FAR)
    from_in = lax.ppermute(back_in, "xl", NEAR)
    peers = [lax.ppermute(part, "z", [(i, i ^ step) for i in range(8)]) for step in (2, 4, 6)]
    part = (part + peers[0]) + (peers[1] + peers[2])
    part = part + lax.ppermute(part, "z", [(i, i ^ 1) for i in range(8)])
    part, from_in, from_out = lax.optimization_barrier((part, from_in, from_out))
    weight = part[2 * MODES]
    local = local + (part[: 2 * MODES] - local * weight) / (weight + 1e-05)
    gathered = lax.all_to_all(jnp.broadcast_to(local[None], (16,) + local.shape), group, 0, 0, tiled=True)
    updated_object = finish(flags, center, from_in, from_out)
    updated_probe = arrange(flags, gathered, lax.ppermute(gathered, "co", NEAR))
    return (updated_object, updated_probe)


def solution(mesh):
    fine = Mesh(mesh.devices.reshape(8, 2, 2, 4, 2), ("z", "xl", "xh", "y", "co"))
    in_specs = (P(None, GX, GY), P(), P(GX, GY, None, None), P(GX, GY, None))
    out_specs = (P(None, GX, GY), P())
    return jax.shard_map(body, mesh=fine, in_specs=in_specs, out_specs=out_specs, check_vma=False)
```

```python
import functools
import math

import jax
import jax.numpy as jnp
import ml_dtypes
import numpy as np
from jax import lax
from jax.experimental import pallas as pl
from jax.experimental.pallas import tpu as pltpu
from jax.sharding import Mesh
from jax.sharding import PartitionSpec as P

W = 256
HALF = 128
POS = 4
MODES = 2
CH = 32
BF = jnp.bfloat16
F32 = jnp.float32


def dft_matrices():
    k = np.arange(W)
    phase = (k[:, None] * k[None, :]) % W
    angle = phase.astype(np.float32) * np.float32(2.0 * math.pi / W)
    norm = np.float32(1.0 / math.sqrt(W))
    c = (np.cos(angle) * norm).astype(ml_dtypes.bfloat16)
    s = (np.sin(angle) * norm).astype(ml_dtypes.bfloat16)
    fwd = np.block([[c, s], [-s, c]])
    bwd = np.block([[c, -s], [s, c]])
    return fwd, bwd


def spot(number, unit):
    return pl.ds(pl.multiple_of(number * unit, unit), HALF)


def kernel(
    offs, flags, tile, rows_in, rows_out, cols_in, cols_out, ends_in, ends_out, probe, amp, fwd_hbm, bwd_hbm,
    mine, other, back_in, back_out, out_mid,
    ext, acc, win, stack, side, far, weight, grads, power, fwd, bwd, sems,
):
    copies = [
        pltpu.make_async_copy(fwd_hbm, fwd, sems.at[0]),
        pltpu.make_async_copy(bwd_hbm, bwd, sems.at[1]),
    ]
    for copy in copies:
        copy.start()
    co, xl = flags[0], flags[1]
    q_in, q_out = 3 * (1 - co), 3 * co
    at_in, at_out = spot(1 - xl, W + HALF), spot(xl, W + HALF)
    middle = pl.ds(HALF, W)
    lanes = lax.broadcasted_iota(jnp.int32, (CH, HALF), 1)
    for q in range(2):
        cols = pl.ds(q * HALF, HALF)
        ext[:, q + 1, middle, :] = tile[:, :, cols]
        ext[:, q + 1, at_in, :] = rows_in[:, :, cols]
        ext[:, q + 1, at_out, :] = rows_out[:, :, cols]
    for q, cols, ends in ((q_in, cols_in, ends_in), (q_out, cols_out, ends_out)):
        ext[:, q, middle, :] = cols[...]
        ext[:, q, at_in, :] = ends[0]
        ext[:, q, at_out, :] = ends[1]
    acc[...] = jnp.zeros_like(acc)
    weight[...] = jnp.zeros_like(weight)
    grads[...] = jnp.zeros_like(grads)
    top_power = jnp.zeros((CH, W), F32)
    for i in range(W // CH):
        rows = pl.ds(i * CH, CH)
        total = jnp.zeros((CH, W), F32)
        for k in range(MODES):
            total += probe[k, 0, rows, :] * probe[k, 0, rows, :] + probe[k, 1, rows, :] * probe[k, 1, rows, :]
        power[rows, :] = total
        top_power = jnp.maximum(top_power, total)
    scale = 1.0 / (jnp.max(top_power, axis=(0, 1), keepdims=True) + 1e-06)
    for copy in copies:
        copy.wait()

    def position(p, carry):
        r = offs[0, p] + HALF
        c = offs[1, p] + HALF
        q = c // HALF
        s = c - q * HALF
        back_shift = lax.rem(HALF - s, HALF)
        keep = lanes < HALF - s
        q2 = jnp.minimum(q + 2, 3)

        def cut(i, carry):
            rows = pl.ds(pl.multiple_of(i * CH, CH), CH)
            w = []
            for d in range(2):
                src = pl.ds(r + i * CH, CH)
                a = pltpu.roll(ext[d, q, src, :], back_shift, 1)
                b = pltpu.roll(ext[d, q + 1, src, :], back_shift, 1)
                e = pltpu.roll(ext[d, q2, src, :], back_shift, 1)
                w.append(jnp.concatenate([jnp.where(keep, a, b), jnp.where(keep, b, e)], 1))
                win[d, rows, :] = w[d]
            weight[rows, :] += w[0] * w[0] + w[1] * w[1]
            for k in range(MODES):
                pr = probe[k, 0, rows, :]
                pi = probe[k, 1, rows, :]
                stack[k, rows, :] = (pr * w[0] - pi * w[1]).astype(BF)
                stack[k, pl.ds(pl.multiple_of(W + i * CH, CH), CH), :] = (pr * w[1] + pi * w[0]).astype(BF)
            return carry

        lax.fori_loop(0, W // CH, cut, 0, unroll=True)
        for k in range(MODES):
            rows_f = jnp.dot(fwd[...], stack[k], preferred_element_type=F32)
            side[k, :, 0:W] = rows_f[0:W].astype(BF)
            side[k, :, W:] = rows_f[W:].astype(BF)
        for k in range(MODES):
            far[k] = jnp.dot(side[k], bwd[...], preferred_element_type=F32)

        def project(i, carry):
            rows = pl.ds(pl.multiple_of(i * CH, CH), CH)
            rows_im = pl.ds(pl.multiple_of(W + i * CH, CH), CH)
            f = [far[k, rows, :] for k in range(MODES)]
            total = f[0] * f[0] + f[1] * f[1]
            intensity = total[:, 0:W] + total[:, W:]
            factor = amp[p, 0, rows, :] * lax.rsqrt(jnp.maximum(intensity, 0.0625))
            for k in range(MODES):
                stack[k, rows, :] = (f[k][:, 0:W] * factor).astype(BF)
                stack[k, rows_im, :] = (f[k][:, W:] * factor).astype(BF)
            return carry

        lax.fori_loop(0, W // CH, project, 0, unroll=True)
        for k in range(MODES):
            rows_b = jnp.dot(bwd[...], stack[k], preferred_element_type=F32)
            side[k, :, 0:W] = rows_b[0:W].astype(BF)
            side[k, :, W:] = rows_b[W:].astype(BF)
        for k in range(MODES):
            far[k] = jnp.dot(side[k], fwd[...], preferred_element_type=F32)

        def spread(i, carry):
            rows = pl.ds(pl.multiple_of(i * CH, CH), CH)
            wr = win[0, rows, :]
            wi = win[1, rows, :]
            both = power[rows, :]
            tr = jnp.zeros((CH, W), F32)
            ti = jnp.zeros((CH, W), F32)
            for k in range(MODES):
                pr = probe[k, 0, rows, :]
                pi = probe[k, 1, rows, :]
                br = far[k, rows, 0:W]
                bi = far[k, rows, W:]
                tr += pr * br + pi * bi
                ti += pr * bi - pi * br
                grads[2 * k, rows, :] += wr * br + wi * bi
                grads[2 * k + 1, rows, :] += wr * bi - wi * br
            dst = pl.ds(r + i * CH, CH)
            for d, t in ((0, tr - both * wr), (1, ti - both * wi)):
                a = pltpu.roll(t[:, 0:HALF], s, 1)
                b = pltpu.roll(t[:, HALF:], s, 1)
                low = lanes < s
                acc[d, q, dst, :] += jnp.where(low, 0.0, a)
                acc[d, q + 1, dst, :] += jnp.where(low, a, b)
                acc[d, q2, dst, :] += jnp.where(low, b, 0.0)
            return carry

        lax.fori_loop(0, W // CH, spread, 0, unroll=True)
        return carry

    lax.fori_loop(0, POS, position, 0, unroll=True)
    for d in range(2):
        for i in range(2 * W // HALF):
            rows = pl.ds(i * HALF, HALF)
            back_in[d, rows, :] = acc[d, q_in, rows, :] * scale
            back_out[d, rows, :] = acc[d, q_out, rows, :] * scale
            for q in range(2):
                cols = pl.ds(q * HALF, HALF)
                step = acc[d, q + 1, rows, :] * scale
                if 1 <= i <= 2:
                    step += tile[d, pl.ds((i - 1) * HALF, HALF), cols]
                out_mid[d, rows, cols] = step
    for out, side_of in ((mine, co), (other, 1 - co)):

        def flush(i, carry):
            rows = pl.ds(pl.multiple_of(side_of * HALF + i * 8, 8), 8)
            for n in range(2 * MODES):
                out[i, n] = grads[n, rows, :]
            out[i, 2 * MODES] = weight[rows, :]
            return carry

        lax.fori_loop(0, 16, flush, 0)


def correct(offsets, flags, border, probe, amplitude):
    fwd, bwd = dft_matrices()
    vmem = pl.BlockSpec(memory_space=pltpu.VMEM)
    smem = pl.BlockSpec(memory_space=pltpu.SMEM)
    part = jax.ShapeDtypeStruct((16, 2 * MODES + 1, 8, W), F32)
    strip = jax.ShapeDtypeStruct((2, 2 * W, HALF), F32)
    return pl.pallas_call(
        kernel,
        out_shape=(part, part, strip, strip, jax.ShapeDtypeStruct((2, 2 * W, W), F32)),
        in_specs=[smem, smem] + [vmem] * 9 + [pl.BlockSpec(memory_space=pl.ANY)] * 2,
        out_specs=(vmem,) * 5,
        scratch_shapes=[
            pltpu.VMEM((2, 4, 2 * W, HALF), F32),
            pltpu.VMEM((2, 4, 2 * W, HALF), F32),
            pltpu.VMEM((2, W, W), F32),
            pltpu.VMEM((MODES, 2 * W, W), BF),
            pltpu.VMEM((MODES, W, 2 * W), BF),
            pltpu.VMEM((MODES, W, 2 * W), F32),
            pltpu.VMEM((W, W), F32),
            pltpu.VMEM((2 * MODES, W, W), F32),
            pltpu.VMEM((W, W), F32),
            pltpu.VMEM((2 * W, 2 * W), BF),
            pltpu.VMEM((2 * W, 2 * W), BF),
            pltpu.SemaphoreType.DMA((2,)),
        ],
        compiler_params=pltpu.CompilerParams(vmem_limit_bytes=20 << 20),
    )(offsets, flags, *border, probe, amplitude, jnp.asarray(fwd), jnp.asarray(bwd))


GX = ("z", "xl")
GY = ("xh", "y", "co")
NEAR = [(0, 1), (1, 0)]
FAR = [(i, (i + 1) % 16 if i % 2 else (i - 1) % 16) for i in range(16)]


def arrange_kernel(half, own, swapped, out):
    h = half[0]
    for source, side_of in ((own, h), (swapped, 1 - h)):
        for i in range(16):
            rows = pl.ds(pl.multiple_of(side_of * HALF + i * 8, 8), 8)
            for n in range(2 * MODES):
                out[n // 2, n % 2, rows, :] = source[i, n]


def arrange(half, own, swapped):
    vmem = pl.BlockSpec(memory_space=pltpu.VMEM)
    return pl.pallas_call(
        arrange_kernel,
        out_shape=jax.ShapeDtypeStruct((MODES, 2, W, W), F32),
        in_specs=[pl.BlockSpec(memory_space=pltpu.SMEM), vmem, vmem],
        out_specs=vmem,
        compiler_params=pltpu.CompilerParams(vmem_limit_bytes=4 << 20),
    )(half, own, swapped)


def in_order(number, near, far, axis):
    first = number == 0
    return jnp.concatenate([jnp.where(first, far, near), jnp.where(first, near, far)], axis)


def body(object_field, probe_field, amplitude, offsets):
    group = ("xh", "xl", "y")
    co, xl = lax.axis_index("co"), lax.axis_index("xl")
    block = (co * 16 + lax.axis_index(group)) * 8
    offs = offsets.transpose(1, 2, 0).reshape(2, POS)
    half_in, half_out = (1 - co) * HALF, co * HALF
    rows_at_in, rows_at_out = (1 - xl) * HALF, xl * HALF
    scalars = (co, xl, block, half_in, half_out, rows_at_in, rows_at_out, 3 * rows_at_in, 3 * rows_at_out)
    flags = jnp.stack([co, xl])
    object_field, flags, *scalars = lax.optimization_barrier((object_field, flags, *scalars))
    co, xl, block, half_in, half_out, rows_at_in, rows_at_out, ends_at_in, ends_at_out = scalars
    cut = lax.dynamic_slice_in_dim
    rows_out = lax.ppermute(cut(object_field, rows_at_out, HALF, 1), GX, FAR)
    rows_in = lax.ppermute(cut(object_field, rows_at_in, HALF, 1), "xl", NEAR)
    cols_out = lax.ppermute(cut(object_field, half_out, HALF, 2), GY, FAR)
    cols_in = lax.ppermute(cut(object_field, half_in, HALF, 2), "co", NEAR)
    ends_out = lax.ppermute(jnp.stack([cut(rows, half_out, HALF, 2) for rows in (rows_in, rows_out)]), GY, FAR)
    ends_in = lax.ppermute(jnp.stack([cut(rows, half_in, HALF, 2) for rows in (rows_in, rows_out)]), "co", NEAR)
    border = (object_field, rows_in, rows_out, cols_in, cols_out, ends_in, ends_out)
    mine, other, back_in, back_out, middle = correct(offs, flags, border, probe_field, amplitude)
    from_out = lax.ppermute(back_out, GY, FAR)
    from_in = lax.ppermute(back_in, "co", NEAR)
    part = mine + lax.ppermute(other, "co", NEAR)
    pieces = lax.all_to_all(part, group, 0, 0, tiled=True)
    part = sum(pieces[i] for i in range(16))
    folded = middle + in_order(co, from_in, from_out, 2)
    part, folded = lax.optimization_barrier((part, folded))
    from_out = lax.ppermute(cut(folded, ends_at_out, HALF, 1), GX, FAR)
    from_in = lax.ppermute(cut(folded, ends_at_in, HALF, 1), "xl", NEAR)
    peers = [lax.ppermute(part, "z", [(i, i ^ step) for i in range(8)]) for step in (2, 4, 6)]
    part = (part + peers[0]) + (peers[1] + peers[2])
    part = part + lax.ppermute(part, "z", [(i, i ^ 1) for i in range(8)])
    part, from_in, from_out = lax.optimization_barrier((part, from_in, from_out))
    local = cut(probe_field.reshape(2 * MODES, W, W), block, 8, 1)
    weight = part[2 * MODES]
    local = local + (part[: 2 * MODES] - local * weight) / (weight + 1e-05)
    gathered = lax.all_to_all(jnp.broadcast_to(local[None], (16,) + local.shape), group, 0, 0, tiled=True)
    updated_object = folded[:, HALF : HALF + W] + in_order(xl, from_in, from_out, 1)
    updated_probe = arrange(flags, gathered, lax.ppermute(gathered, "co", NEAR))
    return (updated_object, updated_probe)


def solution(mesh):
    fine = Mesh(mesh.devices.reshape(8, 2, 2, 4, 2), ("z", "xl", "xh", "y", "co"))
    in_specs = (P(None, GX, GY), P(), P(GX, GY, None, None), P(GX, GY, None))
    out_specs = (P(None, GX, GY), P())
    return jax.shard_map(body, mesh=fine, in_specs=in_specs, out_specs=out_specs, check_vma=False)
```

```python
import functools
import math

import jax
import jax.numpy as jnp
import ml_dtypes
import numpy as np
from jax import lax
from jax.experimental import pallas as pl
from jax.experimental.pallas import tpu as pltpu
from jax.sharding import Mesh
from jax.sharding import PartitionSpec as P

W = 256
HALF = 128
POS = 4
MODES = 2
CH = 32
BF = jnp.bfloat16
F32 = jnp.float32


def dft_matrices():
    k = np.arange(W)
    phase = (k[:, None] * k[None, :]) % W
    angle = phase.astype(np.float32) * np.float32(2.0 * math.pi / W)
    norm = np.float32(1.0 / math.sqrt(W))
    c = (np.cos(angle) * norm).astype(ml_dtypes.bfloat16)
    s = (np.sin(angle) * norm).astype(ml_dtypes.bfloat16)
    fwd = np.block([[c, s], [-s, c]])
    bwd = np.block([[c, -s], [s, c]])
    return fwd, bwd


def spot(number, unit):
    return pl.ds(pl.multiple_of(number * unit, unit), HALF)


def kernel(
    offs, flags, tile, rows_in, rows_out, cols_in, cols_out, ends_in, ends_out, probe, amp, fwd_hbm, bwd_hbm,
    mine, other, out_left, out_right, out_mid,
    ext, acc, win, stack, side, far, weight, grads, power, fwd, bwd, sems,
):
    copies = [
        pltpu.make_async_copy(fwd_hbm, fwd, sems.at[0]),
        pltpu.make_async_copy(bwd_hbm, bwd, sems.at[1]),
    ]
    for copy in copies:
        copy.start()
    co, xl = flags[0], flags[1]
    q_in, q_out = 3 * (1 - co), 3 * co
    at_in, at_out = spot(1 - xl, W + HALF), spot(xl, W + HALF)
    middle = pl.ds(HALF, W)
    lanes = lax.broadcasted_iota(jnp.int32, (CH, HALF), 1)
    for q in range(2):
        cols = pl.ds(q * HALF, HALF)
        ext[:, q + 1, middle, :] = tile[:, :, cols]
        ext[:, q + 1, at_in, :] = rows_in[:, :, cols]
        ext[:, q + 1, at_out, :] = rows_out[:, :, cols]
    for q, cols, ends in ((q_in, cols_in, ends_in), (q_out, cols_out, ends_out)):
        ext[:, q, middle, :] = cols[...]
        ext[:, q, at_out, :] = ends[0]
        ext[:, q, at_in, :] = ends[1]
    acc[...] = jnp.zeros_like(acc)
    weight[...] = jnp.zeros_like(weight)
    grads[...] = jnp.zeros_like(grads)
    top_power = jnp.zeros((CH, W), F32)
    for i in range(W // CH):
        rows = pl.ds(i * CH, CH)
        total = jnp.zeros((CH, W), F32)
        for k in range(MODES):
            total += probe[k, 0, rows, :] * probe[k, 0, rows, :] + probe[k, 1, rows, :] * probe[k, 1, rows, :]
        power[rows, :] = total
        top_power = jnp.maximum(top_power, total)
    scale = 1.0 / (jnp.max(top_power, axis=(0, 1), keepdims=True) + 1e-06)
    for copy in copies:
        copy.wait()

    def position(p, carry):
        r = offs[0, p] + HALF
        c = offs[1, p] + HALF
        q = c // HALF
        s = c - q * HALF
        back_shift = lax.rem(HALF - s, HALF)
        keep = lanes < HALF - s
        q2 = jnp.minimum(q + 2, 3)

        def cut(i, carry):
            rows = pl.ds(pl.multiple_of(i * CH, CH), CH)
            w = []
            for d in range(2):
                src = pl.ds(r + i * CH, CH)
                a = pltpu.roll(ext[d, q, src, :], back_shift, 1)
                b = pltpu.roll(ext[d, q + 1, src, :], back_shift, 1)
                e = pltpu.roll(ext[d, q2, src, :], back_shift, 1)
                w.append(jnp.concatenate([jnp.where(keep, a, b), jnp.where(keep, b, e)], 1))
                win[d, rows, :] = w[d]
            weight[rows, :] += w[0] * w[0] + w[1] * w[1]
            for k in range(MODES):
                pr = probe[k, 0, rows, :]
                pi = probe[k, 1, rows, :]
                stack[k, rows, :] = (pr * w[0] - pi * w[1]).astype(BF)
                stack[k, pl.ds(pl.multiple_of(W + i * CH, CH), CH), :] = (pr * w[1] + pi * w[0]).astype(BF)
            return carry

        lax.fori_loop(0, W // CH, cut, 0, unroll=True)
        for k in range(MODES):
            rows_f = jnp.dot(fwd[...], stack[k], preferred_element_type=F32)
            side[k, :, 0:W] = rows_f[0:W].astype(BF)
            side[k, :, W:] = rows_f[W:].astype(BF)
        for k in range(MODES):
            far[k] = jnp.dot(side[k], bwd[...], preferred_element_type=F32)

        def project(i, carry):
            rows = pl.ds(pl.multiple_of(i * CH, CH), CH)
            rows_im = pl.ds(pl.multiple_of(W + i * CH, CH), CH)
            f = [far[k, rows, :] for k in range(MODES)]
            total = f[0] * f[0] + f[1] * f[1]
            intensity = total[:, 0:W] + total[:, W:]
            factor = amp[p, 0, rows, :] * lax.rsqrt(jnp.maximum(intensity, 0.0625))
            for k in range(MODES):
                stack[k, rows, :] = (f[k][:, 0:W] * factor).astype(BF)
                stack[k, rows_im, :] = (f[k][:, W:] * factor).astype(BF)
            return carry

        lax.fori_loop(0, W // CH, project, 0, unroll=True)
        for k in range(MODES):
            rows_b = jnp.dot(bwd[...], stack[k], preferred_element_type=F32)
            side[k, :, 0:W] = rows_b[0:W].astype(BF)
            side[k, :, W:] = rows_b[W:].astype(BF)
        for k in range(MODES):
            far[k] = jnp.dot(side[k], fwd[...], preferred_element_type=F32)

        def spread(i, carry):
            rows = pl.ds(pl.multiple_of(i * CH, CH), CH)
            wr = win[0, rows, :]
            wi = win[1, rows, :]
            both = power[rows, :]
            tr = jnp.zeros((CH, W), F32)
            ti = jnp.zeros((CH, W), F32)
            for k in range(MODES):
                pr = probe[k, 0, rows, :]
                pi = probe[k, 1, rows, :]
                br = far[k, rows, 0:W]
                bi = far[k, rows, W:]
                tr += pr * br + pi * bi
                ti += pr * bi - pi * br
                grads[2 * k, rows, :] += wr * br + wi * bi
                grads[2 * k + 1, rows, :] += wr * bi - wi * br
            dst = pl.ds(r + i * CH, CH)
            for d, t in ((0, tr - both * wr), (1, ti - both * wi)):
                a = pltpu.roll(t[:, 0:HALF], s, 1)
                b = pltpu.roll(t[:, HALF:], s, 1)
                low = lanes < s
                acc[d, q, dst, :] += jnp.where(low, 0.0, a)
                acc[d, q + 1, dst, :] += jnp.where(low, a, b)
                acc[d, q2, dst, :] += jnp.where(low, b, 0.0)
            return carry

        lax.fori_loop(0, W // CH, spread, 0, unroll=True)
        return carry

    lax.fori_loop(0, POS, position, 0, unroll=True)
    for d in range(2):
        for i in range(2 * W // HALF):
            rows = pl.ds(i * HALF, HALF)
            out_left[d, rows, :] = acc[d, 0, rows, :] * scale
            out_right[d, rows, :] = acc[d, 3, rows, :] * scale
            for q in range(2):
                cols = pl.ds(q * HALF, HALF)
                step = acc[d, q + 1, rows, :] * scale
                if 1 <= i <= 2:
                    step += tile[d, pl.ds((i - 1) * HALF, HALF), cols]
                out_mid[d, rows, cols] = step
    for out, side_of in ((mine, co), (other, 1 - co)):

        def flush(i, carry):
            rows = pl.ds(pl.multiple_of(side_of * HALF + i * 8, 8), 8)
            for n in range(2 * MODES):
                out[i, n] = grads[n, rows, :]
            out[i, 2 * MODES] = weight[rows, :]
            return carry

        lax.fori_loop(0, 16, flush, 0)


def correct(offsets, flags, border, probe, amplitude):
    fwd, bwd = dft_matrices()
    vmem = pl.BlockSpec(memory_space=pltpu.VMEM)
    smem = pl.BlockSpec(memory_space=pltpu.SMEM)
    part = jax.ShapeDtypeStruct((16, 2 * MODES + 1, 8, W), F32)
    strip = jax.ShapeDtypeStruct((2, 2 * W, HALF), F32)
    return pl.pallas_call(
        kernel,
        out_shape=(part, part, strip, strip, jax.ShapeDtypeStruct((2, 2 * W, W), F32)),
        in_specs=[smem, smem] + [vmem] * 9 + [pl.BlockSpec(memory_space=pl.ANY)] * 2,
        out_specs=(vmem,) * 5,
        scratch_shapes=[
            pltpu.VMEM((2, 4, 2 * W, HALF), F32),
            pltpu.VMEM((2, 4, 2 * W, HALF), F32),
            pltpu.VMEM((2, W, W), F32),
            pltpu.VMEM((MODES, 2 * W, W), BF),
            pltpu.VMEM((MODES, W, 2 * W), BF),
            pltpu.VMEM((MODES, W, 2 * W), F32),
            pltpu.VMEM((W, W), F32),
            pltpu.VMEM((2 * MODES, W, W), F32),
            pltpu.VMEM((W, W), F32),
            pltpu.VMEM((2 * W, 2 * W), BF),
            pltpu.VMEM((2 * W, 2 * W), BF),
            pltpu.SemaphoreType.DMA((2,)),
        ],
        compiler_params=pltpu.CompilerParams(vmem_limit_bytes=20 << 20),
    )(offsets, flags, *border, probe, amplitude, jnp.asarray(fwd), jnp.asarray(bwd))


GX = ("z", "xl")
GY = ("xh", "y", "co")
NEAR = [(0, 1), (1, 0)]
UP = [(i, (i + 1) % 16) for i in range(16)]
DOWN = [(j, i) for i, j in UP]
FAR = [(i, (i + 1) % 16 if i % 2 else (i - 1) % 16) for i in range(16)]


def arrange_kernel(half, own, swapped, out):
    h = half[0]
    for source, side_of in ((own, h), (swapped, 1 - h)):
        for i in range(16):
            rows = pl.ds(pl.multiple_of(side_of * HALF + i * 8, 8), 8)
            for n in range(2 * MODES):
                out[n // 2, n % 2, rows, :] = source[i, n]


def arrange(half, own, swapped):
    vmem = pl.BlockSpec(memory_space=pltpu.VMEM)
    return pl.pallas_call(
        arrange_kernel,
        out_shape=jax.ShapeDtypeStruct((MODES, 2, W, W), F32),
        in_specs=[pl.BlockSpec(memory_space=pltpu.SMEM), vmem, vmem],
        out_specs=vmem,
        compiler_params=pltpu.CompilerParams(vmem_limit_bytes=4 << 20),
    )(half, own, swapped)


def body(object_field, probe_field, amplitude, offsets):
    group = ("xh", "xl", "y")
    co, xl = lax.axis_index("co"), lax.axis_index("xl")
    block = (co * 16 + lax.axis_index(group)) * 8
    offs = offsets.transpose(1, 2, 0).reshape(2, POS)
    half_in, half_out = (1 - co) * HALF, co * HALF
    rows_at_in, rows_at_out = (1 - xl) * HALF, xl * HALF
    scalars = (co, block, half_in, half_out, rows_at_in, rows_at_out)
    flags = jnp.stack([co, xl])
    object_field, flags, *scalars = lax.optimization_barrier((object_field, flags, *scalars))
    co, block, half_in, half_out, rows_at_in, rows_at_out = scalars
    cut = lax.dynamic_slice_in_dim
    rows_in = lax.ppermute(cut(object_field, rows_at_in, HALF, 1), "xl", NEAR)
    rows_out = lax.ppermute(cut(object_field, rows_at_out, HALF, 1), GX, FAR)
    cols_in = lax.ppermute(cut(object_field, half_in, HALF, 2), "co", NEAR)
    cols_out = lax.ppermute(cut(object_field, half_out, HALF, 2), GY, FAR)
    rows_out, rows_in = lax.optimization_barrier((rows_out, rows_in))
    ends_in = lax.ppermute(jnp.stack([cut(rows, half_in, HALF, 2) for rows in (rows_out, rows_in)]), "co", NEAR)
    ends_out = lax.ppermute(jnp.stack([cut(rows, half_out, HALF, 2) for rows in (rows_out, rows_in)]), GY, FAR)
    border = (object_field, rows_in, rows_out, cols_in, cols_out, ends_in, ends_out)
    mine, other, out_left, out_right, middle = correct(offs, flags, border, probe_field, amplitude)
    from_right = lax.ppermute(out_left, GY, DOWN)
    from_left = lax.ppermute(out_right, GY, UP)
    part = mine + lax.ppermute(other, "co", NEAR)
    pieces = lax.all_to_all(part, group, 0, 0, tiled=True)
    part = sum(pieces[i] for i in range(16))
    folded = middle + jnp.concatenate([from_left, from_right], 2)
    part, folded = lax.optimization_barrier((part, folded))
    from_below = lax.ppermute(folded[:, :HALF], GX, DOWN)
    from_above = lax.ppermute(folded[:, HALF + W :], GX, UP)
    peers = [lax.ppermute(part, "z", [(i, i ^ step) for i in range(8)]) for step in (2, 4, 6)]
    part = (part + peers[0]) + (peers[1] + peers[2])
    part = part + lax.ppermute(part, "z", [(i, i ^ 1) for i in range(8)])
    part, from_below, from_above = lax.optimization_barrier((part, from_below, from_above))
    local = cut(probe_field.reshape(2 * MODES, W, W), block, 8, 1)
    weight = part[2 * MODES]
    local = local + (part[: 2 * MODES] - local * weight) / (weight + 1e-05)
    gathered = lax.all_to_all(jnp.broadcast_to(local[None], (16,) + local.shape), group, 0, 0, tiled=True)
    updated_object = folded[:, HALF : HALF + W] + jnp.concatenate([from_above, from_below], 1)
    updated_probe = arrange(flags, gathered, lax.ppermute(gathered, "co", NEAR))
    return (updated_object, updated_probe)


def solution(mesh):
    fine = Mesh(mesh.devices.reshape(8, 2, 2, 4, 2), ("z", "xl", "xh", "y", "co"))
    in_specs = (P(None, GX, GY), P(), P(GX, GY, None, None), P(GX, GY, None))
    out_specs = (P(None, GX, GY), P())
    return jax.shard_map(body, mesh=fine, in_specs=in_specs, out_specs=out_specs, check_vma=False)
```

```python
import functools
import math

import jax
import jax.numpy as jnp
import ml_dtypes
import numpy as np
from jax import lax
from jax.experimental import pallas as pl
from jax.experimental.pallas import tpu as pltpu
from jax.sharding import Mesh
from jax.sharding import PartitionSpec as P

W = 256
HALF = 128
POS = 4
MODES = 2
CH = 32
BF = jnp.bfloat16
F32 = jnp.float32


def dft_matrices():
    k = np.arange(W)
    phase = (k[:, None] * k[None, :]) % W
    angle = phase.astype(np.float32) * np.float32(2.0 * math.pi / W)
    norm = np.float32(1.0 / math.sqrt(W))
    c = (np.cos(angle) * norm).astype(ml_dtypes.bfloat16)
    s = (np.sin(angle) * norm).astype(ml_dtypes.bfloat16)
    fwd = np.block([[c, s], [-s, c]])
    bwd = np.block([[c, -s], [s, c]])
    return fwd, bwd


def kernel(
    offs, core, x_low, tile, rows_in, rows_out, cols_in, cols_out, ends_in, ends_out, probe, amp, fwd_hbm, bwd_hbm,
    mine, other, out_left, out_right, out_mid,
    ext, acc, win, stack, side, far, weight, grads, power, fwd, bwd, sems,
):
    copies = [
        pltpu.make_async_copy(fwd_hbm, fwd, sems.at[0]),
        pltpu.make_async_copy(bwd_hbm, bwd, sems.at[1]),
    ]
    for copy in copies:
        copy.start()
    co = core[0]
    middle = pl.ds(HALF, W)
    lanes = lax.broadcasted_iota(jnp.int32, (CH, HALF), 1)
    for q in range(2):
        ext[:, q + 1, middle, :] = tile[:, :, q * HALF : (q + 1) * HALF]
    before, after = pl.ds(0, HALF), pl.ds(HALF + W, HALF)
    for x, at_in, at_out in ((0, after, before), (1, before, after)):

        @pl.when(x_low[0] == x)
        def _():
            for q in range(2):
                ext[:, q + 1, at_in, :] = rows_in[:, :, q * HALF : (q + 1) * HALF]
                ext[:, q + 1, at_out, :] = rows_out[:, :, q * HALF : (q + 1) * HALF]

        for c, q_in, q_out in ((0, 3, 0), (1, 0, 3)):

            @pl.when((x_low[0] == x) & (co == c))
            def _():
                for q, cols, ends in ((q_in, cols_in, ends_in), (q_out, cols_out, ends_out)):
                    ext[:, q, middle, :] = cols[...]
                    ext[:, q, at_out, :] = ends[0]
                    ext[:, q, at_in, :] = ends[1]

    acc[...] = jnp.zeros_like(acc)
    weight[...] = jnp.zeros_like(weight)
    grads[...] = jnp.zeros_like(grads)
    top_power = jnp.zeros((CH, W), F32)
    for i in range(W // CH):
        rows = pl.ds(i * CH, CH)
        total = jnp.zeros((CH, W), F32)
        for k in range(MODES):
            total += probe[k, 0, rows, :] * probe[k, 0, rows, :] + probe[k, 1, rows, :] * probe[k, 1, rows, :]
        power[rows, :] = total
        top_power = jnp.maximum(top_power, total)
    scale = 1.0 / (jnp.max(top_power, axis=(0, 1), keepdims=True) + 1e-06)

    def position(p):
        r = offs[0, p] + HALF
        c = offs[1, p] + HALF
        q = c // HALF
        s = c - q * HALF
        back_shift = lax.rem(HALF - s, HALF)
        keep = lanes < HALF - s
        q2 = jnp.minimum(q + 2, 3)

        def cut(i, carry):
            rows = pl.ds(pl.multiple_of(i * CH, CH), CH)
            w = []
            for d in range(2):
                src = pl.ds(r + i * CH, CH)
                a = pltpu.roll(ext[d, q, src, :], back_shift, 1)
                b = pltpu.roll(ext[d, q + 1, src, :], back_shift, 1)
                e = pltpu.roll(ext[d, q2, src, :], back_shift, 1)
                w.append(jnp.concatenate([jnp.where(keep, a, b), jnp.where(keep, b, e)], 1))
                win[d, rows, :] = w[d]
            weight[rows, :] += w[0] * w[0] + w[1] * w[1]
            for k in range(MODES):
                pr = probe[k, 0, rows, :]
                pi = probe[k, 1, rows, :]
                stack[k, rows, :] = (pr * w[0] - pi * w[1]).astype(BF)
                stack[k, pl.ds(pl.multiple_of(W + i * CH, CH), CH), :] = (pr * w[1] + pi * w[0]).astype(BF)
            return carry

        lax.fori_loop(0, W // CH, cut, 0, unroll=True)
        if p == 0:
            for copy in copies:
                copy.wait()
        for k in range(MODES):
            rows_f = jnp.dot(fwd[...], stack[k], preferred_element_type=F32)
            side[k, :, 0:W] = rows_f[0:W].astype(BF)
            side[k, :, W:] = rows_f[W:].astype(BF)
        for k in range(MODES):
            far[k] = jnp.dot(side[k], bwd[...], preferred_element_type=F32)

        def project(i, carry):
            rows = pl.ds(pl.multiple_of(i * CH, CH), CH)
            rows_im = pl.ds(pl.multiple_of(W + i * CH, CH), CH)
            f = [far[k, rows, :] for k in range(MODES)]
            total = f[0] * f[0] + f[1] * f[1]
            intensity = total[:, 0:W] + total[:, W:]
            factor = amp[p, 0, rows, :] * lax.rsqrt(jnp.maximum(intensity, 0.0625))
            for k in range(MODES):
                stack[k, rows, :] = (f[k][:, 0:W] * factor).astype(BF)
                stack[k, rows_im, :] = (f[k][:, W:] * factor).astype(BF)
            return carry

        lax.fori_loop(0, W // CH, project, 0, unroll=True)
        for k in range(MODES):
            rows_b = jnp.dot(bwd[...], stack[k], preferred_element_type=F32)
            side[k, :, 0:W] = rows_b[0:W].astype(BF)
            side[k, :, W:] = rows_b[W:].astype(BF)
        for k in range(MODES):
            far[k] = jnp.dot(side[k], fwd[...], preferred_element_type=F32)

        def spread(i, carry):
            rows = pl.ds(pl.multiple_of(i * CH, CH), CH)
            wr = win[0, rows, :]
            wi = win[1, rows, :]
            both = power[rows, :]
            tr = jnp.zeros((CH, W), F32)
            ti = jnp.zeros((CH, W), F32)
            for k in range(MODES):
                pr = probe[k, 0, rows, :]
                pi = probe[k, 1, rows, :]
                br = far[k, rows, 0:W]
                bi = far[k, rows, W:]
                tr += pr * br + pi * bi
                ti += pr * bi - pi * br
                grads[2 * k, rows, :] += wr * br + wi * bi
                grads[2 * k + 1, rows, :] += wr * bi - wi * br
            dst = pl.ds(r + i * CH, CH)
            for d, t in ((0, tr - both * wr), (1, ti - both * wi)):
                a = pltpu.roll(t[:, 0:HALF], s, 1)
                b = pltpu.roll(t[:, HALF:], s, 1)
                low = lanes < s
                acc[d, q, dst, :] += jnp.where(low, 0.0, a)
                acc[d, q + 1, dst, :] += jnp.where(low, a, b)
                acc[d, q2, dst, :] += jnp.where(low, b, 0.0)
            return carry

        lax.fori_loop(0, W // CH, spread, 0, unroll=True)

    for p in range(POS):
        position(p)
    for d in range(2):
        for i in range(2 * W // HALF):
            rows = pl.ds(i * HALF, HALF)
            out_left[d, rows, :] = acc[d, 0, rows, :] * scale
            out_right[d, rows, :] = acc[d, 3, rows, :] * scale
            for q in range(2):
                cols = pl.ds(q * HALF, HALF)
                step = acc[d, q + 1, rows, :] * scale
                if 1 <= i <= 2:
                    step += tile[d, pl.ds((i - 1) * HALF, HALF), cols]
                out_mid[d, rows, cols] = step
    for out, side_of in ((mine, co), (other, 1 - co)):

        def flush(i, carry):
            rows = pl.ds(pl.multiple_of(side_of * HALF + i * 8, 8), 8)
            for n in range(2 * MODES):
                out[i, n] = grads[n, rows, :]
            out[i, 2 * MODES] = weight[rows, :]
            return carry

        lax.fori_loop(0, 16, flush, 0)


def correct(offsets, place, border, probe, amplitude):
    fwd, bwd = dft_matrices()
    vmem = pl.BlockSpec(memory_space=pltpu.VMEM)
    smem = pl.BlockSpec(memory_space=pltpu.SMEM)
    part = jax.ShapeDtypeStruct((16, 2 * MODES + 1, 8, W), F32)
    strip = jax.ShapeDtypeStruct((2, 2 * W, HALF), F32)
    return pl.pallas_call(
        kernel,
        out_shape=(part, part, strip, strip, jax.ShapeDtypeStruct((2, 2 * W, W), F32)),
        in_specs=[smem] * 3 + [vmem] * 9 + [pl.BlockSpec(memory_space=pl.ANY)] * 2,
        out_specs=(vmem,) * 5,
        scratch_shapes=[
            pltpu.VMEM((2, 4, 2 * W, HALF), F32),
            pltpu.VMEM((2, 4, 2 * W, HALF), F32),
            pltpu.VMEM((2, W, W), F32),
            pltpu.VMEM((MODES, 2 * W, W), BF),
            pltpu.VMEM((MODES, W, 2 * W), BF),
            pltpu.VMEM((MODES, W, 2 * W), F32),
            pltpu.VMEM((W, W), F32),
            pltpu.VMEM((2 * MODES, W, W), F32),
            pltpu.VMEM((W, W), F32),
            pltpu.VMEM((2 * W, 2 * W), BF),
            pltpu.VMEM((2 * W, 2 * W), BF),
            pltpu.SemaphoreType.DMA((2,)),
        ],
        compiler_params=pltpu.CompilerParams(vmem_limit_bytes=20 << 20),
    )(offsets, *place, *border, probe, amplitude, jnp.asarray(fwd), jnp.asarray(bwd))


GX = ("z", "xl")
GY = ("xh", "y", "co")
NEAR = [(0, 1), (1, 0)]
UP = [(i, (i + 1) % 16) for i in range(16)]
DOWN = [(j, i) for i, j in UP]
FAR = [(i, (i + 1) % 16 if i % 2 else (i - 1) % 16) for i in range(16)]


def arrange_kernel(half, own, swapped, out):
    h = half[0]
    for source, side_of in ((own, h), (swapped, 1 - h)):
        for i in range(16):
            rows = pl.ds(pl.multiple_of(side_of * HALF + i * 8, 8), 8)
            for n in range(2 * MODES):
                out[n // 2, n % 2, rows, :] = source[i, n]


def arrange(half, own, swapped):
    vmem = pl.BlockSpec(memory_space=pltpu.VMEM)
    return pl.pallas_call(
        arrange_kernel,
        out_shape=jax.ShapeDtypeStruct((MODES, 2, W, W), F32),
        in_specs=[pl.BlockSpec(memory_space=pltpu.SMEM), vmem, vmem],
        out_specs=vmem,
        compiler_params=pltpu.CompilerParams(vmem_limit_bytes=4 << 20),
    )(half, own, swapped)


def body(object_field, probe_field, amplitude, offsets):
    group = ("xh", "xl", "y")
    co, xl = lax.axis_index("co"), lax.axis_index("xl")
    block = (co * 16 + lax.axis_index(group)) * 8
    offs = offsets.transpose(1, 2, 0).reshape(2, POS)
    half_in, half_out = (1 - co) * HALF, co * HALF
    rows_at_in, rows_at_out = (1 - xl) * HALF, xl * HALF
    scalars = (co, block, half_in, half_out, rows_at_in, rows_at_out)
    place = (co.reshape(1), xl.reshape(1))
    object_field, place, *scalars = lax.optimization_barrier((object_field, place, *scalars))
    co, block, half_in, half_out, rows_at_in, rows_at_out = scalars
    cut = lax.dynamic_slice_in_dim
    rows_in = lax.ppermute(cut(object_field, rows_at_in, HALF, 1), "xl", NEAR)
    rows_out = lax.ppermute(cut(object_field, rows_at_out, HALF, 1), GX, FAR)
    cols_in = lax.ppermute(cut(object_field, half_in, HALF, 2), "co", NEAR)
    cols_out = lax.ppermute(cut(object_field, half_out, HALF, 2), GY, FAR)
    rows_out, rows_in = lax.optimization_barrier((rows_out, rows_in))
    ends_in = lax.ppermute(jnp.stack([cut(rows, half_in, HALF, 2) for rows in (rows_out, rows_in)]), "co", NEAR)
    ends_out = lax.ppermute(jnp.stack([cut(rows, half_out, HALF, 2) for rows in (rows_out, rows_in)]), GY, FAR)
    border = (object_field, rows_in, rows_out, cols_in, cols_out, ends_in, ends_out)
    mine, other, out_left, out_right, middle = correct(offs, place, border, probe_field, amplitude)
    from_right = lax.ppermute(out_left, GY, DOWN)
    from_left = lax.ppermute(out_right, GY, UP)
    part = mine + lax.ppermute(other, "co", NEAR)
    pieces = lax.all_to_all(part, group, 0, 0, tiled=True)
    part = sum(pieces[i] for i in range(16))
    folded = middle + jnp.concatenate([from_left, from_right], 2)
    part, folded = lax.optimization_barrier((part, folded))
    from_below = lax.ppermute(folded[:, :HALF], GX, DOWN)
    from_above = lax.ppermute(folded[:, HALF + W :], GX, UP)
    peers = [lax.ppermute(part, "z", [(i, i ^ step) for i in range(8)]) for step in (2, 4, 6)]
    part = (part + peers[0]) + (peers[1] + peers[2])
    part = part + lax.ppermute(part, "z", [(i, i ^ 1) for i in range(8)])
    part, from_below, from_above = lax.optimization_barrier((part, from_below, from_above))
    local = cut(probe_field.reshape(2 * MODES, W, W), block, 8, 1)
    weight = part[2 * MODES]
    local = local + (part[: 2 * MODES] - local * weight) / (weight + 1e-05)
    gathered = lax.all_to_all(jnp.broadcast_to(local[None], (16,) + local.shape), group, 0, 0, tiled=True)
    updated_object = folded[:, HALF : HALF + W] + jnp.concatenate([from_above, from_below], 1)
    updated_probe = arrange(place[0], gathered, lax.ppermute(gathered, "co", NEAR))
    return (updated_object, updated_probe)


def solution(mesh):
    fine = Mesh(mesh.devices.reshape(8, 2, 2, 4, 2), ("z", "xl", "xh", "y", "co"))
    in_specs = (P(None, GX, GY), P(), P(GX, GY, None, None), P(GX, GY, None))
    out_specs = (P(None, GX, GY), P())
    return jax.shard_map(body, mesh=fine, in_specs=in_specs, out_specs=out_specs, check_vma=False)
```

```python
import functools
import math

import jax
import jax.numpy as jnp
import ml_dtypes
import numpy as np
from jax import lax
from jax.experimental import pallas as pl
from jax.experimental.pallas import tpu as pltpu
from jax.sharding import Mesh
from jax.sharding import PartitionSpec as P

W = 256
HALF = 128
POS = 4
MODES = 2
CH = 32
BF = jnp.bfloat16
F32 = jnp.float32


def dft_matrices():
    k = np.arange(W)
    phase = (k[:, None] * k[None, :]) % W
    angle = phase.astype(np.float32) * np.float32(2.0 * math.pi / W)
    norm = np.float32(1.0 / math.sqrt(W))
    c = (np.cos(angle) * norm).astype(ml_dtypes.bfloat16)
    s = (np.sin(angle) * norm).astype(ml_dtypes.bfloat16)
    fwd = np.block([[c, s], [-s, c]])
    bwd = np.block([[c, -s], [s, c]])
    return fwd, bwd


def kernel(
    offs, half, tile, top, bot, left, right, left_ends, right_ends, probe, amp, fwd_hbm, bwd_hbm,
    mine, other, out_left, out_mid, out_right,
    ext, acc, win, stack, side, far, weight, grads, power, fwd, bwd, sems,
):
    copies = [
        pltpu.make_async_copy(fwd_hbm, fwd, sems.at[0]),
        pltpu.make_async_copy(bwd_hbm, bwd, sems.at[1]),
    ]
    for copy in copies:
        copy.start()
    lanes = lax.broadcasted_iota(jnp.int32, (CH, HALF), 1)
    for q in range(2):
        cols = pl.ds(q * HALF, HALF)
        ext[:, q + 1, 0:HALF, :] = top[:, :, cols]
        ext[:, q + 1, HALF : HALF + W, :] = tile[:, :, cols]
        ext[:, q + 1, HALF + W :, :] = bot[:, :, cols]
    for q, middle, ends in ((0, left, left_ends), (3, right, right_ends)):
        ext[:, q, 0:HALF, :] = ends[0]
        ext[:, q, HALF : HALF + W, :] = middle[...]
        ext[:, q, HALF + W :, :] = ends[1]
    acc[...] = jnp.zeros_like(acc)
    weight[...] = jnp.zeros_like(weight)
    grads[...] = jnp.zeros_like(grads)
    top_power = jnp.zeros((CH, W), F32)
    for i in range(W // CH):
        rows = pl.ds(i * CH, CH)
        total = jnp.zeros((CH, W), F32)
        for k in range(MODES):
            total += probe[k, 0, rows, :] * probe[k, 0, rows, :] + probe[k, 1, rows, :] * probe[k, 1, rows, :]
        power[rows, :] = total
        top_power = jnp.maximum(top_power, total)
    scale = 1.0 / (jnp.max(top_power, axis=(0, 1), keepdims=True) + 1e-06)

    def position(p):
        r = offs[0, p] + HALF
        c = offs[1, p] + HALF
        q = c // HALF
        s = c - q * HALF
        back_shift = lax.rem(HALF - s, HALF)
        keep = lanes < HALF - s
        q2 = jnp.minimum(q + 2, 3)

        def cut(i, carry):
            rows = pl.ds(pl.multiple_of(i * CH, CH), CH)
            w = []
            for d in range(2):
                src = pl.ds(r + i * CH, CH)
                a = pltpu.roll(ext[d, q, src, :], back_shift, 1)
                b = pltpu.roll(ext[d, q + 1, src, :], back_shift, 1)
                e = pltpu.roll(ext[d, q2, src, :], back_shift, 1)
                w.append(jnp.concatenate([jnp.where(keep, a, b), jnp.where(keep, b, e)], 1))
                win[d, rows, :] = w[d]
            weight[rows, :] += w[0] * w[0] + w[1] * w[1]
            for k in range(MODES):
                pr = probe[k, 0, rows, :]
                pi = probe[k, 1, rows, :]
                stack[k, rows, :] = (pr * w[0] - pi * w[1]).astype(BF)
                stack[k, pl.ds(pl.multiple_of(W + i * CH, CH), CH), :] = (pr * w[1] + pi * w[0]).astype(BF)
            return carry

        lax.fori_loop(0, W // CH, cut, 0, unroll=True)
        if p == 0:
            for copy in copies:
                copy.wait()
        for k in range(MODES):
            rows_f = jnp.dot(fwd[...], stack[k], preferred_element_type=F32)
            side[k, :, 0:W] = rows_f[0:W].astype(BF)
            side[k, :, W:] = rows_f[W:].astype(BF)
        for k in range(MODES):
            far[k] = jnp.dot(side[k], bwd[...], preferred_element_type=F32)

        def project(i, carry):
            rows = pl.ds(pl.multiple_of(i * CH, CH), CH)
            rows_im = pl.ds(pl.multiple_of(W + i * CH, CH), CH)
            f = [far[k, rows, :] for k in range(MODES)]
            total = f[0] * f[0] + f[1] * f[1]
            intensity = total[:, 0:W] + total[:, W:]
            factor = amp[p, 0, rows, :] * lax.rsqrt(jnp.maximum(intensity, 0.0625))
            for k in range(MODES):
                stack[k, rows, :] = (f[k][:, 0:W] * factor).astype(BF)
                stack[k, rows_im, :] = (f[k][:, W:] * factor).astype(BF)
            return carry

        lax.fori_loop(0, W // CH, project, 0, unroll=True)
        for k in range(MODES):
            rows_b = jnp.dot(bwd[...], stack[k], preferred_element_type=F32)
            side[k, :, 0:W] = rows_b[0:W].astype(BF)
            side[k, :, W:] = rows_b[W:].astype(BF)
        for k in range(MODES):
            far[k] = jnp.dot(side[k], fwd[...], preferred_element_type=F32)

        def spread(i, carry):
            rows = pl.ds(pl.multiple_of(i * CH, CH), CH)
            wr = win[0, rows, :]
            wi = win[1, rows, :]
            both = power[rows, :]
            tr = jnp.zeros((CH, W), F32)
            ti = jnp.zeros((CH, W), F32)
            for k in range(MODES):
                pr = probe[k, 0, rows, :]
                pi = probe[k, 1, rows, :]
                br = far[k, rows, 0:W]
                bi = far[k, rows, W:]
                tr += pr * br + pi * bi
                ti += pr * bi - pi * br
                grads[2 * k, rows, :] += wr * br + wi * bi
                grads[2 * k + 1, rows, :] += wr * bi - wi * br
            dst = pl.ds(r + i * CH, CH)
            for d, t in ((0, tr - both * wr), (1, ti - both * wi)):
                a = pltpu.roll(t[:, 0:HALF], s, 1)
                b = pltpu.roll(t[:, HALF:], s, 1)
                low = lanes < s
                acc[d, q, dst, :] += jnp.where(low, 0.0, a)
                acc[d, q + 1, dst, :] += jnp.where(low, a, b)
                acc[d, q2, dst, :] += jnp.where(low, b, 0.0)
            return carry

        lax.fori_loop(0, W // CH, spread, 0, unroll=True)

    for p in range(POS):
        position(p)
    for d in range(2):
        for i in range(2 * W // HALF):
            rows = pl.ds(i * HALF, HALF)
            out_left[d, rows, :] = acc[d, 0, rows, :] * scale
            out_right[d, rows, :] = acc[d, 3, rows, :] * scale
            for q in range(2):
                cols = pl.ds(q * HALF, HALF)
                step = acc[d, q + 1, rows, :] * scale
                if 1 <= i <= 2:
                    step += tile[d, pl.ds((i - 1) * HALF, HALF), cols]
                out_mid[d, rows, cols] = step
    h = half[0]
    for out, side_of in ((mine, h), (other, 1 - h)):

        def flush(i, carry):
            rows = pl.ds(pl.multiple_of(side_of * HALF + i * 8, 8), 8)
            for n in range(2 * MODES):
                out[i, n] = grads[n, rows, :]
            out[i, 2 * MODES] = weight[rows, :]
            return carry

        lax.fori_loop(0, 16, flush, 0)


def correct(offsets, half, border, probe, amplitude):
    fwd, bwd = dft_matrices()
    vmem = pl.BlockSpec(memory_space=pltpu.VMEM)
    smem = pl.BlockSpec(memory_space=pltpu.SMEM)
    part = jax.ShapeDtypeStruct((16, 2 * MODES + 1, 8, W), F32)
    strip = jax.ShapeDtypeStruct((2, 2 * W, HALF), F32)
    return pl.pallas_call(
        kernel,
        out_shape=(part, part, strip, jax.ShapeDtypeStruct((2, 2 * W, W), F32), strip),
        in_specs=[smem, smem] + [vmem] * 9 + [pl.BlockSpec(memory_space=pl.ANY)] * 2,
        out_specs=(vmem,) * 5,
        scratch_shapes=[
            pltpu.VMEM((2, 4, 2 * W, HALF), F32),
            pltpu.VMEM((2, 4, 2 * W, HALF), F32),
            pltpu.VMEM((2, W, W), F32),
            pltpu.VMEM((MODES, 2 * W, W), BF),
            pltpu.VMEM((MODES, W, 2 * W), BF),
            pltpu.VMEM((MODES, W, 2 * W), F32),
            pltpu.VMEM((W, W), F32),
            pltpu.VMEM((2 * MODES, W, W), F32),
            pltpu.VMEM((W, W), F32),
            pltpu.VMEM((2 * W, 2 * W), BF),
            pltpu.VMEM((2 * W, 2 * W), BF),
            pltpu.SemaphoreType.DMA((2,)),
        ],
        compiler_params=pltpu.CompilerParams(vmem_limit_bytes=20 << 20),
    )(offsets, half, *border, probe, amplitude, jnp.asarray(fwd), jnp.asarray(bwd))


GX = ("z", "xl")
GY = ("xh", "y", "co")
UP = [(i, (i + 1) % 16) for i in range(16)]
DOWN = [(j, i) for i, j in UP]
SWAP = [(0, 1), (1, 0)]


def arrange_kernel(half, own, swapped, out):
    h = half[0]
    for source, side_of in ((own, h), (swapped, 1 - h)):
        for i in range(16):
            rows = pl.ds(pl.multiple_of(side_of * HALF + i * 8, 8), 8)
            for n in range(2 * MODES):
                out[n // 2, n % 2, rows, :] = source[i, n]


def arrange(half, own, swapped):
    vmem = pl.BlockSpec(memory_space=pltpu.VMEM)
    return pl.pallas_call(
        arrange_kernel,
        out_shape=jax.ShapeDtypeStruct((MODES, 2, W, W), F32),
        in_specs=[pl.BlockSpec(memory_space=pltpu.SMEM), vmem, vmem],
        out_specs=vmem,
        compiler_params=pltpu.CompilerParams(vmem_limit_bytes=4 << 20),
    )(half, own, swapped)


def body(object_field, probe_field, amplitude, offsets):
    group = ("xh", "xl", "y")
    co = lax.axis_index("co")
    half = co.reshape(1)
    block = (co * 16 + lax.axis_index(group)) * 8
    offs = offsets.transpose(1, 2, 0).reshape(2, POS)
    object_field, half, block = lax.optimization_barrier((object_field, half, block))
    first, last = slice(0, HALF), slice(HALF, W)
    top = lax.ppermute(object_field[:, last], GX, UP)
    bot = lax.ppermute(object_field[:, first], GX, DOWN)
    left = lax.ppermute(object_field[:, :, last], GY, UP)
    right = lax.ppermute(object_field[:, :, first], GY, DOWN)
    bot, top = lax.optimization_barrier((bot, top))
    left_ends = lax.ppermute(jnp.stack([top[:, :, last], bot[:, :, last]]), GY, UP)
    right_ends = lax.ppermute(jnp.stack([top[:, :, first], bot[:, :, first]]), GY, DOWN)
    border = (object_field, top, bot, left, right, left_ends, right_ends)
    mine, other, out_left, out_mid, out_right = correct(offs, half, border, probe_field, amplitude)
    part = mine + lax.ppermute(other, "co", SWAP)
    from_right = lax.ppermute(out_left, GY, DOWN)
    from_left = lax.ppermute(out_right, GY, UP)
    pieces = lax.all_to_all(part, group, 0, 0, tiled=True)
    part = sum(pieces[i] for i in range(16))
    folded = out_mid + jnp.concatenate([from_left, from_right], 2)
    part, folded = lax.optimization_barrier((part, folded))
    from_below = lax.ppermute(folded[:, :HALF], GX, DOWN)
    from_above = lax.ppermute(folded[:, HALF + W :], GX, UP)
    peers = [lax.ppermute(part, "z", [(i, i ^ step) for i in range(8)]) for step in (2, 4, 6)]
    part = (part + peers[0]) + (peers[1] + peers[2])
    part = part + lax.ppermute(part, "z", [(i, i ^ 1) for i in range(8)])
    part, from_below, from_above = lax.optimization_barrier((part, from_below, from_above))
    planes = probe_field.reshape(2 * MODES, W, W)
    local = lax.dynamic_slice_in_dim(planes, block, 8, 1)
    weight = part[2 * MODES]
    local = local + (part[: 2 * MODES] - local * weight) / (weight + 1e-05)
    gathered = lax.all_to_all(jnp.broadcast_to(local[None], (16,) + local.shape), group, 0, 0, tiled=True)
    updated_object = folded[:, HALF : HALF + W] + jnp.concatenate([from_above, from_below], 1)
    updated_probe = arrange(half, gathered, lax.ppermute(gathered, "co", SWAP))
    return (updated_object, updated_probe)


def solution(mesh):
    fine = Mesh(mesh.devices.reshape(8, 2, 2, 4, 2), ("z", "xl", "xh", "y", "co"))
    in_specs = (P(None, GX, GY), P(), P(GX, GY, None, None), P(GX, GY, None))
    out_specs = (P(None, GX, GY), P())
    return jax.shard_map(body, mesh=fine, in_specs=in_specs, out_specs=out_specs, check_vma=False)
```

```python
import functools
import math

import jax
import jax.numpy as jnp
import ml_dtypes
import numpy as np
from jax import lax
from jax.experimental import pallas as pl
from jax.experimental.pallas import tpu as pltpu
from jax.sharding import Mesh
from jax.sharding import PartitionSpec as P

W = 256
HALF = 128
POS = 4
MODES = 2
CH = 32
BF = jnp.bfloat16
F32 = jnp.float32


def dft_matrices():
    k = np.arange(W)
    phase = (k[:, None] * k[None, :]) % W
    angle = phase.astype(np.float32) * np.float32(2.0 * math.pi / W)
    norm = np.float32(1.0 / math.sqrt(W))
    c = (np.cos(angle) * norm).astype(ml_dtypes.bfloat16)
    s = (np.sin(angle) * norm).astype(ml_dtypes.bfloat16)
    fwd = np.block([[c, s], [-s, c]])
    bwd = np.block([[c, -s], [s, c]])
    return fwd, bwd


def kernel(
    offs, half, tile, top, bot, left, right, left_ends, right_ends, probe, amp, fwd_hbm, bwd_hbm,
    mine, other, out_left, out_mid, out_right,
    ext, acc, win, stack, side, far, weight, grads, power, fwd, bwd, sems,
):
    copies = [
        pltpu.make_async_copy(fwd_hbm, fwd, sems.at[0]),
        pltpu.make_async_copy(bwd_hbm, bwd, sems.at[1]),
    ]
    for copy in copies:
        copy.start()
    lanes = lax.broadcasted_iota(jnp.int32, (CH, HALF), 1)
    for q in range(2):
        cols = pl.ds(q * HALF, HALF)
        ext[:, q + 1, 0:HALF, :] = top[:, :, cols]
        ext[:, q + 1, HALF : HALF + W, :] = tile[:, :, cols]
        ext[:, q + 1, HALF + W :, :] = bot[:, :, cols]
    for q, middle, ends in ((0, left, left_ends), (3, right, right_ends)):
        ext[:, q, 0:HALF, :] = ends[0]
        ext[:, q, HALF : HALF + W, :] = middle[...]
        ext[:, q, HALF + W :, :] = ends[1]
    acc[...] = jnp.zeros_like(acc)
    weight[...] = jnp.zeros_like(weight)
    grads[...] = jnp.zeros_like(grads)
    top_power = jnp.zeros((CH, W), F32)
    for i in range(W // CH):
        rows = pl.ds(i * CH, CH)
        total = jnp.zeros((CH, W), F32)
        for k in range(MODES):
            total += probe[k, 0, rows, :] * probe[k, 0, rows, :] + probe[k, 1, rows, :] * probe[k, 1, rows, :]
        power[rows, :] = total
        top_power = jnp.maximum(top_power, total)
    scale = 1.0 / (jnp.max(top_power, axis=(0, 1), keepdims=True) + 1e-06)

    def position(p):
        r = offs[0, p] + HALF
        c = offs[1, p] + HALF
        q = c // HALF
        s = c - q * HALF
        back_shift = lax.rem(HALF - s, HALF)
        keep = lanes < HALF - s
        q2 = jnp.minimum(q + 2, 3)

        def cut(i, carry):
            rows = pl.ds(pl.multiple_of(i * CH, CH), CH)
            w = []
            for d in range(2):
                src = pl.ds(r + i * CH, CH)
                a = pltpu.roll(ext[d, q, src, :], back_shift, 1)
                b = pltpu.roll(ext[d, q + 1, src, :], back_shift, 1)
                e = pltpu.roll(ext[d, q2, src, :], back_shift, 1)
                w.append(jnp.concatenate([jnp.where(keep, a, b), jnp.where(keep, b, e)], 1))
                win[d, rows, :] = w[d]
            weight[rows, :] += w[0] * w[0] + w[1] * w[1]
            for k in range(MODES):
                pr = probe[k, 0, rows, :]
                pi = probe[k, 1, rows, :]
                stack[k, rows, :] = (pr * w[0] - pi * w[1]).astype(BF)
                stack[k, pl.ds(pl.multiple_of(W + i * CH, CH), CH), :] = (pr * w[1] + pi * w[0]).astype(BF)
            return carry

        lax.fori_loop(0, W // CH, cut, 0, unroll=True)
        if p == 0:
            for copy in copies:
                copy.wait()
        for k in range(MODES):
            rows_f = jnp.dot(fwd[...], stack[k], preferred_element_type=F32)
            side[k, :, 0:W] = rows_f[0:W].astype(BF)
            side[k, :, W:] = rows_f[W:].astype(BF)
        for k in range(MODES):
            far[k] = jnp.dot(side[k], bwd[...], preferred_element_type=F32)

        def project(i, carry):
            rows = pl.ds(pl.multiple_of(i * CH, CH), CH)
            rows_im = pl.ds(pl.multiple_of(W + i * CH, CH), CH)
            f = [far[k, rows, :] for k in range(MODES)]
            total = f[0] * f[0] + f[1] * f[1]
            intensity = total[:, 0:W] + total[:, W:]
            factor = amp[p, 0, rows, :] * lax.rsqrt(jnp.maximum(intensity, 0.0625))
            for k in range(MODES):
                stack[k, rows, :] = (f[k][:, 0:W] * factor).astype(BF)
                stack[k, rows_im, :] = (f[k][:, W:] * factor).astype(BF)
            return carry

        lax.fori_loop(0, W // CH, project, 0, unroll=True)
        for k in range(MODES):
            rows_b = jnp.dot(bwd[...], stack[k], preferred_element_type=F32)
            side[k, :, 0:W] = rows_b[0:W].astype(BF)
            side[k, :, W:] = rows_b[W:].astype(BF)
        for k in range(MODES):
            far[k] = jnp.dot(side[k], fwd[...], preferred_element_type=F32)

        def spread(i, carry):
            rows = pl.ds(pl.multiple_of(i * CH, CH), CH)
            wr = win[0, rows, :]
            wi = win[1, rows, :]
            both = power[rows, :]
            tr = jnp.zeros((CH, W), F32)
            ti = jnp.zeros((CH, W), F32)
            for k in range(MODES):
                pr = probe[k, 0, rows, :]
                pi = probe[k, 1, rows, :]
                br = far[k, rows, 0:W]
                bi = far[k, rows, W:]
                tr += pr * br + pi * bi
                ti += pr * bi - pi * br
                grads[2 * k, rows, :] += wr * br + wi * bi
                grads[2 * k + 1, rows, :] += wr * bi - wi * br
            dst = pl.ds(r + i * CH, CH)
            for d, t in ((0, tr - both * wr), (1, ti - both * wi)):
                a = pltpu.roll(t[:, 0:HALF], s, 1)
                b = pltpu.roll(t[:, HALF:], s, 1)
                low = lanes < s
                acc[d, q, dst, :] += jnp.where(low, 0.0, a)
                acc[d, q + 1, dst, :] += jnp.where(low, a, b)
                acc[d, q2, dst, :] += jnp.where(low, b, 0.0)
            return carry

        lax.fori_loop(0, W // CH, spread, 0, unroll=True)

    for p in range(POS):
        position(p)
    for d in range(2):
        for i in range(2 * W // HALF):
            rows = pl.ds(i * HALF, HALF)
            out_left[d, rows, :] = acc[d, 0, rows, :] * scale
            out_right[d, rows, :] = acc[d, 3, rows, :] * scale
            for q in range(2):
                cols = pl.ds(q * HALF, HALF)
                step = acc[d, q + 1, rows, :] * scale
                if 1 <= i <= 2:
                    step += tile[d, pl.ds((i - 1) * HALF, HALF), cols]
                out_mid[d, rows, cols] = step
    h = half[0]
    for out, side_of in ((mine, h), (other, 1 - h)):

        def flush(i, carry):
            rows = pl.ds(pl.multiple_of(side_of * HALF + i * 8, 8), 8)
            for n in range(2 * MODES):
                out[i, n] = grads[n, rows, :]
            out[i, 2 * MODES] = weight[rows, :]
            return carry

        lax.fori_loop(0, 16, flush, 0)


def correct(offsets, half, border, probe, amplitude):
    fwd, bwd = dft_matrices()
    vmem = pl.BlockSpec(memory_space=pltpu.VMEM)
    smem = pl.BlockSpec(memory_space=pltpu.SMEM)
    part = jax.ShapeDtypeStruct((16, 2 * MODES + 1, 8, W), F32)
    strip = jax.ShapeDtypeStruct((2, 2 * W, HALF), F32)
    return pl.pallas_call(
        kernel,
        out_shape=(part, part, strip, jax.ShapeDtypeStruct((2, 2 * W, W), F32), strip),
        in_specs=[smem, smem] + [vmem] * 9 + [pl.BlockSpec(memory_space=pl.ANY)] * 2,
        out_specs=(vmem,) * 5,
        scratch_shapes=[
            pltpu.VMEM((2, 4, 2 * W, HALF), F32),
            pltpu.VMEM((2, 4, 2 * W, HALF), F32),
            pltpu.VMEM((2, W, W), F32),
            pltpu.VMEM((MODES, 2 * W, W), BF),
            pltpu.VMEM((MODES, W, 2 * W), BF),
            pltpu.VMEM((MODES, W, 2 * W), F32),
            pltpu.VMEM((W, W), F32),
            pltpu.VMEM((2 * MODES, W, W), F32),
            pltpu.VMEM((W, W), F32),
            pltpu.VMEM((2 * W, 2 * W), BF),
            pltpu.VMEM((2 * W, 2 * W), BF),
            pltpu.SemaphoreType.DMA((2,)),
        ],
        compiler_params=pltpu.CompilerParams(vmem_limit_bytes=20 << 20),
    )(offsets, half, *border, probe, amplitude, jnp.asarray(fwd), jnp.asarray(bwd))


GX = ("z", "xl")
GY = ("xh", "y", "co")
UP = [(i, (i + 1) % 16) for i in range(16)]
DOWN = [(j, i) for i, j in UP]
SWAP = [(0, 1), (1, 0)]


def arrange_kernel(half, own, swapped, out):
    h = half[0]
    for source, side_of in ((own, h), (swapped, 1 - h)):
        for i in range(16):
            rows = pl.ds(pl.multiple_of(side_of * HALF + i * 8, 8), 8)
            for n in range(2 * MODES):
                out[n // 2, n % 2, rows, :] = source[i, n]


def arrange(half, own, swapped):
    vmem = pl.BlockSpec(memory_space=pltpu.VMEM)
    return pl.pallas_call(
        arrange_kernel,
        out_shape=jax.ShapeDtypeStruct((MODES, 2, W, W), F32),
        in_specs=[pl.BlockSpec(memory_space=pltpu.SMEM), vmem, vmem],
        out_specs=vmem,
        compiler_params=pltpu.CompilerParams(vmem_limit_bytes=4 << 20),
    )(half, own, swapped)


def body(object_field, probe_field, amplitude, offsets):
    group = ("xh", "xl", "y")
    co = lax.axis_index("co")
    half = co.reshape(1)
    block = (co * 16 + lax.axis_index(group)) * 8
    offs = offsets.transpose(1, 2, 0).reshape(2, POS)
    object_field, half, block = lax.optimization_barrier((object_field, half, block))
    first, last = slice(0, HALF), slice(HALF, W)
    top = lax.ppermute(object_field[:, last], GX, UP)
    bot = lax.ppermute(object_field[:, first], GX, DOWN)
    left = lax.ppermute(object_field[:, :, last], GY, UP)
    right = lax.ppermute(object_field[:, :, first], GY, DOWN)
    bot, top = lax.optimization_barrier((bot, top))
    left_ends = lax.ppermute(jnp.stack([top[:, :, last], bot[:, :, last]]), GY, UP)
    right_ends = lax.ppermute(jnp.stack([top[:, :, first], bot[:, :, first]]), GY, DOWN)
    border = (object_field, top, bot, left, right, left_ends, right_ends)
    mine, other, out_left, out_mid, out_right = correct(offs, half, border, probe_field, amplitude)
    part = mine + lax.ppermute(other, "co", SWAP)
    from_right = lax.ppermute(out_left, GY, DOWN)
    from_left = lax.ppermute(out_right, GY, UP)
    pieces = lax.all_to_all(part, group, 0, 0, tiled=True)
    part = sum(pieces[i] for i in range(16))
    folded = out_mid + jnp.concatenate([from_left, from_right], 2)
    part, folded = lax.optimization_barrier((part, folded))
    from_below = lax.ppermute(folded[:, :HALF], GX, DOWN)
    from_above = lax.ppermute(folded[:, HALF + W :], GX, UP)
    peers = [lax.ppermute(part, "z", [(i, i ^ step) for i in range(8)]) for step in (1, 2, 3)]
    part = (part + peers[0]) + (peers[1] + peers[2])
    part = part + lax.ppermute(part, "z", [(i, i ^ 4) for i in range(8)])
    part, from_below, from_above = lax.optimization_barrier((part, from_below, from_above))
    planes = probe_field.reshape(2 * MODES, W, W)
    local = lax.dynamic_slice_in_dim(planes, block, 8, 1)
    weight = part[2 * MODES]
    local = local + (part[: 2 * MODES] - local * weight) / (weight + 1e-05)
    gathered = lax.all_to_all(jnp.broadcast_to(local[None], (16,) + local.shape), group, 0, 0, tiled=True)
    updated_object = folded[:, HALF : HALF + W] + jnp.concatenate([from_above, from_below], 1)
    updated_probe = arrange(half, gathered, lax.ppermute(gathered, "co", SWAP))
    return (updated_object, updated_probe)


def solution(mesh):
    fine = Mesh(mesh.devices.reshape(8, 2, 2, 4, 2), ("z", "xl", "xh", "y", "co"))
    in_specs = (P(None, GX, GY), P(), P(GX, GY, None, None), P(GX, GY, None))
    out_specs = (P(None, GX, GY), P())
    return jax.shard_map(body, mesh=fine, in_specs=in_specs, out_specs=out_specs, check_vma=False)
```

```python
import functools
import math

import jax
import jax.numpy as jnp
import ml_dtypes
import numpy as np
from jax import lax
from jax.experimental import pallas as pl
from jax.experimental.pallas import tpu as pltpu
from jax.sharding import Mesh
from jax.sharding import PartitionSpec as P

W = 256
HALF = 128
POS = 4
MODES = 2
CH = 32
BF = jnp.bfloat16
F32 = jnp.float32


def dft_matrices():
    k = np.arange(W)
    phase = (k[:, None] * k[None, :]) % W
    angle = phase.astype(np.float32) * np.float32(2.0 * math.pi / W)
    norm = np.float32(1.0 / math.sqrt(W))
    c = (np.cos(angle) * norm).astype(ml_dtypes.bfloat16)
    s = (np.sin(angle) * norm).astype(ml_dtypes.bfloat16)
    fwd = np.block([[c, s], [-s, c]])
    bwd = np.block([[c, -s], [s, c]])
    return fwd, bwd


def kernel(
    offs, half, tile, top, bot, left, right, left_ends, right_ends, probe, amp, fwd_hbm, bwd_hbm,
    mine, other, out_left, out_mid, out_right,
    ext, acc, win, stack, side, far, weight, grads, power, fwd, bwd, sems,
):
    copies = [
        pltpu.make_async_copy(fwd_hbm, fwd, sems.at[0]),
        pltpu.make_async_copy(bwd_hbm, bwd, sems.at[1]),
    ]
    for copy in copies:
        copy.start()
    lanes = lax.broadcasted_iota(jnp.int32, (CH, HALF), 1)
    for q in range(2):
        cols = pl.ds(q * HALF, HALF)
        ext[:, q + 1, 0:HALF, :] = top[:, :, cols]
        ext[:, q + 1, HALF : HALF + W, :] = tile[:, :, cols]
        ext[:, q + 1, HALF + W :, :] = bot[:, :, cols]
    for q, middle, ends in ((0, left, left_ends), (3, right, right_ends)):
        ext[:, q, 0:HALF, :] = ends[0]
        ext[:, q, HALF : HALF + W, :] = middle[...]
        ext[:, q, HALF + W :, :] = ends[1]
    acc[...] = jnp.zeros_like(acc)
    weight[...] = jnp.zeros_like(weight)
    grads[...] = jnp.zeros_like(grads)
    top_power = jnp.zeros((CH, W), F32)
    for i in range(W // CH):
        rows = pl.ds(i * CH, CH)
        total = jnp.zeros((CH, W), F32)
        for k in range(MODES):
            total += probe[k, 0, rows, :] * probe[k, 0, rows, :] + probe[k, 1, rows, :] * probe[k, 1, rows, :]
        power[rows, :] = total
        top_power = jnp.maximum(top_power, total)
    scale = 1.0 / (jnp.max(top_power, axis=(0, 1), keepdims=True) + 1e-06)

    def position(p):
        r = offs[0, p] + HALF
        c = offs[1, p] + HALF
        q = c // HALF
        s = c - q * HALF
        back_shift = lax.rem(HALF - s, HALF)
        keep = lanes < HALF - s
        q2 = jnp.minimum(q + 2, 3)

        def cut(i, carry):
            rows = pl.ds(pl.multiple_of(i * CH, CH), CH)
            w = []
            for d in range(2):
                src = pl.ds(r + i * CH, CH)
                a = pltpu.roll(ext[d, q, src, :], back_shift, 1)
                b = pltpu.roll(ext[d, q + 1, src, :], back_shift, 1)
                e = pltpu.roll(ext[d, q2, src, :], back_shift, 1)
                w.append(jnp.concatenate([jnp.where(keep, a, b), jnp.where(keep, b, e)], 1))
                win[d, rows, :] = w[d]
            weight[rows, :] += w[0] * w[0] + w[1] * w[1]
            for k in range(MODES):
                pr = probe[k, 0, rows, :]
                pi = probe[k, 1, rows, :]
                stack[k, rows, :] = (pr * w[0] - pi * w[1]).astype(BF)
                stack[k, pl.ds(pl.multiple_of(W + i * CH, CH), CH), :] = (pr * w[1] + pi * w[0]).astype(BF)
            return carry

        lax.fori_loop(0, W // CH, cut, 0, unroll=True)
        if p == 0:
            for copy in copies:
                copy.wait()
        for k in range(MODES):
            rows_f = jnp.dot(fwd[...], stack[k], preferred_element_type=F32)
            side[k, :, 0:W] = rows_f[0:W].astype(BF)
            side[k, :, W:] = rows_f[W:].astype(BF)
        for k in range(MODES):
            far[k] = jnp.dot(side[k], bwd[...], preferred_element_type=F32)

        def project(i, carry):
            rows = pl.ds(pl.multiple_of(i * CH, CH), CH)
            rows_im = pl.ds(pl.multiple_of(W + i * CH, CH), CH)
            f = [far[k, rows, :] for k in range(MODES)]
            total = f[0] * f[0] + f[1] * f[1]
            intensity = total[:, 0:W] + total[:, W:]
            factor = amp[p, 0, rows, :] * lax.rsqrt(jnp.maximum(intensity, 0.0625))
            for k in range(MODES):
                stack[k, rows, :] = (f[k][:, 0:W] * factor).astype(BF)
                stack[k, rows_im, :] = (f[k][:, W:] * factor).astype(BF)
            return carry

        lax.fori_loop(0, W // CH, project, 0, unroll=True)
        for k in range(MODES):
            rows_b = jnp.dot(bwd[...], stack[k], preferred_element_type=F32)
            side[k, :, 0:W] = rows_b[0:W].astype(BF)
            side[k, :, W:] = rows_b[W:].astype(BF)
        for k in range(MODES):
            far[k] = jnp.dot(side[k], fwd[...], preferred_element_type=F32)

        def spread(i, carry):
            rows = pl.ds(pl.multiple_of(i * CH, CH), CH)
            wr = win[0, rows, :]
            wi = win[1, rows, :]
            both = power[rows, :]
            tr = jnp.zeros((CH, W), F32)
            ti = jnp.zeros((CH, W), F32)
            for k in range(MODES):
                pr = probe[k, 0, rows, :]
                pi = probe[k, 1, rows, :]
                br = far[k, rows, 0:W]
                bi = far[k, rows, W:]
                tr += pr * br + pi * bi
                ti += pr * bi - pi * br
                grads[2 * k, rows, :] += wr * br + wi * bi
                grads[2 * k + 1, rows, :] += wr * bi - wi * br
            dst = pl.ds(r + i * CH, CH)
            for d, t in ((0, tr - both * wr), (1, ti - both * wi)):
                a = pltpu.roll(t[:, 0:HALF], s, 1)
                b = pltpu.roll(t[:, HALF:], s, 1)
                low = lanes < s
                acc[d, q, dst, :] += jnp.where(low, 0.0, a)
                acc[d, q + 1, dst, :] += jnp.where(low, a, b)
                acc[d, q2, dst, :] += jnp.where(low, b, 0.0)
            return carry

        lax.fori_loop(0, W // CH, spread, 0, unroll=True)

    for p in range(POS):
        position(p)
    for d in range(2):
        for i in range(2 * W // HALF):
            rows = pl.ds(i * HALF, HALF)
            out_left[d, rows, :] = acc[d, 0, rows, :] * scale
            out_right[d, rows, :] = acc[d, 3, rows, :] * scale
            for q in range(2):
                cols = pl.ds(q * HALF, HALF)
                step = acc[d, q + 1, rows, :] * scale
                if 1 <= i <= 2:
                    step += tile[d, pl.ds((i - 1) * HALF, HALF), cols]
                out_mid[d, rows, cols] = step
    h = half[0]
    for out, side_of in ((mine, h), (other, 1 - h)):

        def flush(i, carry):
            rows = pl.ds(pl.multiple_of(side_of * HALF + i * 8, 8), 8)
            for n in range(2 * MODES):
                out[i, n] = grads[n, rows, :]
            out[i, 2 * MODES] = weight[rows, :]
            return carry

        lax.fori_loop(0, 16, flush, 0)


def correct(offsets, half, border, probe, amplitude):
    fwd, bwd = dft_matrices()
    vmem = pl.BlockSpec(memory_space=pltpu.VMEM)
    smem = pl.BlockSpec(memory_space=pltpu.SMEM)
    part = jax.ShapeDtypeStruct((16, 2 * MODES + 1, 8, W), F32)
    strip = jax.ShapeDtypeStruct((2, 2 * W, HALF), F32)
    return pl.pallas_call(
        kernel,
        out_shape=(part, part, strip, jax.ShapeDtypeStruct((2, 2 * W, W), F32), strip),
        in_specs=[smem, smem] + [vmem] * 9 + [pl.BlockSpec(memory_space=pl.ANY)] * 2,
        out_specs=(vmem,) * 5,
        scratch_shapes=[
            pltpu.VMEM((2, 4, 2 * W, HALF), F32),
            pltpu.VMEM((2, 4, 2 * W, HALF), F32),
            pltpu.VMEM((2, W, W), F32),
            pltpu.VMEM((MODES, 2 * W, W), BF),
            pltpu.VMEM((MODES, W, 2 * W), BF),
            pltpu.VMEM((MODES, W, 2 * W), F32),
            pltpu.VMEM((W, W), F32),
            pltpu.VMEM((2 * MODES, W, W), F32),
            pltpu.VMEM((W, W), F32),
            pltpu.VMEM((2 * W, 2 * W), BF),
            pltpu.VMEM((2 * W, 2 * W), BF),
            pltpu.SemaphoreType.DMA((2,)),
        ],
        compiler_params=pltpu.CompilerParams(vmem_limit_bytes=20 << 20),
    )(offsets, half, *border, probe, amplitude, jnp.asarray(fwd), jnp.asarray(bwd))


GX = ("z", "xl")
GY = ("xh", "y", "co")
UP = [(i, (i + 1) % 16) for i in range(16)]
DOWN = [(j, i) for i, j in UP]
SWAP = [(0, 1), (1, 0)]


def arrange_kernel(half, own, swapped, out):
    h = half[0]
    for source, side_of in ((own, h), (swapped, 1 - h)):
        for i in range(16):
            rows = pl.ds(pl.multiple_of(side_of * HALF + i * 8, 8), 8)
            for n in range(2 * MODES):
                out[n // 2, n % 2, rows, :] = source[i, n]


def arrange(half, own, swapped):
    vmem = pl.BlockSpec(memory_space=pltpu.VMEM)
    return pl.pallas_call(
        arrange_kernel,
        out_shape=jax.ShapeDtypeStruct((MODES, 2, W, W), F32),
        in_specs=[pl.BlockSpec(memory_space=pltpu.SMEM), vmem, vmem],
        out_specs=vmem,
        compiler_params=pltpu.CompilerParams(vmem_limit_bytes=4 << 20),
    )(half, own, swapped)


def body(object_field, probe_field, amplitude, offsets):
    group = ("xh", "xl", "y")
    co = lax.axis_index("co")
    half = co.reshape(1)
    block = (co * 16 + lax.axis_index(group)) * 8
    offs = offsets.transpose(1, 2, 0).reshape(2, POS)
    object_field, half, block = lax.optimization_barrier((object_field, half, block))
    first, last = slice(0, HALF), slice(HALF, W)
    top = lax.ppermute(object_field[:, last], GX, UP)
    bot = lax.ppermute(object_field[:, first], GX, DOWN)
    left = lax.ppermute(object_field[:, :, last], GY, UP)
    right = lax.ppermute(object_field[:, :, first], GY, DOWN)
    bot, top = lax.optimization_barrier((bot, top))
    left_ends = lax.ppermute(jnp.stack([top[:, :, last], bot[:, :, last]]), GY, UP)
    right_ends = lax.ppermute(jnp.stack([top[:, :, first], bot[:, :, first]]), GY, DOWN)
    border = (object_field, top, bot, left, right, left_ends, right_ends)
    mine, other, out_left, out_mid, out_right = correct(offs, half, border, probe_field, amplitude)
    part = mine + lax.ppermute(other, "co", SWAP)
    from_right = lax.ppermute(out_left, GY, DOWN)
    from_left = lax.ppermute(out_right, GY, UP)
    pieces = lax.all_to_all(part, group, 0, 0, tiled=True)
    part = sum(pieces[i] for i in range(16))
    folded = out_mid + jnp.concatenate([from_left, from_right], 2)
    part, folded = lax.optimization_barrier((part, folded))
    from_below = lax.ppermute(folded[:, :HALF], GX, DOWN)
    from_above = lax.ppermute(folded[:, HALF + W :], GX, UP)
    peers = [lax.ppermute(part, "z", [(i, i ^ step) for i in range(8)]) for step in (3, 2, 1)]
    part = (part + peers[0]) + (peers[1] + peers[2])
    part = part + lax.ppermute(part, "z", [(i, i ^ 4) for i in range(8)])
    part, from_below, from_above = lax.optimization_barrier((part, from_below, from_above))
    planes = probe_field.reshape(2 * MODES, W, W)
    local = lax.dynamic_slice_in_dim(planes, block, 8, 1)
    weight = part[2 * MODES]
    local = local + (part[: 2 * MODES] - local * weight) / (weight + 1e-05)
    gathered = lax.all_to_all(jnp.broadcast_to(local[None], (16,) + local.shape), group, 0, 0, tiled=True)
    updated_object = folded[:, HALF : HALF + W] + jnp.concatenate([from_above, from_below], 1)
    updated_probe = arrange(half, gathered, lax.ppermute(gathered, "co", SWAP))
    return (updated_object, updated_probe)


def solution(mesh):
    fine = Mesh(mesh.devices.reshape(8, 2, 2, 4, 2), ("z", "xl", "xh", "y", "co"))
    in_specs = (P(None, GX, GY), P(), P(GX, GY, None, None), P(GX, GY, None))
    out_specs = (P(None, GX, GY), P())
    return jax.shard_map(body, mesh=fine, in_specs=in_specs, out_specs=out_specs, check_vma=False)
```

```python
import functools
import math

import jax
import jax.numpy as jnp
import ml_dtypes
import numpy as np
from jax import lax
from jax.experimental import pallas as pl
from jax.experimental.pallas import tpu as pltpu
from jax.sharding import Mesh
from jax.sharding import PartitionSpec as P

W = 256
HALF = 128
POS = 4
MODES = 2
CH = 64
BF = jnp.bfloat16
F32 = jnp.float32


def dft_matrices():
    k = np.arange(W)
    phase = (k[:, None] * k[None, :]) % W
    angle = phase.astype(np.float32) * np.float32(2.0 * math.pi / W)
    norm = np.float32(1.0 / math.sqrt(W))
    c = (np.cos(angle) * norm).astype(ml_dtypes.bfloat16)
    s = (np.sin(angle) * norm).astype(ml_dtypes.bfloat16)
    fwd = np.block([[c, s], [-s, c]])
    bwd = np.block([[c, -s], [s, c]])
    return fwd, bwd


def kernel(
    offs, half, tile, top, bot, left, right, left_ends, right_ends, probe, amp, fwd_hbm, bwd_hbm,
    mine, other, out_left, out_mid, out_right,
    ext, acc, win, stack, side, far, weight, grads, power, fwd, bwd, sems,
):
    copies = [
        pltpu.make_async_copy(fwd_hbm, fwd, sems.at[0]),
        pltpu.make_async_copy(bwd_hbm, bwd, sems.at[1]),
    ]
    for copy in copies:
        copy.start()
    lanes = lax.broadcasted_iota(jnp.int32, (CH, HALF), 1)
    for q in range(2):
        cols = pl.ds(q * HALF, HALF)
        ext[:, q + 1, 0:HALF, :] = top[:, :, cols]
        ext[:, q + 1, HALF : HALF + W, :] = tile[:, :, cols]
        ext[:, q + 1, HALF + W :, :] = bot[:, :, cols]
    for q, middle, ends in ((0, left, left_ends), (3, right, right_ends)):
        ext[:, q, 0:HALF, :] = ends[0]
        ext[:, q, HALF : HALF + W, :] = middle[...]
        ext[:, q, HALF + W :, :] = ends[1]
    acc[...] = jnp.zeros_like(acc)
    weight[...] = jnp.zeros_like(weight)
    grads[...] = jnp.zeros_like(grads)
    top_power = jnp.zeros((CH, W), F32)
    for i in range(W // CH):
        rows = pl.ds(i * CH, CH)
        total = jnp.zeros((CH, W), F32)
        for k in range(MODES):
            total += probe[k, 0, rows, :] * probe[k, 0, rows, :] + probe[k, 1, rows, :] * probe[k, 1, rows, :]
        power[rows, :] = total
        top_power = jnp.maximum(top_power, total)
    scale = 1.0 / (jnp.max(top_power, axis=(0, 1), keepdims=True) + 1e-06)

    def position(p):
        r = offs[0, p] + HALF
        c = offs[1, p] + HALF
        q = c // HALF
        s = c - q * HALF
        back_shift = lax.rem(HALF - s, HALF)
        keep = lanes < HALF - s
        q2 = jnp.minimum(q + 2, 3)

        def cut(i, carry):
            rows = pl.ds(pl.multiple_of(i * CH, CH), CH)
            w = []
            for d in range(2):
                src = pl.ds(r + i * CH, CH)
                a = pltpu.roll(ext[d, q, src, :], back_shift, 1)
                b = pltpu.roll(ext[d, q + 1, src, :], back_shift, 1)
                e = pltpu.roll(ext[d, q2, src, :], back_shift, 1)
                w.append(jnp.concatenate([jnp.where(keep, a, b), jnp.where(keep, b, e)], 1))
                win[d, rows, :] = w[d]
            weight[rows, :] += w[0] * w[0] + w[1] * w[1]
            for k in range(MODES):
                pr = probe[k, 0, rows, :]
                pi = probe[k, 1, rows, :]
                stack[k, rows, :] = (pr * w[0] - pi * w[1]).astype(BF)
                stack[k, pl.ds(pl.multiple_of(W + i * CH, CH), CH), :] = (pr * w[1] + pi * w[0]).astype(BF)
            return carry

        lax.fori_loop(0, W // CH, cut, 0, unroll=True)
        if p == 0:
            for copy in copies:
                copy.wait()
        for k in range(MODES):
            rows_f = jnp.dot(fwd[...], stack[k], preferred_element_type=F32)
            side[k, :, 0:W] = rows_f[0:W].astype(BF)
            side[k, :, W:] = rows_f[W:].astype(BF)
        for k in range(MODES):
            far[k] = jnp.dot(side[k], bwd[...], preferred_element_type=F32)

        def project(i, carry):
            rows = pl.ds(pl.multiple_of(i * CH, CH), CH)
            rows_im = pl.ds(pl.multiple_of(W + i * CH, CH), CH)
            f = [far[k, rows, :] for k in range(MODES)]
            total = f[0] * f[0] + f[1] * f[1]
            intensity = total[:, 0:W] + total[:, W:]
            factor = amp[p, 0, rows, :] * lax.rsqrt(jnp.maximum(intensity, 0.0625))
            for k in range(MODES):
                stack[k, rows, :] = (f[k][:, 0:W] * factor).astype(BF)
                stack[k, rows_im, :] = (f[k][:, W:] * factor).astype(BF)
            return carry

        lax.fori_loop(0, W // CH, project, 0, unroll=True)
        for k in range(MODES):
            rows_b = jnp.dot(bwd[...], stack[k], preferred_element_type=F32)
            side[k, :, 0:W] = rows_b[0:W].astype(BF)
            side[k, :, W:] = rows_b[W:].astype(BF)
        for k in range(MODES):
            far[k] = jnp.dot(side[k], fwd[...], preferred_element_type=F32)

        def spread(i, carry):
            rows = pl.ds(pl.multiple_of(i * CH, CH), CH)
            wr = win[0, rows, :]
            wi = win[1, rows, :]
            both = power[rows, :]
            tr = jnp.zeros((CH, W), F32)
            ti = jnp.zeros((CH, W), F32)
            for k in range(MODES):
                pr = probe[k, 0, rows, :]
                pi = probe[k, 1, rows, :]
                br = far[k, rows, 0:W]
                bi = far[k, rows, W:]
                tr += pr * br + pi * bi
                ti += pr * bi - pi * br
                grads[2 * k, rows, :] += wr * br + wi * bi
                grads[2 * k + 1, rows, :] += wr * bi - wi * br
            dst = pl.ds(r + i * CH, CH)
            for d, t in ((0, tr - both * wr), (1, ti - both * wi)):
                a = pltpu.roll(t[:, 0:HALF], s, 1)
                b = pltpu.roll(t[:, HALF:], s, 1)
                low = lanes < s
                acc[d, q, dst, :] += jnp.where(low, 0.0, a)
                acc[d, q + 1, dst, :] += jnp.where(low, a, b)
                acc[d, q2, dst, :] += jnp.where(low, b, 0.0)
            return carry

        lax.fori_loop(0, W // CH, spread, 0, unroll=True)

    for p in range(POS):
        position(p)
    for d in range(2):
        for i in range(2 * W // HALF):
            rows = pl.ds(i * HALF, HALF)
            out_left[d, rows, :] = acc[d, 0, rows, :] * scale
            out_right[d, rows, :] = acc[d, 3, rows, :] * scale
            for q in range(2):
                cols = pl.ds(q * HALF, HALF)
                step = acc[d, q + 1, rows, :] * scale
                if 1 <= i <= 2:
                    step += tile[d, pl.ds((i - 1) * HALF, HALF), cols]
                out_mid[d, rows, cols] = step
    h = half[0]
    for out, side_of in ((mine, h), (other, 1 - h)):

        def flush(i, carry):
            rows = pl.ds(pl.multiple_of(side_of * HALF + i * 8, 8), 8)
            for n in range(2 * MODES):
                out[i, n] = grads[n, rows, :]
            out[i, 2 * MODES] = weight[rows, :]
            return carry

        lax.fori_loop(0, 16, flush, 0)


def correct(offsets, half, border, probe, amplitude):
    fwd, bwd = dft_matrices()
    vmem = pl.BlockSpec(memory_space=pltpu.VMEM)
    smem = pl.BlockSpec(memory_space=pltpu.SMEM)
    part = jax.ShapeDtypeStruct((16, 2 * MODES + 1, 8, W), F32)
    strip = jax.ShapeDtypeStruct((2, 2 * W, HALF), F32)
    return pl.pallas_call(
        kernel,
        out_shape=(part, part, strip, jax.ShapeDtypeStruct((2, 2 * W, W), F32), strip),
        in_specs=[smem, smem] + [vmem] * 9 + [pl.BlockSpec(memory_space=pl.ANY)] * 2,
        out_specs=(vmem,) * 5,
        scratch_shapes=[
            pltpu.VMEM((2, 4, 2 * W, HALF), F32),
            pltpu.VMEM((2, 4, 2 * W, HALF), F32),
            pltpu.VMEM((2, W, W), F32),
            pltpu.VMEM((MODES, 2 * W, W), BF),
            pltpu.VMEM((MODES, W, 2 * W), BF),
            pltpu.VMEM((MODES, W, 2 * W), F32),
            pltpu.VMEM((W, W), F32),
            pltpu.VMEM((2 * MODES, W, W), F32),
            pltpu.VMEM((W, W), F32),
            pltpu.VMEM((2 * W, 2 * W), BF),
            pltpu.VMEM((2 * W, 2 * W), BF),
            pltpu.SemaphoreType.DMA((2,)),
        ],
        compiler_params=pltpu.CompilerParams(vmem_limit_bytes=20 << 20),
    )(offsets, half, *border, probe, amplitude, jnp.asarray(fwd), jnp.asarray(bwd))


GX = ("z", "xl")
GY = ("xh", "y", "co")
UP = [(i, (i + 1) % 16) for i in range(16)]
DOWN = [(j, i) for i, j in UP]
SWAP = [(0, 1), (1, 0)]


def arrange_kernel(half, own, swapped, out):
    h = half[0]
    for source, side_of in ((own, h), (swapped, 1 - h)):
        for i in range(16):
            rows = pl.ds(pl.multiple_of(side_of * HALF + i * 8, 8), 8)
            for n in range(2 * MODES):
                out[n // 2, n % 2, rows, :] = source[i, n]


def arrange(half, own, swapped):
    vmem = pl.BlockSpec(memory_space=pltpu.VMEM)
    return pl.pallas_call(
        arrange_kernel,
        out_shape=jax.ShapeDtypeStruct((MODES, 2, W, W), F32),
        in_specs=[pl.BlockSpec(memory_space=pltpu.SMEM), vmem, vmem],
        out_specs=vmem,
        compiler_params=pltpu.CompilerParams(vmem_limit_bytes=4 << 20),
    )(half, own, swapped)


def body(object_field, probe_field, amplitude, offsets):
    group = ("xh", "xl", "y")
    co = lax.axis_index("co")
    half = co.reshape(1)
    block = (co * 16 + lax.axis_index(group)) * 8
    offs = offsets.transpose(1, 2, 0).reshape(2, POS)
    object_field, half, block = lax.optimization_barrier((object_field, half, block))
    first, last = slice(0, HALF), slice(HALF, W)
    top = lax.ppermute(object_field[:, last], GX, UP)
    bot = lax.ppermute(object_field[:, first], GX, DOWN)
    left = lax.ppermute(object_field[:, :, last], GY, UP)
    right = lax.ppermute(object_field[:, :, first], GY, DOWN)
    bot, top = lax.optimization_barrier((bot, top))
    left_ends = lax.ppermute(jnp.stack([top[:, :, last], bot[:, :, last]]), GY, UP)
    right_ends = lax.ppermute(jnp.stack([top[:, :, first], bot[:, :, first]]), GY, DOWN)
    border = (object_field, top, bot, left, right, left_ends, right_ends)
    mine, other, out_left, out_mid, out_right = correct(offs, half, border, probe_field, amplitude)
    part = mine + lax.ppermute(other, "co", SWAP)
    from_right = lax.ppermute(out_left, GY, DOWN)
    from_left = lax.ppermute(out_right, GY, UP)
    pieces = lax.all_to_all(part, group, 0, 0, tiled=True)
    part = sum(pieces[i] for i in range(16))
    folded = out_mid + jnp.concatenate([from_left, from_right], 2)
    part, folded = lax.optimization_barrier((part, folded))
    from_below = lax.ppermute(folded[:, :HALF], GX, DOWN)
    from_above = lax.ppermute(folded[:, HALF + W :], GX, UP)
    peers = [lax.ppermute(part, "z", [(i, i ^ step) for i in range(8)]) for step in (1, 2, 3)]
    part = (part + peers[0]) + (peers[1] + peers[2])
    part = part + lax.ppermute(part, "z", [(i, i ^ 4) for i in range(8)])
    part, from_below, from_above = lax.optimization_barrier((part, from_below, from_above))
    planes = probe_field.reshape(2 * MODES, W, W)
    local = lax.dynamic_slice_in_dim(planes, block, 8, 1)
    weight = part[2 * MODES]
    local = local + (part[: 2 * MODES] - local * weight) / (weight + 1e-05)
    gathered = lax.all_to_all(jnp.broadcast_to(local[None], (16,) + local.shape), group, 0, 0, tiled=True)
    updated_object = folded[:, HALF : HALF + W] + jnp.concatenate([from_above, from_below], 1)
    updated_probe = arrange(half, gathered, lax.ppermute(gathered, "co", SWAP))
    return (updated_object, updated_probe)


def solution(mesh):
    fine = Mesh(mesh.devices.reshape(8, 2, 2, 4, 2), ("z", "xl", "xh", "y", "co"))
    in_specs = (P(None, GX, GY), P(), P(GX, GY, None, None), P(GX, GY, None))
    out_specs = (P(None, GX, GY), P())
    return jax.shard_map(body, mesh=fine, in_specs=in_specs, out_specs=out_specs, check_vma=False)
```

```python
import functools
import math

import jax
import jax.numpy as jnp
import ml_dtypes
import numpy as np
from jax import lax
from jax.experimental import pallas as pl
from jax.experimental.pallas import tpu as pltpu
from jax.sharding import Mesh
from jax.sharding import PartitionSpec as P

W = 256
HALF = 128
POS = 4
MODES = 2
CH = 32
BF = jnp.bfloat16
F32 = jnp.float32


def dft_matrices():
    k = np.arange(W)
    phase = (k[:, None] * k[None, :]) % W
    angle = phase.astype(np.float32) * np.float32(2.0 * math.pi / W)
    norm = np.float32(1.0 / math.sqrt(W))
    c = (np.cos(angle) * norm).astype(ml_dtypes.bfloat16)
    s = (np.sin(angle) * norm).astype(ml_dtypes.bfloat16)
    fwd = np.block([[c, s], [-s, c]])
    bwd = np.block([[c, -s], [s, c]])
    return fwd, bwd


def kernel(
    offs, half, tile, top, bot, left, right, left_ends, right_ends, probe, amp, fwd_hbm, bwd_hbm,
    mine, other, out_left, out_mid, out_right,
    ext, acc, win, stack, side, far, weight, grads, power, fwd, bwd, sems,
):
    copies = [
        pltpu.make_async_copy(fwd_hbm, fwd, sems.at[0]),
        pltpu.make_async_copy(bwd_hbm, bwd, sems.at[1]),
    ]
    for copy in copies:
        copy.start()
    lanes = lax.broadcasted_iota(jnp.int32, (CH, HALF), 1)
    for q in range(2):
        cols = pl.ds(q * HALF, HALF)
        ext[:, q + 1, 0:HALF, :] = top[:, :, cols]
        ext[:, q + 1, HALF : HALF + W, :] = tile[:, :, cols]
        ext[:, q + 1, HALF + W :, :] = bot[:, :, cols]
    for q, middle, ends in ((0, left, left_ends), (3, right, right_ends)):
        ext[:, q, 0:HALF, :] = ends[0]
        ext[:, q, HALF : HALF + W, :] = middle[...]
        ext[:, q, HALF + W :, :] = ends[1]
    acc[...] = jnp.zeros_like(acc)
    weight[...] = jnp.zeros_like(weight)
    grads[...] = jnp.zeros_like(grads)
    top_power = jnp.zeros((CH, W), F32)
    for i in range(W // CH):
        rows = pl.ds(i * CH, CH)
        total = jnp.zeros((CH, W), F32)
        for k in range(MODES):
            total += probe[k, 0, rows, :] * probe[k, 0, rows, :] + probe[k, 1, rows, :] * probe[k, 1, rows, :]
        power[rows, :] = total
        top_power = jnp.maximum(top_power, total)
    scale = 1.0 / (jnp.max(top_power, axis=(0, 1), keepdims=True) + 1e-06)

    def position(p):
        r = offs[0, p] + HALF
        c = offs[1, p] + HALF
        q = c // HALF
        s = c - q * HALF
        back_shift = lax.rem(HALF - s, HALF)
        keep = lanes < HALF - s
        q2 = jnp.minimum(q + 2, 3)

        def cut(i, carry):
            rows = pl.ds(pl.multiple_of(i * CH, CH), CH)
            w = []
            for d in range(2):
                src = pl.ds(r + i * CH, CH)
                a = pltpu.roll(ext[d, q, src, :], back_shift, 1)
                b = pltpu.roll(ext[d, q + 1, src, :], back_shift, 1)
                e = pltpu.roll(ext[d, q2, src, :], back_shift, 1)
                w.append(jnp.concatenate([jnp.where(keep, a, b), jnp.where(keep, b, e)], 1))
                win[d, rows, :] = w[d]
            weight[rows, :] += w[0] * w[0] + w[1] * w[1]
            for k in range(MODES):
                pr = probe[k, 0, rows, :]
                pi = probe[k, 1, rows, :]
                stack[k, rows, :] = (pr * w[0] - pi * w[1]).astype(BF)
                stack[k, pl.ds(pl.multiple_of(W + i * CH, CH), CH), :] = (pr * w[1] + pi * w[0]).astype(BF)
            return carry

        lax.fori_loop(0, W // CH, cut, 0, unroll=True)
        if p == 0:
            for copy in copies:
                copy.wait()
        for k in range(MODES):
            rows_f = jnp.dot(fwd[...], stack[k], preferred_element_type=F32)
            side[k, :, 0:W] = rows_f[0:W].astype(BF)
            side[k, :, W:] = rows_f[W:].astype(BF)
        for k in range(MODES):
            far[k] = jnp.dot(side[k], bwd[...], preferred_element_type=F32)

        def project(i, carry):
            rows = pl.ds(pl.multiple_of(i * CH, CH), CH)
            rows_im = pl.ds(pl.multiple_of(W + i * CH, CH), CH)
            f = [far[k, rows, :] for k in range(MODES)]
            total = f[0] * f[0] + f[1] * f[1]
            intensity = total[:, 0:W] + total[:, W:]
            factor = amp[p, 0, rows, :] * lax.rsqrt(jnp.maximum(intensity, 0.0625))
            for k in range(MODES):
                stack[k, rows, :] = (f[k][:, 0:W] * factor).astype(BF)
                stack[k, rows_im, :] = (f[k][:, W:] * factor).astype(BF)
            return carry

        lax.fori_loop(0, W // CH, project, 0, unroll=True)
        for k in range(MODES):
            rows_b = jnp.dot(bwd[...], stack[k], preferred_element_type=F32)
            side[k, :, 0:W] = rows_b[0:W].astype(BF)
            side[k, :, W:] = rows_b[W:].astype(BF)
        for k in range(MODES):
            far[k] = jnp.dot(side[k], fwd[...], preferred_element_type=F32)

        def spread(i, carry):
            rows = pl.ds(pl.multiple_of(i * CH, CH), CH)
            wr = win[0, rows, :]
            wi = win[1, rows, :]
            both = power[rows, :]
            tr = jnp.zeros((CH, W), F32)
            ti = jnp.zeros((CH, W), F32)
            for k in range(MODES):
                pr = probe[k, 0, rows, :]
                pi = probe[k, 1, rows, :]
                br = far[k, rows, 0:W]
                bi = far[k, rows, W:]
                tr += pr * br + pi * bi
                ti += pr * bi - pi * br
                grads[2 * k, rows, :] += wr * br + wi * bi
                grads[2 * k + 1, rows, :] += wr * bi - wi * br
            dst = pl.ds(r + i * CH, CH)
            for d, t in ((0, tr - both * wr), (1, ti - both * wi)):
                a = pltpu.roll(t[:, 0:HALF], s, 1)
                b = pltpu.roll(t[:, HALF:], s, 1)
                low = lanes < s
                acc[d, q, dst, :] += jnp.where(low, 0.0, a)
                acc[d, q + 1, dst, :] += jnp.where(low, a, b)
                acc[d, q2, dst, :] += jnp.where(low, b, 0.0)
            return carry

        lax.fori_loop(0, W // CH, spread, 0, unroll=True)

    for p in range(POS):
        position(p)
    for d in range(2):
        for i in range(2 * W // HALF):
            rows = pl.ds(i * HALF, HALF)
            out_left[d, rows, :] = acc[d, 0, rows, :] * scale
            out_right[d, rows, :] = acc[d, 3, rows, :] * scale
            for q in range(2):
                cols = pl.ds(q * HALF, HALF)
                step = acc[d, q + 1, rows, :] * scale
                if 1 <= i <= 2:
                    step += tile[d, pl.ds((i - 1) * HALF, HALF), cols]
                out_mid[d, rows, cols] = step
    h = half[0]
    for out, side_of in ((mine, h), (other, 1 - h)):

        def flush(i, carry):
            rows = pl.ds(pl.multiple_of(side_of * HALF + i * 8, 8), 8)
            for n in range(2 * MODES):
                out[i, n] = grads[n, rows, :]
            out[i, 2 * MODES] = weight[rows, :]
            return carry

        lax.fori_loop(0, 16, flush, 0)


def correct(offsets, half, border, probe, amplitude):
    fwd, bwd = dft_matrices()
    vmem = pl.BlockSpec(memory_space=pltpu.VMEM)
    smem = pl.BlockSpec(memory_space=pltpu.SMEM)
    part = jax.ShapeDtypeStruct((16, 2 * MODES + 1, 8, W), F32)
    strip = jax.ShapeDtypeStruct((2, 2 * W, HALF), F32)
    return pl.pallas_call(
        kernel,
        out_shape=(part, part, strip, jax.ShapeDtypeStruct((2, 2 * W, W), F32), strip),
        in_specs=[smem, smem] + [vmem] * 9 + [pl.BlockSpec(memory_space=pl.ANY)] * 2,
        out_specs=(vmem,) * 5,
        scratch_shapes=[
            pltpu.VMEM((2, 4, 2 * W, HALF), F32),
            pltpu.VMEM((2, 4, 2 * W, HALF), F32),
            pltpu.VMEM((2, W, W), F32),
            pltpu.VMEM((MODES, 2 * W, W), BF),
            pltpu.VMEM((MODES, W, 2 * W), BF),
            pltpu.VMEM((MODES, W, 2 * W), F32),
            pltpu.VMEM((W, W), F32),
            pltpu.VMEM((2 * MODES, W, W), F32),
            pltpu.VMEM((W, W), F32),
            pltpu.VMEM((2 * W, 2 * W), BF),
            pltpu.VMEM((2 * W, 2 * W), BF),
            pltpu.SemaphoreType.DMA((2,)),
        ],
        compiler_params=pltpu.CompilerParams(vmem_limit_bytes=20 << 20),
    )(offsets, half, *border, probe, amplitude, jnp.asarray(fwd), jnp.asarray(bwd))


GX = ("z", "xl")
GY = ("xh", "y", "co")
UP = [(i, (i + 1) % 16) for i in range(16)]
DOWN = [(j, i) for i, j in UP]
SWAP = [(0, 1), (1, 0)]


def arrange_kernel(half, own, swapped, out):
    h = half[0]
    for source, side_of in ((own, h), (swapped, 1 - h)):
        for i in range(16):
            rows = pl.ds(pl.multiple_of(side_of * HALF + i * 8, 8), 8)
            for n in range(2 * MODES):
                out[n // 2, n % 2, rows, :] = source[i, n]


def arrange(half, own, swapped):
    vmem = pl.BlockSpec(memory_space=pltpu.VMEM)
    return pl.pallas_call(
        arrange_kernel,
        out_shape=jax.ShapeDtypeStruct((MODES, 2, W, W), F32),
        in_specs=[pl.BlockSpec(memory_space=pltpu.SMEM), vmem, vmem],
        out_specs=vmem,
        compiler_params=pltpu.CompilerParams(vmem_limit_bytes=4 << 20),
    )(half, own, swapped)


def body(object_field, probe_field, amplitude, offsets):
    group = ("xh", "xl", "y")
    co = lax.axis_index("co")
    half = co.reshape(1)
    block = (co * 16 + lax.axis_index(group)) * 8
    offs = offsets.transpose(1, 2, 0).reshape(2, POS)
    object_field, half, block = lax.optimization_barrier((object_field, half, block))
    first, last = slice(0, HALF), slice(HALF, W)
    top = lax.ppermute(object_field[:, last], GX, UP)
    bot = lax.ppermute(object_field[:, first], GX, DOWN)
    left = lax.ppermute(object_field[:, :, last], GY, UP)
    right = lax.ppermute(object_field[:, :, first], GY, DOWN)
    bot, top = lax.optimization_barrier((bot, top))
    left_ends = lax.ppermute(jnp.stack([top[:, :, last], bot[:, :, last]]), GY, UP)
    right_ends = lax.ppermute(jnp.stack([top[:, :, first], bot[:, :, first]]), GY, DOWN)
    border = (object_field, top, bot, left, right, left_ends, right_ends)
    mine, other, out_left, out_mid, out_right = correct(offs, half, border, probe_field, amplitude)
    part = mine + lax.ppermute(other, "co", SWAP)
    from_right = lax.ppermute(out_left, GY, DOWN)
    from_left = lax.ppermute(out_right, GY, UP)
    pieces = lax.all_to_all(part, group, 0, 0, tiled=True)
    part = sum(pieces[i] for i in range(16))
    folded = out_mid + jnp.concatenate([from_left, from_right], 2)
    part, folded = lax.optimization_barrier((part, folded))
    from_below = lax.ppermute(folded[:, :HALF], GX, DOWN)
    from_above = lax.ppermute(folded[:, HALF + W :], GX, UP)
    peers = [lax.ppermute(part, "z", [(i, i ^ step) for i in range(8)]) for step in (1, 4, 5)]
    part = (part + peers[0]) + (peers[1] + peers[2])
    part = part + lax.ppermute(part, "z", [(i, i ^ 2) for i in range(8)])
    part, from_below, from_above = lax.optimization_barrier((part, from_below, from_above))
    planes = probe_field.reshape(2 * MODES, W, W)
    local = lax.dynamic_slice_in_dim(planes, block, 8, 1)
    weight = part[2 * MODES]
    local = local + (part[: 2 * MODES] - local * weight) / (weight + 1e-05)
    gathered = lax.all_to_all(jnp.broadcast_to(local[None], (16,) + local.shape), group, 0, 0, tiled=True)
    updated_object = folded[:, HALF : HALF + W] + jnp.concatenate([from_above, from_below], 1)
    updated_probe = arrange(half, gathered, lax.ppermute(gathered, "co", SWAP))
    return (updated_object, updated_probe)


def solution(mesh):
    fine = Mesh(mesh.devices.reshape(8, 2, 2, 4, 2), ("z", "xl", "xh", "y", "co"))
    in_specs = (P(None, GX, GY), P(), P(GX, GY, None, None), P(GX, GY, None))
    out_specs = (P(None, GX, GY), P())
    return jax.shard_map(body, mesh=fine, in_specs=in_specs, out_specs=out_specs, check_vma=False)
```
